256 devices in a mesh: rcv: 64 (over x_lo, y, z), ref: 4 (over x_hi, core).
Axes of the slice: x: 4 (x_hi: 2, x_lo: 2; x = x_hi * 2 + x_lo), y: 4, z: 8, core: 2. Of those that a mesh axis runs over, the one named last changes fastest.
Arguments:
- receiver_spectra: bfloat16 [512, 8192], P('rcv', 'ref'), may hold values from -6 to 6
- reference_spectra: bfloat16 [8192, 1024], P('rcv', 'ref'), may hold values from -6 to 6
- receiver_counts: int32 [512], P('rcv'), may hold values from 1 to 16
- reference_counts: int32 [1024], P('ref'), may hold values from 1 to 16
- column_station: int32 [1024], P('ref'), may hold values from 0 to 1023, as said below
- lag_window: int32 [2, 512, 1024], P(None, 'rcv', 'ref'), may hold values from 0 to 256, as said below
- observed: bfloat16 [512, 1024, 512], P('rcv', 'ref'), may hold values from 0.19921875 to 2
Outputs:
- receiver_grad: float32 [512, 8192], P('rcv', 'ref')
- reference_grad: float32 [8192, 1024], P('rcv', 'ref')
The draws below stay inside these ranges and needn't reach their ends.
Inputs may be any that keep to these rules, and one draw needn't show every extreme that they name: `receiver_counts`: number of valid leading segments of each station. `column_station`: A permutation of the 1024 reference stations that maps each block of 256 consecutive pair columns onto the same block of stations. lag_window[0] is a first lag below 256; lag_window[1] is a number of lags from 64 to 256.
All inputs are finite; a program needn't handle non-finite values.
Results may differ from the reference program's by a relative error of at most 0.0014.
Values may be sent and summed in bfloat16 or wider, within the bound.
A program may use at most 64 MiB of HBM per device.

```python
import math
import jax
import jax.numpy as jnp
from jax import lax

RCV_DEV = 8
REF_DEV = 256
L = 512
S = 16
F = 256
K = 8192
NR = 512
NS = 1024


def draw_column_station(key, part):
    block_total = NS // REF_DEV

    def one_block(block_id):
        shuffled = jax.random.permutation(jax.random.fold_in(jax.random.fold_in(key, 11), block_id), REF_DEV)
        return shuffled.astype(jnp.int32) + block_id * REF_DEV
    return jax.vmap(one_block)(jnp.arange(block_total, dtype=jnp.int32)).reshape(NS).astype(jnp.int32)


def draw_lag_window(key, part):
    start_key, span_key = jax.random.split(jax.random.fold_in(key, 7))
    starts = jax.random.randint(start_key, (NR, NS), 0, L // 2)
    spans = jax.random.randint(span_key, (NR, NS), L // 8, L // 2 + 1)
    return jnp.stack([starts, spans]).astype(jnp.int32)


def place_ends(values, own_key, least, top_value):
    place = [jax.random.randint(jax.random.fold_in(own_key, axis), (), 0, length) for axis, length in enumerate(values.shape)]
    longest = values.shape.index(max(values.shape))
    beside = place[:longest] + [(place[longest] + 1) % values.shape[longest]] + place[longest + 1:]
    return values.at[tuple(place)].set(least).at[tuple(beside)].set(top_value)


def block_scale(own_key, extent, cuts, least, largest):
    gain = 1.0
    for position, parts in cuts:
        draws = jax.random.uniform(jax.random.fold_in(jax.random.fold_in(own_key, 6), position), (parts,), jnp.float32, least / len(cuts), largest / len(cuts))
        gain = gain * jnp.repeat(jnp.exp(draws), extent[position] // parts).reshape((-1,) + (1,) * (len(extent) - 1 - position))
    return gain


def bell_draw(own_key, dims, width, reach, cuts=(), held_as=jnp.bfloat16):
    drawn = width * jax.random.normal(own_key, dims, jnp.float32)
    if cuts:
        drawn = drawn * block_scale(own_key, dims, cuts, -0.22, 0.18)
    return jnp.clip(drawn, -reach, reach).astype(held_as)


def setup_inputs(seed: int = 0) -> dict:
    key_list = jax.random.split(jax.random.key(seed), 8)
    receiver_spectra = bell_draw(key_list[0], (NR, K), 1.0, 6.0, ((0, 64), (1, 4)))
    reference_spectra = bell_draw(key_list[1], (K, NS), 1.0, 6.0, ((0, 64), (1, 4)))
    receiver_counts = place_ends(jax.random.randint(key_list[2], (NR,), 1, S + 1), jax.random.fold_in(key_list[2], 1), 1, S).astype(jnp.int32)
    reference_counts = place_ends(jax.random.randint(key_list[3], (NS,), 1, S + 1), jax.random.fold_in(key_list[3], 1), 1, S).astype(jnp.int32)
    column_station = draw_column_station(jax.random.fold_in(key_list[7], 71), 0)
    lag_window = draw_lag_window(jax.random.fold_in(key_list[7], 71), 0)
    observed = jnp.clip(0.19921875 + 1.8007812 * jax.random.uniform(key_list[6], (NR, NS, L), jnp.float32) ** block_scale(key_list[6], (NR, NS, L), ((0, 64), (1, 4)), -0.2, 0.2), 0.19921875, 2.0).astype(jnp.bfloat16)
    return dict(receiver_spectra=receiver_spectra, reference_spectra=reference_spectra, receiver_counts=receiver_counts, reference_counts=reference_counts, column_station=column_station, lag_window=lag_window, observed=observed)


env_floor = 0.05
misfit_scale = 0.03125

def lag_table(freq_total, lag_total):
    freq_ids = jnp.arange(freq_total, dtype=jnp.int32)[:, None]
    lag_ids = jnp.arange(lag_total, dtype=jnp.int32)[None, :] - lag_total // 2
    phase_ids = freq_ids * lag_ids % lag_total
    phase_angle = phase_ids.astype(jnp.float32) * (2.0 * math.pi / lag_total)
    cosine = jnp.cos(phase_angle) / math.sqrt(freq_total)
    sine_part = jnp.sin(phase_angle) / math.sqrt(freq_total)
    real_rows = jnp.concatenate([cosine, sine_part], axis=1)
    imag_rows = jnp.concatenate([-sine_part, cosine], axis=1)
    stacked = jnp.stack([real_rows, imag_rows], axis=1)
    return stacked.reshape(2 * freq_total, 2 * lag_total).astype(jnp.bfloat16)

def segment_masks(receiver_counts, pair_counts, seg_total):
    seg_ids = jnp.arange(seg_total, dtype=jnp.int32)
    receiver_mask = (seg_ids[None, :] < receiver_counts[:, None]).astype(jnp.float32)
    reference_mask = (seg_ids[:, None] < pair_counts[None, :]).astype(jnp.float32)
    return (receiver_mask, reference_mask)

def receiver_operand(receiver_vals):
    real_part = receiver_vals[:, :, 0, :]
    imag_part = receiver_vals[:, :, 1, :]
    first_row = jnp.concatenate([real_part, imag_part], axis=-1)
    second_row = jnp.concatenate([imag_part, -real_part], axis=-1)
    return jnp.stack([first_row, second_row], axis=2)

def reference_operand(reference_vals):
    real_part = reference_vals[:, 0]
    imag_part = reference_vals[:, 1]
    first_row = jnp.stack([real_part, imag_part], axis=1)
    second_row = jnp.stack([-imag_part, real_part], axis=1)
    return jnp.stack([first_row, second_row], axis=1)

def pair_block(receiver_op, reference_flat, pair_norm, window, observed_block, lag_matrix):
    row_total = receiver_op.shape[0]
    col_total = reference_flat.shape[2]
    highest = lax.Precision.HIGHEST
    cross_spec = jnp.einsum('ifqk,fkj->ijfq', receiver_op, reference_flat, precision=highest)
    spectra = (cross_spec / pair_norm[:, :, None, None]).astype(jnp.bfloat16)
    matrix_wide = lag_matrix.astype(jnp.float32)
    lagged = jnp.dot(spectra.reshape(row_total * col_total, 2 * F).astype(jnp.float32), matrix_wide, precision=highest)
    lagged = lagged.reshape(row_total, col_total, 2 * L)
    correlation = lagged[..., :L]
    hilbert_part = lagged[..., L:]
    envelope = jnp.sqrt(correlation * correlation + hilbert_part * hilbert_part + env_floor)
    lag_ids = jnp.arange(L, dtype=jnp.int32)
    inside = (lag_ids >= window[0][..., None]) & (lag_ids < (window[0] + window[1])[..., None])
    misfit = jnp.where(inside, envelope - observed_block.astype(jnp.float32), 0.0) * misfit_scale
    weights = jnp.concatenate([misfit * correlation / envelope, misfit * hilbert_part / envelope], axis=-1).astype(jnp.bfloat16)
    back_proj = jnp.dot(weights.reshape(row_total * col_total, 2 * L).astype(jnp.float32), matrix_wide.T, precision=highest)
    back_proj = back_proj.reshape(row_total, col_total, F, 2)
    return (back_proj / pair_norm[:, :, None, None]).astype(jnp.bfloat16)

def reference(receiver_spectra, reference_spectra, receiver_counts, reference_counts, column_station, lag_window, observed):
    highest = lax.Precision.HIGHEST
    lag_matrix = lag_table(F, L)
    pair_counts = jnp.take(reference_counts, column_station)
    receiver_mask, reference_mask = segment_masks(receiver_counts, pair_counts, S)
    receiver_vals = receiver_spectra.astype(jnp.float32).reshape(NR, F, 2, S) * receiver_mask[:, None, None, :]
    reference_vals = jnp.take(reference_spectra, column_station, axis=1).astype(jnp.float32).reshape(F, 2, S, NS)
    reference_vals = reference_vals * reference_mask[None, None, :, :]
    receiver_op = receiver_operand(receiver_vals)
    reference_flat = reference_vals.reshape(F, 2 * S, NS)
    reference_op = reference_operand(reference_vals)
    block_total = NR // RCV_DEV

    def block_step(carry_sum, block_id):
        begin_row = block_id * RCV_DEV
        op_block = lax.dynamic_slice_in_dim(receiver_op, begin_row, RCV_DEV, 0)
        count_block = lax.dynamic_slice_in_dim(receiver_counts, begin_row, RCV_DEV, 0)
        mask_block = lax.dynamic_slice_in_dim(receiver_mask, begin_row, RCV_DEV, 0)
        window = lax.dynamic_slice_in_dim(lag_window, begin_row, RCV_DEV, 1)
        observed_block = lax.dynamic_slice_in_dim(observed, begin_row, RCV_DEV, 0)
        pair_norm = jnp.minimum(count_block[:, None], pair_counts[None, :]).astype(jnp.float32)
        grad_spec = pair_block(op_block, reference_flat, pair_norm, window, observed_block, lag_matrix).astype(jnp.float32)
        receiver_part = jnp.einsum('ijfq,fqcsj->ifcs', grad_spec, reference_op, precision=highest)
        receiver_part = receiver_part * mask_block[:, None, None, :]
        reference_part = jnp.einsum('ijfq,ifqk->fkj', grad_spec, op_block, precision=highest)
        return (carry_sum + reference_part, receiver_part.reshape(RCV_DEV, K))
    reference_total, receiver_blocks = lax.scan(block_step, jnp.zeros((F, 2 * S, NS), jnp.float32), jnp.arange(block_total, dtype=jnp.int32))
    receiver_grad = receiver_blocks.reshape(NR, K)
    permuted = (reference_total.reshape(F, 2, S, NS) * reference_mask[None, None, :, :]).reshape(K, NS)
    reference_grad = jnp.zeros((K, NS), jnp.float32).at[:, column_station].set(permuted)
    return (receiver_grad, reference_grad)
```

```python
import functools
import math

import jax
import jax.numpy as jnp
import numpy as np
from jax import lax
from jax.experimental import pallas as pl
from jax.experimental.pallas import tpu as pltpu
from jax.sharding import PartitionSpec as P

L = 512
S = 16
F = 256
NP = 8
NZ = 8
NI = 8
NJ = 256
NG = 4
MESH = pl.DeviceIdType.MESH
BF = jnp.bfloat16
F32 = jnp.float32

env_floor = 0.05
misfit_scale = 0.03125


def lag_table():
    freq_ids = np.arange(F, dtype=np.int64)[:, None]
    lag_ids = np.arange(L, dtype=np.int64)[None, :] - L // 2
    angle = ((freq_ids * lag_ids) % L).astype(np.float64) * (2.0 * math.pi / L)
    cosine = np.cos(angle) / math.sqrt(F)
    sine = np.sin(angle) / math.sqrt(F)
    real_rows = np.concatenate([cosine, sine], axis=1)
    imag_rows = np.concatenate([-sine, cosine], axis=1)
    stacked = np.stack([real_rows, imag_rows], axis=1).reshape(2 * F, 2 * L)
    return stacked.astype(np.float32)


def kernel(
    u_ref, v_ref, rc_ref, fc_ref, cs_ref, win_ref, obs_ref, m_ref, mt_ref,
    rg_out, wg_out,
    um, us, vg, bt, bb, rinv, ninv, obst, xs, xr, gs, zs, zr, w, rbuf, lbuf, rgp, rgr,
    u_send, u_recv, v_send, v_recv, x_send, x_recv, z_send, z_recv,
    g_send, g_recv, r_send, r_recv, l_send, l_recv, own_sem,
):
    r = lax.axis_index("rcv")
    q = lax.axis_index("ref")
    p = r // NZ
    z = r % NZ

    def signal(rr, qq):
        pl.semaphore_signal(barrier, inc=1, device_id=(rr, qq), device_id_type=MESH)

    def remote(src, dst, send, recv, rr, qq):
        return pltpu.make_async_remote_copy(
            src_ref=src, dst_ref=dst, send_sem=send, recv_sem=recv,
            device_id=(rr, qq), device_id_type=MESH,
        )

    def plane(k):
        return ((p + k) % NP) * NZ + z

    def wait_bytes(ref, sem):
        pltpu.make_async_copy(ref, ref, sem).wait()

    barrier = pltpu.get_barrier_semaphore()
    for k in range(1, NP):
        signal(plane(k), q)
    for k in range(1, NZ):
        signal(p * NZ + (z + k) % NZ, q)
    for k in range(NP):
        own = jnp.logical_and(k == 0, p // 2 == q)

        @pl.when(jnp.logical_not(own))
        def _():
            signal(plane(k), p // 2)

    for half in range(2):
        for qq in range(4):
            rr = (2 * q + half) * NZ + z
            own = jnp.logical_and(rr == r, qq == q)

            @pl.when(jnp.logical_not(own))
            def _():
                signal(rr, qq)

    order = cs_ref[...] - q * NJ
    stations = lax.broadcasted_iota(jnp.int32, (NJ, NJ), 0)
    onehot = jnp.where(stations == order, 1.0, 0.0)
    onehot_b = onehot.astype(BF)
    counts8 = jnp.broadcast_to(fc_ref[...].astype(F32), (8, NJ)).astype(BF)
    pc = jnp.dot(counts8, onehot_b, preferred_element_type=F32)[0:1, :]
    seg_row = lax.broadcasted_iota(jnp.int32, (128, NJ), 0) % S
    row_mask = seg_row.astype(F32) < pc
    vp = jnp.dot(v_ref[...], onehot_b, preferred_element_type=F32)
    vg[z] = jnp.where(row_mask, vp, 0.0).astype(BF)
    seg_lane = lax.broadcasted_iota(jnp.int32, (NI, 2048), 1) % S
    rcounts = rc_ref[...]
    masked = jnp.where(seg_lane < rcounts, u_ref[...].astype(F32), 0.0).astype(BF)
    tail = jnp.broadcast_to(rcounts.astype(F32), (NI, 128)).astype(BF)
    for half in range(2):
        um[half, :, 0:1024] = masked[:, half * 1024 : (half + 1) * 1024]
        um[half, :, 1024:1152] = tail
    ninv[...] = 1.0 / jnp.minimum(rcounts.astype(F32), pc)

    mine = jnp.where(p // 2 == q, 2, 0)
    pl.semaphore_wait(barrier, 2 * (NP - 1) + 2 * NP - mine)

    for half in range(2):
        for qq in range(4):
            pp = 2 * q + half
            rr = pp * NZ + z
            own = jnp.logical_and(rr == r, qq == q)
            slot = (p - pp + NP) % NP

            @pl.when(jnp.logical_not(own))
            def _():
                remote(um.at[half], us.at[slot], u_send.at[half, qq], u_recv.at[slot], rr, qq).start()

            @pl.when(own)
            def _():
                pltpu.make_async_copy(um.at[half], us.at[slot], u_recv.at[slot]).start()

    for k in (1, 7, 2, 6, 3, 5, 4):
        remote(vg.at[z], vg.at[z], v_send.at[k], v_recv.at[z], p * NZ + (z + k) % NZ, q).start()

    def turn(i, c):
        obst[i] = jnp.transpose(obs_ref[i].astype(F32), (1, 0)).astype(BF)
        return c

    lax.fori_loop(0, NI, turn, 0)

    row16 = lax.broadcasted_iota(jnp.int32, (16, 256), 0)
    lane256 = lax.broadcasted_iota(jnp.int32, (16, 256), 1)
    diag = (lane256 // 32) == (row16 // 2)
    mask0 = jnp.logical_and(diag, row16 % 2 == 0)
    mask1 = jnp.logical_and(diag, row16 % 2 == 1)

    def operand(k, c):
        wait_bytes(us.at[k], u_recv.at[k])
        uf = us[k, :, 0:1024].astype(F32)
        part = (lax.broadcasted_iota(jnp.int32, (NI, 1024), 1) // S) % 2
        turned = jnp.where(part == 0, pltpu.roll(uf, 1024 - S, 1), -pltpu.roll(uf, S, 1))
        rinv[k] = 1.0 / jnp.minimum(us[k, :, 1024:1025].astype(F32), pc)
        for g in range(NG):
            a = uf[:, g * 256 : (g + 1) * 256]
            b = turned[:, g * 256 : (g + 1) * 256]
            for i in range(NI):
                blk = jnp.where(mask0, a[i : i + 1], jnp.where(mask1, b[i : i + 1], 0.0))
                bt[g, i, pl.ds(k * 16, 16), :] = blk.astype(BF)
        return c

    lax.fori_loop(0, NP, operand, 0)

    for k in range(1, NZ):
        zz = (z + k) % NZ
        wait_bytes(vg.at[zz], v_recv.at[zz])

    def cross(i, c):
        scale = jnp.concatenate(
            [jnp.broadcast_to(rinv[k, pl.ds(i, 1), :], (16, NJ)) for k in range(NP)], axis=0
        )
        for g in range(NG):
            block = vg[2 * g : 2 * g + 2].reshape(256, NJ)
            x = jnp.dot(bt[g, i], block, preferred_element_type=F32) * scale
            x = x.astype(BF)
            xr[i, p, g * 16 : (g + 1) * 16, :] = x[0:16]
            for k in range(1, NP):
                xs[i, k, g * 16 : (g + 1) * 16, :] = x[k * 16 : (k + 1) * 16]
        for k in range(1, NP):
            remote(xs.at[i, k], xr.at[i, p], x_send.at[i], x_recv.at[i], plane(k), q).start()
        return c

    lax.fori_loop(0, NI, cross, 0)

    def flip(g, c):
        for i in range(0, NI, 2):
            both = bt[g, i : i + 2].reshape(256, 256).astype(F32)
            bb[g, :, i * 128 : (i + 2) * 128] = jnp.transpose(both, (1, 0)).astype(BF)
        return c

    lax.fori_loop(0, NG, flip, 0)

    TB = 128

    def pairs(i, c):
        wait_bytes(xs.at[i, 1:NP], x_recv.at[i])
        x = xr[i].reshape(2 * F, NJ)
        first = win_ref[0, pl.ds(i, 1), :]
        last = first + win_ref[1, pl.ds(i, 1), :]
        for b in range(L // TB):
            cor = jnp.dot(mt_ref[b * TB : (b + 1) * TB, :], x, preferred_element_type=F32)
            hil = jnp.dot(mt_ref[L + b * TB : L + (b + 1) * TB, :], x, preferred_element_type=F32)
            rs = lax.rsqrt(cor * cor + hil * hil + env_floor)
            lag = lax.broadcasted_iota(jnp.int32, (TB, NJ), 0) + b * TB
            inside = jnp.logical_and(lag >= first, lag < last)
            seen = obst[i, b * TB : (b + 1) * TB, :].astype(F32)
            wt = jnp.where(inside, (1.0 - seen * rs) * misfit_scale, 0.0)
            gs[b * TB : (b + 1) * TB, :] = (wt * cor).astype(BF)
            gs[L + b * TB : L + (b + 1) * TB, :] = (wt * hil).astype(BF)
        scale = ninv[pl.ds(i, 1), :]
        for b in range(4):
            back = jnp.dot(m_ref[b * 128 : (b + 1) * 128, :], gs[...], preferred_element_type=F32)
            zs[i, 2 * b : 2 * b + 2] = (back * scale).astype(BF).reshape(2, NG, 16, NJ)
        for k in range(1, NP):
            remote(
                zs.at[i, (p + k) % NP], zr.at[:, i, NP - k], z_send.at[i], z_recv.at[i], plane(k), q
            ).start()
        zr[:, i, 0] = zs[i, p]
        return c

    lax.fori_loop(0, NI, pairs, 0)

    lane8 = (lax.broadcasted_iota(jnp.int32, (NP, 256), 1) // S) % 2

    def receivers(i, c):
        wait_bytes(zs.at[i, 1:NP], z_recv.at[i])
        for g in range(NG):
            block = vg[2 * g : 2 * g + 2].reshape(256, NJ)
            t = lax.dot_general(
                zr[g, i].reshape(128, NJ), block, (((1,), (1,)), ((), ())), preferred_element_type=F32
            ).reshape(NP, 16, 256)
            a0 = jnp.sum(jnp.where(mask0[None], t, 0.0), axis=1)
            a1 = jnp.sum(jnp.where(mask1[None], t, 0.0), axis=1)
            rg = a0 + jnp.where(lane8 == 0, -pltpu.roll(a1, 256 - S, 1), pltpu.roll(a1, S, 1))
            for k in range(NP):
                rgp[k, pl.ds(i, 1), g * 256 : (g + 1) * 256] = rg[k : k + 1]
        return c

    lax.fori_loop(0, NI, receivers, 0)

    for g in range(NG):
        part = jnp.dot(bb[g], zr[g].reshape(1024, NJ), preferred_element_type=F32)
        w[2 * g : 2 * g + 2] = part.reshape(2, 128, NJ)

    right = p * NZ + (z + 1) % NZ
    left = p * NZ + (z + NZ - 1) % NZ
    remote(w.at[(z + 4) % NZ], rbuf.at[0], r_send.at[0], r_recv.at[0], right, q).start()
    remote(w.at[(z + 5) % NZ], lbuf.at[0], l_send.at[0], l_recv.at[0], left, q).start()
    for k in range(NP):
        own = jnp.logical_and(k == 0, p // 2 == q)

        @pl.when(jnp.logical_not(own))
        def _():
            remote(rgp.at[k], rgr.at[q, p % 2], g_send.at[k], g_recv.at[q, p % 2], plane(k), p // 2).start()

        @pl.when(own)
        def _():
            pltpu.make_async_copy(rgp.at[k], rgr.at[q, p % 2], g_recv.at[q, p % 2]).start()

    for s in range(1, 4):
        wait_bytes(rbuf.at[s - 1], r_recv.at[s - 1])
        rbuf[s - 1] = rbuf[s - 1] + w[(z + 4 - s) % NZ]
        remote(rbuf.at[s - 1], rbuf.at[s], r_send.at[s], r_recv.at[s], right, q).start()
        if s < 3:
            wait_bytes(lbuf.at[s - 1], l_recv.at[s - 1])
            lbuf[s - 1] = lbuf[s - 1] + w[(z + 5 + s) % NZ]
            remote(lbuf.at[s - 1], lbuf.at[s], l_send.at[s], l_recv.at[s], left, q).start()

    for half in range(2):
        for qq in range(4):
            wait_bytes(rgr.at[qq, half], g_recv.at[qq, half])
        total = (rgr[0, half] + rgr[1, half]) + (rgr[2, half] + rgr[3, half])
        keep = seg_lane[:, 0:1024] < rcounts
        rg_out[:, half * 1024 : (half + 1) * 1024] = jnp.where(keep, total, 0.0)

    wait_bytes(rbuf.at[3], r_recv.at[3])
    wait_bytes(lbuf.at[2], l_recv.at[2])
    done = jnp.where(row_mask, w[z] + rbuf[3] + lbuf[2], 0.0)
    wg_out[...] = lax.dot_general(
        done, onehot, (((1,), (1,)), ((), ())),
        precision=lax.Precision.HIGHEST, preferred_element_type=F32,
    )

    for half in range(2):
        for qq in range(4):
            own = jnp.logical_and((2 * q + half) * NZ + z == r, qq == q)

            @pl.when(jnp.logical_not(own))
            def _():
                wait_bytes(um.at[half], u_send.at[half, qq])

    for k in range(1, NZ):
        wait_bytes(vg.at[z], v_send.at[k])
    for i in range(NI):
        wait_bytes(xs.at[i, 1:NP], x_send.at[i])
        wait_bytes(zs.at[i, 1:NP], z_send.at[i])
    for k in range(NP):
        own = jnp.logical_and(k == 0, p // 2 == q)

        @pl.when(jnp.logical_not(own))
        def _():
            wait_bytes(rgp.at[k], g_send.at[k])

    for s in range(4):
        wait_bytes(rbuf.at[s], r_send.at[s])
    for s in range(3):
        wait_bytes(lbuf.at[s], l_send.at[s])


def shards(receiver_spectra, reference_spectra, receiver_counts, reference_counts, column_station, lag_window, observed):
    table = lag_table()
    m = jnp.asarray(table, dtype=BF)
    mt = jnp.asarray(np.ascontiguousarray(table.T), dtype=BF)
    vmem = pl.BlockSpec(memory_space=pltpu.VMEM)
    dma = pltpu.SemaphoreType.DMA
    return pl.pallas_call(
        kernel,
        out_shape=(
            jax.ShapeDtypeStruct((NI, 2048), F32),
            jax.ShapeDtypeStruct((128, NJ), F32),
        ),
        in_specs=[vmem] * 9,
        out_specs=(vmem, vmem),
        scratch_shapes=[
            pltpu.VMEM((2, NI, 1152), BF),
            pltpu.VMEM((NP, NI, 1152), BF),
            pltpu.VMEM((NZ, 128, NJ), BF),
            pltpu.VMEM((NG, NI, 128, 256), BF),
            pltpu.VMEM((NG, 256, 1024), BF),
            pltpu.VMEM((NP, NI, NJ), F32),
            pltpu.VMEM((NI, NJ), F32),
            pltpu.VMEM((NI, L, NJ), BF),
            pltpu.VMEM((NI, NP, 64, NJ), BF),
            pltpu.VMEM((NI, NP, 64, NJ), BF),
            pltpu.VMEM((2 * L, NJ), BF),
            pltpu.VMEM((NI, NP, NG, 16, NJ), BF),
            pltpu.VMEM((NG, NI, NP, 16, NJ), BF),
            pltpu.VMEM((NZ, 128, NJ), F32),
            pltpu.VMEM((4, 128, NJ), F32),
            pltpu.VMEM((3, 128, NJ), F32),
            pltpu.VMEM((NP, NI, 1024), F32),
            pltpu.VMEM((4, 2, NI, 1024), F32),
            dma((2, 4)), dma((NP,)), dma((NZ,)), dma((NZ,)),
            dma((NI,)), dma((NI,)), dma((NI,)), dma((NI,)),
            dma((NP,)), dma((4, 2)), dma((4,)), dma((4,)), dma((3,)), dma((3,)), dma((1,)),
        ],
        compiler_params=pltpu.CompilerParams(
            collective_id=0, has_side_effects=True, vmem_limit_bytes=60 * 1024 * 1024
        ),
    )(
        receiver_spectra,
        reference_spectra,
        receiver_counts.reshape(NI, 1),
        reference_counts.reshape(1, NJ),
        column_station.reshape(1, NJ),
        lag_window,
        observed,
        m,
        mt,
    )


def solution(mesh):
    return jax.shard_map(
        shards,
        mesh=mesh,
        in_specs=(
            P("rcv", "ref"), P("rcv", "ref"), P("rcv"), P("ref"), P("ref"),
            P(None, "rcv", "ref"), P("rcv", "ref", None),
        ),
        out_specs=(P("rcv", "ref"), P("rcv", "ref")),
        check_vma=False,
    )
```

```python
import math

import jax
import jax.numpy as jnp
import numpy as np
from jax import lax
from jax.experimental import pallas as pl
from jax.experimental.pallas import tpu as pltpu
from jax.sharding import PartitionSpec as P

L = 512
S = 16
F = 256
NP = 8
NZ = 8
NI = 8
NJ = 256
NG = 4
MESH = pl.DeviceIdType.MESH
BF = jnp.bfloat16
F32 = jnp.float32

env_floor = 0.05
misfit_scale = 0.03125


def lag_table():
    freq_ids = np.arange(F, dtype=np.int64)[:, None]
    lag_ids = np.arange(L, dtype=np.int64)[None, :] - L // 2
    angle = ((freq_ids * lag_ids) % L).astype(np.float64) * (2.0 * math.pi / L)
    cosine = np.cos(angle) / math.sqrt(F)
    sine = np.sin(angle) / math.sqrt(F)
    real_rows = np.concatenate([cosine, sine], axis=1)
    imag_rows = np.concatenate([-sine, cosine], axis=1)
    stacked = np.stack([real_rows, imag_rows], axis=1).reshape(2 * F, 2 * L)
    return stacked.astype(np.float32)


def kernel(
    u_ref, v_ref, rc_ref, fc_ref, cs_ref, win_ref, obs_hbm, m_hbm, mt_hbm,
    rg_out, wg_out,
    um, us, vg, bt, bb, rinv, ninv, first, last, obs, m_ref, mt_ref, obst, xs, xr, gs, zs, zr,
    w, rbuf, lbuf, rgp, rgr,
    in_sem, u_send, u_recv, v_send, v_recv, x_send, x_recv, z_send, z_recv,
    g_send, g_recv, r_send, r_recv, l_send, l_recv,
):
    r = lax.axis_index("rcv")
    q = lax.axis_index("ref")
    p = r // NZ
    z = r % NZ

    def signal(rr, qq):
        pl.semaphore_signal(barrier, inc=1, device_id=(rr, qq), device_id_type=MESH)

    def remote(src, dst, send, recv, rr, qq):
        return pltpu.make_async_remote_copy(
            src_ref=src, dst_ref=dst, send_sem=send, recv_sem=recv,
            device_id=(rr, qq), device_id_type=MESH,
        )

    def plane(k):
        return ((p + k) % NP) * NZ + z

    def wait_bytes(ref, sem):
        pltpu.make_async_copy(ref, ref, sem).wait()

    barrier = pltpu.get_barrier_semaphore()
    for k in range(1, NP):
        signal(plane(k), q)
    for k in range(1, NZ):
        signal(p * NZ + (z + k) % NZ, q)
    for k in range(NP):
        own = jnp.logical_and(k == 0, p // 2 == q)

        @pl.when(jnp.logical_not(own))
        def _():
            signal(plane(k), p // 2)

    for half in range(2):
        for qq in range(4):
            rr = (2 * q + half) * NZ + z
            own = jnp.logical_and(rr == r, qq == q)

            @pl.when(jnp.logical_not(own))
            def _():
                signal(rr, qq)

    loads = [pltpu.make_async_copy(obs_hbm.at[i], obs.at[i], in_sem.at[i]) for i in range(NI)]
    loads.append(pltpu.make_async_copy(mt_hbm, mt_ref, in_sem.at[NI]))
    loads.append(pltpu.make_async_copy(m_hbm, m_ref, in_sem.at[NI + 1]))
    for load in loads:
        load.start()

    eye = lax.broadcasted_iota(jnp.int32, (NI, NI), 0) == lax.broadcasted_iota(jnp.int32, (NI, NI), 1)
    rcounts = jnp.sum(jnp.where(eye, rc_ref[...].astype(F32), 0.0), axis=1, keepdims=True)
    pc = fc_ref[...].astype(F32)
    row_mask = (lax.broadcasted_iota(jnp.int32, (128, NJ), 0) % S).astype(F32) < pc
    mine = jnp.where(row_mask, v_ref[...].astype(F32), 0.0).astype(BF)
    for h in range(2):
        vg[h, z] = mine[:, h * 128 : (h + 1) * 128]
    seg_lane = (lax.broadcasted_iota(jnp.int32, (NI, 1024), 1) % S).astype(F32)
    keep = seg_lane < rcounts
    for half in range(2):
        part = u_ref[:, half * 1024 : (half + 1) * 1024].astype(F32)
        um[half, :, 0:1024] = jnp.where(keep, part, 0.0).astype(BF)
        um[half, :, 1024:1152] = jnp.broadcast_to(rcounts, (NI, 128)).astype(BF)

    order = cs_ref[...] - q * NJ
    stations = lax.broadcasted_iota(jnp.int32, (NJ, NJ), 0)
    onehot = jnp.where(stations == order, 1.0, 0.0).astype(BF)
    nt = (((1,), (1,)), ((), ()))
    begin = lax.dot_general(win_ref[0].astype(F32).astype(BF), onehot, nt, preferred_element_type=F32)
    span = lax.dot_general(win_ref[1].astype(F32).astype(BF), onehot, nt, preferred_element_type=F32)
    inv = 1.0 / jnp.minimum(rcounts, pc)
    for h in range(2):
        for i in range(NI):
            u, lanes, side = 4 * h + i // 2, pl.ds((i % 2) * 128, 128), slice(h * 128, (h + 1) * 128)
            first[u : u + 1, lanes] = begin[i : i + 1, side]
            last[u : u + 1, lanes] = begin[i : i + 1, side] + span[i : i + 1, side]
            ninv[u : u + 1, lanes] = inv[i : i + 1, side]
    for i in range(NI):
        loads[i].wait()

    def turn(ii, c):
        for par in range(2):
            seen = jnp.dot(onehot, obs[2 * ii + par], preferred_element_type=F32)
            seen = jnp.transpose(seen, (1, 0)).astype(BF)
            for h in range(2):
                obst[4 * h + ii, :, par * 128 : (par + 1) * 128] = seen[:, h * 128 : (h + 1) * 128]
        return c

    lax.fori_loop(0, NI // 2, turn, 0)

    pl.semaphore_wait(barrier, 2 * (NP - 1) + 2 * NP - jnp.where(p // 2 == q, 2, 0))

    for half in range(2):
        for qq in range(4):
            pp = 2 * q + half
            rr = pp * NZ + z
            own = jnp.logical_and(rr == r, qq == q)
            slot = (p - pp + NP) % NP

            @pl.when(jnp.logical_not(own))
            def _():
                remote(um.at[half], us.at[slot], u_send.at[half, qq], u_recv.at[slot], rr, qq).start()

            @pl.when(own)
            def _():
                pltpu.make_async_copy(um.at[half], us.at[slot], u_recv.at[slot]).start()

    for h in range(2):
        for k in (1, 7, 2, 6, 3, 5, 4):
            remote(
                vg.at[h, z], vg.at[h, z], v_send.at[h], v_recv.at[h, z], p * NZ + (z + k) % NZ, q
            ).start()

    row16 = lax.broadcasted_iota(jnp.int32, (16, 256), 0)
    lane256 = lax.broadcasted_iota(jnp.int32, (16, 256), 1)
    diag = (lane256 // 32) == (row16 // 2)
    mask0 = jnp.logical_and(diag, row16 % 2 == 0)
    mask1 = jnp.logical_and(diag, row16 % 2 == 1)

    def operand(k, c):
        wait_bytes(us.at[k], u_recv.at[k])
        uf = us[k, :, 0:1024].astype(F32)
        part = (lax.broadcasted_iota(jnp.int32, (NI, 1024), 1) // S) % 2
        turned = jnp.where(part == 0, pltpu.roll(uf, 1024 - S, 1), -pltpu.roll(uf, S, 1))
        inverse = 1.0 / jnp.minimum(us[k, :, 1024:1025].astype(F32), pc)
        for h in range(2):
            rinv[h, k] = inverse[:, h * 128 : (h + 1) * 128]
        for g in range(NG):
            a = uf[:, g * 256 : (g + 1) * 256]
            b = turned[:, g * 256 : (g + 1) * 256]
            for i in range(NI):
                blk = jnp.where(mask0, a[i : i + 1], jnp.where(mask1, b[i : i + 1], 0.0))
                bt[g, i // 2, i % 2, pl.ds(k * 16, 16), :] = blk.astype(BF)
        return c

    lax.fori_loop(0, NP, operand, 0)

    for h in range(2):
        for k in range(1, NZ):
            zz = (z + k) % NZ
            wait_bytes(vg.at[h, zz], v_recv.at[h, zz])

        def cross(ii, c):
            u = 4 * h + ii
            scale = jnp.concatenate(
                [
                    jnp.broadcast_to(rinv[h, k, pl.ds(2 * ii + par, 1), :], (16, 128))
                    for par in range(2)
                    for k in range(NP)
                ],
                axis=0,
            )
            for g in range(NG):
                block = vg[h, 2 * g : 2 * g + 2].reshape(256, 128)
                x = jnp.dot(bt[g, ii].reshape(256, 256), block, preferred_element_type=F32) * scale
                x = x.astype(BF)
                for par in range(2):
                    lanes = slice(par * 128, (par + 1) * 128)
                    rows = slice(g * 16, (g + 1) * 16)
                    xr[u, p, rows, lanes] = x[par * 128 : par * 128 + 16]
                    for k in range(1, NP):
                        xs[u, k, rows, lanes] = x[par * 128 + k * 16 : par * 128 + (k + 1) * 16]
            for k in range(1, NP):
                remote(xs.at[u, k], xr.at[u, p], x_send.at[u], x_recv.at[u], plane(k), q).start()
            return c

        lax.fori_loop(0, 4, cross, 0)

    def flip(g, c):
        for ii in range(4):
            for par in range(2):
                bb[g, par, :, ii * 128 : (ii + 1) * 128] = jnp.transpose(
                    bt[g, ii, par].astype(F32), (1, 0)
                ).astype(BF)
        return c

    lax.fori_loop(0, NG, flip, 0)

    TB = 128
    loads[NI].wait()
    loads[NI + 1].wait()

    def pairs(u, c):
        wait_bytes(xs.at[u, 1:NP], x_recv.at[u])
        x = xr[u].reshape(2 * F, NJ)
        lo = first[pl.ds(u, 1), :]
        hi = last[pl.ds(u, 1), :]
        for b in range(L // TB):
            cor = jnp.dot(mt_ref[b * TB : (b + 1) * TB, :], x, preferred_element_type=F32)
            hil = jnp.dot(mt_ref[L + b * TB : L + (b + 1) * TB, :], x, preferred_element_type=F32)
            rs = lax.rsqrt(cor * cor + hil * hil + env_floor)
            lag = (lax.broadcasted_iota(jnp.int32, (TB, NJ), 0) + b * TB).astype(F32)
            inside = jnp.logical_and(lag >= lo, lag < hi)
            seen = obst[u, b * TB : (b + 1) * TB, :].astype(F32)
            wt = jnp.where(inside, (1.0 - seen * rs) * misfit_scale, 0.0)
            gs[b * TB : (b + 1) * TB, :] = (wt * cor).astype(BF)
            gs[L + b * TB : L + (b + 1) * TB, :] = (wt * hil).astype(BF)
        scale = ninv[pl.ds(u, 1), :]
        for b in range(4):
            back = jnp.dot(m_ref[b * 128 : (b + 1) * 128, :], gs[...], preferred_element_type=F32)
            zs[u, 2 * b : 2 * b + 2] = (back * scale).astype(BF).reshape(2, NG, 16, NJ)
        for k in range(1, NP):
            remote(
                zs.at[u, (p + k) % NP], zr.at[:, u, NP - k], z_send.at[u], z_recv.at[u], plane(k), q
            ).start()
        zr[:, u, 0] = zs[u, p]
        return c

    lax.fori_loop(0, 8, pairs, 0)

    right = p * NZ + (z + 1) % NZ
    left = p * NZ + (z + NZ - 1) % NZ

    def arrived(u):
        wait_bytes(zs.at[u, 1:NP], z_recv.at[u])

    def sums(h):
        for g in range(NG):
            part = jnp.dot(
                bb[g, 0], zr[g, 4 * h : 4 * h + 4, :, :, 0:128].reshape(512, 128), preferred_element_type=F32
            ) + jnp.dot(
                bb[g, 1], zr[g, 4 * h : 4 * h + 4, :, :, 128:256].reshape(512, 128), preferred_element_type=F32
            )
            w[h, 2 * g : 2 * g + 2] = part.reshape(2, 128, 128)

    def ring(h, s):
        for n in range(2):
            rows = slice(n * 64, (n + 1) * 64)
            if s > 0:
                wait_bytes(rbuf.at[h, s - 1, rows], r_recv.at[h, s - 1, n])
                rbuf[h, s - 1, rows] = rbuf[h, s - 1, rows] + w[h, (z + 4 - s) % NZ, rows]
            src = rbuf.at[h, s - 1, rows] if s > 0 else w.at[h, (z + 4) % NZ, rows]
            remote(src, rbuf.at[h, s, rows], r_send.at[h, s, n], r_recv.at[h, s, n], right, q).start()
            if s > 2:
                continue
            if s > 0:
                wait_bytes(lbuf.at[h, s - 1, rows], l_recv.at[h, s - 1, n])
                lbuf[h, s - 1, rows] = lbuf[h, s - 1, rows] + w[h, (z + 5 + s) % NZ, rows]
            src = lbuf.at[h, s - 1, rows] if s > 0 else w.at[h, (z + 5) % NZ, rows]
            remote(src, lbuf.at[h, s, rows], l_send.at[h, s, n], l_recv.at[h, s, n], left, q).start()

    def ring_end(h):
        for n in range(2):
            rows = slice(n * 64, (n + 1) * 64)
            wait_bytes(rbuf.at[h, 3, rows], r_recv.at[h, 3, n])
            wait_bytes(lbuf.at[h, 2, rows], l_recv.at[h, 2, n])
            keep = row_mask[rows, h * 128 : (h + 1) * 128]
            done = w[h, z, rows] + rbuf[h, 3, rows] + lbuf[h, 2, rows]
            wg_out[rows, h * 128 : (h + 1) * 128] = jnp.where(keep, done, 0.0)

    lane8 = (lax.broadcasted_iota(jnp.int32, (NP, 256), 1) // S) % 2

    def receivers(ii):
        for g in range(NG):
            for par in range(2):
                t = None
                for h in range(2):
                    got = zr[g, 4 * h + ii, :, :, par * 128 : (par + 1) * 128].reshape(128, 128)
                    block = vg[h, 2 * g : 2 * g + 2].reshape(256, 128)
                    part = lax.dot_general(got, block, nt, preferred_element_type=F32)
                    t = part if t is None else t + part
                t = t.reshape(NP, 16, 256)
                a0 = jnp.sum(jnp.where(mask0[None], t, 0.0), axis=1)
                a1 = jnp.sum(jnp.where(mask1[None], t, 0.0), axis=1)
                rg = a0 + jnp.where(lane8 == 0, -pltpu.roll(a1, 256 - S, 1), pltpu.roll(a1, S, 1))
                i = 2 * ii + par
                for k in range(NP):
                    rgp[k, i : i + 1, g * 256 : (g + 1) * 256] = rg[k : k + 1]

    for u in range(4):
        arrived(u)
    sums(0)
    ring(0, 0)
    for s in range(1, 4):
        arrived(3 + s)
        receivers(s - 1)
        ring(0, s)
    arrived(7)
    sums(1)
    ring(1, 0)
    receivers(3)
    for k in range(NP):
        own = jnp.logical_and(k == 0, p // 2 == q)

        @pl.when(jnp.logical_not(own))
        def _():
            remote(rgp.at[k], rgr.at[q, p % 2], g_send.at[k], g_recv.at[q, p % 2], plane(k), p // 2).start()

        @pl.when(own)
        def _():
            pltpu.make_async_copy(rgp.at[k], rgr.at[q, p % 2], g_recv.at[q, p % 2]).start()

    ring(1, 1)
    ring_end(0)
    ring(1, 2)
    ring(1, 3)
    for half in range(2):
        for qq in range(4):
            wait_bytes(rgr.at[qq, half], g_recv.at[qq, half])
        total = (rgr[0, half] + rgr[1, half]) + (rgr[2, half] + rgr[3, half])
        rg_out[:, half * 1024 : (half + 1) * 1024] = jnp.where(keep, total, 0.0)
    ring_end(1)

    for half in range(2):
        for qq in range(4):
            own = jnp.logical_and((2 * q + half) * NZ + z == r, qq == q)

            @pl.when(jnp.logical_not(own))
            def _():
                wait_bytes(um.at[half], u_send.at[half, qq])

    for h in range(2):
        wait_bytes(vg.at[h, 1:NZ], v_send.at[h])
    for u in range(8):
        wait_bytes(xs.at[u, 1:NP], x_send.at[u])
        wait_bytes(zs.at[u, 1:NP], z_send.at[u])
    for k in range(NP):
        own = jnp.logical_and(k == 0, p // 2 == q)

        @pl.when(jnp.logical_not(own))
        def _():
            wait_bytes(rgp.at[k], g_send.at[k])

    for h in range(2):
        for n in range(2):
            rows = slice(n * 64, (n + 1) * 64)
            for s in range(4):
                wait_bytes(rbuf.at[h, s, rows], r_send.at[h, s, n])
            for s in range(3):
                wait_bytes(lbuf.at[h, s, rows], l_send.at[h, s, n])


def shards(receiver_spectra, reference_spectra, receiver_counts, reference_counts, column_station, lag_window, observed):
    table = lag_table()
    m = jnp.asarray(table, dtype=BF)
    mt = jnp.asarray(np.ascontiguousarray(table.T), dtype=BF)
    vmem = pl.BlockSpec(memory_space=pltpu.VMEM)
    hbm = pl.BlockSpec(memory_space=pl.ANY)
    dma = pltpu.SemaphoreType.DMA
    return pl.pallas_call(
        kernel,
        out_shape=(
            jax.ShapeDtypeStruct((NI, 2048), F32),
            jax.ShapeDtypeStruct((128, NJ), F32),
        ),
        in_specs=[vmem] * 6 + [hbm] * 3,
        out_specs=(vmem, vmem),
        scratch_shapes=[
            pltpu.VMEM((2, NI, 1152), BF),
            pltpu.VMEM((NP, NI, 1152), BF),
            pltpu.VMEM((2, NZ, 128, 128), BF),
            pltpu.VMEM((NG, 4, 2, 128, 256), BF),
            pltpu.VMEM((NG, 2, 256, 512), BF),
            pltpu.VMEM((2, NP, NI, 128), F32),
            pltpu.VMEM((8, NJ), F32),
            pltpu.VMEM((8, NJ), F32),
            pltpu.VMEM((8, NJ), F32),
            pltpu.VMEM((NI, NJ, L), BF),
            pltpu.VMEM((2 * F, 2 * L), BF),
            pltpu.VMEM((2 * L, 2 * F), BF),
            pltpu.VMEM((8, L, NJ), BF),
            pltpu.VMEM((8, NP, 64, NJ), BF),
            pltpu.VMEM((8, NP, 64, NJ), BF),
            pltpu.VMEM((2 * L, NJ), BF),
            pltpu.VMEM((8, NP, NG, 16, NJ), BF),
            pltpu.VMEM((NG, 8, NP, 16, NJ), BF),
            pltpu.VMEM((2, NZ, 128, 128), F32),
            pltpu.VMEM((2, 4, 128, 128), F32),
            pltpu.VMEM((2, 3, 128, 128), F32),
            pltpu.VMEM((NP, NI, 1024), F32),
            pltpu.VMEM((4, 2, NI, 1024), F32),
            dma((NI + 2,)), dma((2, 4)), dma((NP,)), dma((2,)), dma((2, NZ)),
            dma((8,)), dma((8,)), dma((8,)), dma((8,)),
            dma((NP,)), dma((4, 2)), dma((2, 4, 2)), dma((2, 4, 2)), dma((2, 3, 2)), dma((2, 3, 2)),
        ],
        compiler_params=pltpu.CompilerParams(
            collective_id=0, has_side_effects=True, vmem_limit_bytes=60 * 1024 * 1024
        ),
    )(
        receiver_spectra,
        reference_spectra,
        receiver_counts.reshape(1, NI),
        reference_counts.reshape(1, NJ),
        column_station.reshape(1, NJ),
        lag_window,
        observed,
        m,
        mt,
    )


def solution(mesh):
    return jax.shard_map(
        shards,
        mesh=mesh,
        in_specs=(
            P("rcv", "ref"), P("rcv", "ref"), P("rcv"), P("ref"), P("ref"),
            P(None, "rcv", "ref"), P("rcv", "ref", None),
        ),
        out_specs=(P("rcv", "ref"), P("rcv", "ref")),
        check_vma=False,
    )
```

```python
import math

import jax
import jax.numpy as jnp
import numpy as np
from jax import lax
from jax.experimental import pallas as pl
from jax.experimental.pallas import tpu as pltpu
from jax.sharding import PartitionSpec as P

L = 512
S = 16
F = 256
NP = 8
NZ = 8
NI = 8
NJ = 256
NG = 4
MESH = pl.DeviceIdType.MESH
BF = jnp.bfloat16
F32 = jnp.float32

env_floor = 0.05
misfit_scale = 0.03125


def lag_table():
    freq_ids = np.arange(F, dtype=np.int64)[:, None]
    lag_ids = np.arange(L, dtype=np.int64)[None, :] - L // 2
    angle = ((freq_ids * lag_ids) % L).astype(np.float64) * (2.0 * math.pi / L)
    cosine = np.cos(angle) / math.sqrt(F)
    sine = np.sin(angle) / math.sqrt(F)
    real_rows = np.concatenate([cosine, sine], axis=1)
    imag_rows = np.concatenate([-sine, cosine], axis=1)
    stacked = np.stack([real_rows, imag_rows], axis=1).reshape(2 * F, 2 * L)
    return stacked.astype(np.float32)


def kernel(
    u_ref, v_ref, rc_ref, fc_ref, cs_ref, win_ref, obs_hbm, m_hbm, mt_hbm,
    rg_out, wg_out,
    um, us, vg, bt, bb, rinv, ninv, first, last, obs, m_ref, mt_ref, obst, xs, xr, gs, zs, zr,
    w, rbuf, lbuf, rgp, rgr,
    in_sem, u_send, u_recv, v_send, v_recv, x_send, x_recv, z_send, z_recv,
    g_send, g_recv, r_send, r_recv, l_send, l_recv,
):
    r = lax.axis_index("rcv")
    q = lax.axis_index("ref")
    p = r // NZ
    z = r % NZ

    def signal(rr, qq):
        pl.semaphore_signal(barrier, inc=1, device_id=(rr, qq), device_id_type=MESH)

    def remote(src, dst, send, recv, rr, qq):
        return pltpu.make_async_remote_copy(
            src_ref=src, dst_ref=dst, send_sem=send, recv_sem=recv,
            device_id=(rr, qq), device_id_type=MESH,
        )

    def plane(k):
        return ((p + k) % NP) * NZ + z

    def wait_bytes(ref, sem):
        pltpu.make_async_copy(ref, ref, sem).wait()

    barrier = pltpu.get_barrier_semaphore()
    for k in range(1, NP):
        signal(plane(k), q)
    for k in range(1, NZ):
        signal(p * NZ + (z + k) % NZ, q)
    for k in range(NP):
        own = jnp.logical_and(k == 0, p // 2 == q)

        @pl.when(jnp.logical_not(own))
        def _():
            signal(plane(k), p // 2)

    for half in range(2):
        for qq in range(4):
            rr = (2 * q + half) * NZ + z
            own = jnp.logical_and(rr == r, qq == q)

            @pl.when(jnp.logical_not(own))
            def _():
                signal(rr, qq)

    loads = [pltpu.make_async_copy(obs_hbm.at[i], obs.at[i], in_sem.at[i]) for i in range(NI)]
    loads.append(pltpu.make_async_copy(mt_hbm, mt_ref, in_sem.at[NI]))
    loads.append(pltpu.make_async_copy(m_hbm, m_ref, in_sem.at[NI + 1]))
    for load in loads:
        load.start()

    eye = lax.broadcasted_iota(jnp.int32, (NI, NI), 0) == lax.broadcasted_iota(jnp.int32, (NI, NI), 1)
    rcounts = jnp.sum(jnp.where(eye, rc_ref[...].astype(F32), 0.0), axis=1, keepdims=True)
    pc = fc_ref[...].astype(F32)
    row_mask = (lax.broadcasted_iota(jnp.int32, (128, NJ), 0) % S).astype(F32) < pc
    mine = jnp.where(row_mask, v_ref[...].astype(F32), 0.0).astype(BF)
    for h in range(2):
        vg[h, z] = mine[:, h * 128 : (h + 1) * 128]
    seg_lane = (lax.broadcasted_iota(jnp.int32, (NI, 1024), 1) % S).astype(F32)
    keep = seg_lane < rcounts
    for half in range(2):
        part = u_ref[:, half * 1024 : (half + 1) * 1024].astype(F32)
        um[half, :, 0:1024] = jnp.where(keep, part, 0.0).astype(BF)
        um[half, :, 1024:1152] = jnp.broadcast_to(rcounts, (NI, 128)).astype(BF)

    order = cs_ref[...] - q * NJ
    stations = lax.broadcasted_iota(jnp.int32, (NJ, NJ), 0)
    onehot = jnp.where(stations == order, 1.0, 0.0).astype(BF)
    nt = (((1,), (1,)), ((), ()))
    begin = lax.dot_general(win_ref[0].astype(F32).astype(BF), onehot, nt, preferred_element_type=F32)
    span = lax.dot_general(win_ref[1].astype(F32).astype(BF), onehot, nt, preferred_element_type=F32)
    inv = 1.0 / jnp.minimum(rcounts, pc)
    for h in range(2):
        for i in range(NI):
            u, lanes, side = 4 * h + i // 2, pl.ds((i % 2) * 128, 128), slice(h * 128, (h + 1) * 128)
            first[u : u + 1, lanes] = begin[i : i + 1, side]
            last[u : u + 1, lanes] = begin[i : i + 1, side] + span[i : i + 1, side]
            ninv[u : u + 1, lanes] = inv[i : i + 1, side]
    for i in range(NI):
        loads[i].wait()

    def turn(ii, c):
        for par in range(2):
            seen = jnp.dot(onehot, obs[2 * ii + par], preferred_element_type=F32)
            seen = jnp.transpose(seen, (1, 0)).astype(BF)
            for h in range(2):
                obst[4 * h + ii, :, par * 128 : (par + 1) * 128] = seen[:, h * 128 : (h + 1) * 128]
        return c

    lax.fori_loop(0, NI // 2, turn, 0)

    pl.semaphore_wait(barrier, 2 * (NP - 1) + 2 * NP - jnp.where(p // 2 == q, 2, 0))

    for half in range(2):
        for qq in range(4):
            pp = 2 * q + half
            rr = pp * NZ + z
            own = jnp.logical_and(rr == r, qq == q)
            slot = (p - pp + NP) % NP

            @pl.when(jnp.logical_not(own))
            def _():
                remote(um.at[half], us.at[slot], u_send.at[half, qq], u_recv.at[slot], rr, qq).start()

            @pl.when(own)
            def _():
                pltpu.make_async_copy(um.at[half], us.at[slot], u_recv.at[slot]).start()

    for h in range(2):
        for k in (1, 7, 2, 6, 3, 5, 4):
            remote(
                vg.at[h, z], vg.at[h, z], v_send.at[h], v_recv.at[h, z], p * NZ + (z + k) % NZ, q
            ).start()

    row16 = lax.broadcasted_iota(jnp.int32, (16, 256), 0)
    lane256 = lax.broadcasted_iota(jnp.int32, (16, 256), 1)
    diag = (lane256 // 32) == (row16 // 2)
    mask0 = jnp.logical_and(diag, row16 % 2 == 0)
    mask1 = jnp.logical_and(diag, row16 % 2 == 1)

    def operand(k, c):
        wait_bytes(us.at[k], u_recv.at[k])
        uf = us[k, :, 0:1024].astype(F32)
        part = (lax.broadcasted_iota(jnp.int32, (NI, 1024), 1) // S) % 2
        turned = jnp.where(part == 0, pltpu.roll(uf, 1024 - S, 1), -pltpu.roll(uf, S, 1))
        inverse = 1.0 / jnp.minimum(us[k, :, 1024:1025].astype(F32), pc)
        for h in range(2):
            rinv[h, k] = inverse[:, h * 128 : (h + 1) * 128]
        for g in range(NG):
            a = uf[:, g * 256 : (g + 1) * 256]
            b = turned[:, g * 256 : (g + 1) * 256]
            for i in range(NI):
                blk = jnp.where(mask0, a[i : i + 1], jnp.where(mask1, b[i : i + 1], 0.0))
                bt[g, i // 2, i % 2, pl.ds(k * 16, 16), :] = blk.astype(BF)
        return c

    lax.fori_loop(0, NP, operand, 0)

    for h in range(2):
        for k in range(1, NZ):
            zz = (z + k) % NZ
            wait_bytes(vg.at[h, zz], v_recv.at[h, zz])

        def cross(ii, c):
            u = 4 * h + ii
            scale = jnp.concatenate(
                [
                    jnp.broadcast_to(rinv[h, k, pl.ds(2 * ii + par, 1), :], (16, 128))
                    for par in range(2)
                    for k in range(NP)
                ],
                axis=0,
            )
            for g in range(NG):
                block = vg[h, 2 * g : 2 * g + 2].reshape(256, 128)
                x = jnp.dot(bt[g, ii].reshape(256, 256), block, preferred_element_type=F32) * scale
                x = x.astype(BF)
                for par in range(2):
                    lanes = slice(par * 128, (par + 1) * 128)
                    rows = slice(g * 16, (g + 1) * 16)
                    xr[u, p, rows, lanes] = x[par * 128 : par * 128 + 16]
                    for k in range(1, NP):
                        xs[u, k, rows, lanes] = x[par * 128 + k * 16 : par * 128 + (k + 1) * 16]
            for k in range(1, NP):
                remote(xs.at[u, k], xr.at[u, p], x_send.at[u], x_recv.at[u], plane(k), q).start()
            return c

        lax.fori_loop(0, 4, cross, 0)

    def flip(g, c):
        for ii in range(4):
            for par in range(2):
                bb[g, par, :, ii * 128 : (ii + 1) * 128] = jnp.transpose(
                    bt[g, ii, par].astype(F32), (1, 0)
                ).astype(BF)
        return c

    lax.fori_loop(0, NG, flip, 0)

    TB = 128
    loads[NI].wait()
    loads[NI + 1].wait()

    def pairs(u, c):
        wait_bytes(xs.at[u, 1:NP], x_recv.at[u])
        x = xr[u].reshape(2 * F, NJ)
        lo = first[pl.ds(u, 1), :]
        hi = last[pl.ds(u, 1), :]
        for b in range(L // TB):
            cor = jnp.dot(mt_ref[b * TB : (b + 1) * TB, :], x, preferred_element_type=F32)
            hil = jnp.dot(mt_ref[L + b * TB : L + (b + 1) * TB, :], x, preferred_element_type=F32)
            rs = lax.rsqrt(cor * cor + hil * hil + env_floor)
            lag = (lax.broadcasted_iota(jnp.int32, (TB, NJ), 0) + b * TB).astype(F32)
            inside = jnp.logical_and(lag >= lo, lag < hi)
            seen = obst[u, b * TB : (b + 1) * TB, :].astype(F32)
            wt = jnp.where(inside, (1.0 - seen * rs) * misfit_scale, 0.0)
            gs[b * TB : (b + 1) * TB, :] = (wt * cor).astype(BF)
            gs[L + b * TB : L + (b + 1) * TB, :] = (wt * hil).astype(BF)
        scale = ninv[pl.ds(u, 1), :]
        for b in range(4):
            back = jnp.dot(m_ref[b * 128 : (b + 1) * 128, :], gs[...], preferred_element_type=F32)
            zs[u, 2 * b : 2 * b + 2] = (back * scale).astype(BF).reshape(2, NG, 16, NJ)
        for k in range(1, NP):
            remote(
                zs.at[u, (p + k) % NP], zr.at[:, u, NP - k], z_send.at[u], z_recv.at[u], plane(k), q
            ).start()
        zr[:, u, 0] = zs[u, p]
        return c

    lax.fori_loop(0, 8, pairs, 0)

    right = p * NZ + (z + 1) % NZ
    left = p * NZ + (z + NZ - 1) % NZ

    def arrived(u):
        wait_bytes(zs.at[u, 1:NP], z_recv.at[u])

    def sums(h):
        for g in range(NG):
            part = jnp.dot(
                bb[g, 0], zr[g, 4 * h : 4 * h + 4, :, :, 0:128].reshape(512, 128), preferred_element_type=F32
            ) + jnp.dot(
                bb[g, 1], zr[g, 4 * h : 4 * h + 4, :, :, 128:256].reshape(512, 128), preferred_element_type=F32
            )
            w[h, 2 * g : 2 * g + 2] = part.reshape(2, 128, 128)

    def ring(h, s):
        for n in range(2):
            rows = slice(n * 64, (n + 1) * 64)
            if s > 0:
                wait_bytes(rbuf.at[h, s - 1, rows], r_recv.at[h, s - 1, n])
                rbuf[h, s - 1, rows] = rbuf[h, s - 1, rows] + w[h, (z + 4 - s) % NZ, rows]
            src = rbuf.at[h, s - 1, rows] if s > 0 else w.at[h, (z + 4) % NZ, rows]
            remote(src, rbuf.at[h, s, rows], r_send.at[h, s, n], r_recv.at[h, s, n], right, q).start()
            if s > 2:
                continue
            if s > 0:
                wait_bytes(lbuf.at[h, s - 1, rows], l_recv.at[h, s - 1, n])
                lbuf[h, s - 1, rows] = lbuf[h, s - 1, rows] + w[h, (z + 5 + s) % NZ, rows]
            src = lbuf.at[h, s - 1, rows] if s > 0 else w.at[h, (z + 5) % NZ, rows]
            remote(src, lbuf.at[h, s, rows], l_send.at[h, s, n], l_recv.at[h, s, n], left, q).start()

    def ring_end(h):
        for n in range(2):
            rows = slice(n * 64, (n + 1) * 64)
            wait_bytes(rbuf.at[h, 3, rows], r_recv.at[h, 3, n])
            wait_bytes(lbuf.at[h, 2, rows], l_recv.at[h, 2, n])
            keep = row_mask[rows, h * 128 : (h + 1) * 128]
            done = w[h, z, rows] + rbuf[h, 3, rows] + lbuf[h, 2, rows]
            wg_out[rows, h * 128 : (h + 1) * 128] = jnp.where(keep, done, 0.0)

    lane8 = (lax.broadcasted_iota(jnp.int32, (NP, 256), 1) // S) % 2

    def receivers(ii):
        for g in range(NG):
            for par in range(2):
                t = None
                for h in range(2):
                    got = zr[g, 4 * h + ii, :, :, par * 128 : (par + 1) * 128].reshape(128, 128)
                    block = vg[h, 2 * g : 2 * g + 2].reshape(256, 128)
                    part = lax.dot_general(got, block, nt, preferred_element_type=F32)
                    t = part if t is None else t + part
                t = t.reshape(NP, 16, 256)
                a0 = jnp.sum(jnp.where(mask0[None], t, 0.0), axis=1)
                a1 = jnp.sum(jnp.where(mask1[None], t, 0.0), axis=1)
                rg = a0 + jnp.where(lane8 == 0, -pltpu.roll(a1, 256 - S, 1), pltpu.roll(a1, S, 1))
                i = 2 * ii + par
                for k in range(NP):
                    rgp[k, i : i + 1, g * 256 : (g + 1) * 256] = rg[k : k + 1]

    for u in range(4):
        arrived(u)
    sums(0)
    ring(0, 0)
    for s in range(1, 4):
        arrived(3 + s)
        receivers(s - 1)
        ring(0, s)
    arrived(7)
    sums(1)
    ring(1, 0)
    receivers(3)
    for k in range(NP):
        own = jnp.logical_and(k == 0, p // 2 == q)

        @pl.when(jnp.logical_not(own))
        def _():
            remote(rgp.at[k], rgr.at[q, p % 2], g_send.at[k], g_recv.at[q, p % 2], plane(k), p // 2).start()

        @pl.when(own)
        def _():
            pltpu.make_async_copy(rgp.at[k], rgr.at[q, p % 2], g_recv.at[q, p % 2]).start()

    ring(1, 1)
    ring_end(0)
    ring(1, 2)
    ring(1, 3)
    for half in range(2):
        for qq in range(4):
            wait_bytes(rgr.at[qq, half], g_recv.at[qq, half])
        total = (rgr[0, half] + rgr[1, half]) + (rgr[2, half] + rgr[3, half])
        rg_out[:, half * 1024 : (half + 1) * 1024] = jnp.where(keep, total, 0.0)
    ring_end(1)

    for half in range(2):
        for qq in range(4):
            own = jnp.logical_and((2 * q + half) * NZ + z == r, qq == q)

            @pl.when(jnp.logical_not(own))
            def _():
                wait_bytes(um.at[half], u_send.at[half, qq])

    for h in range(2):
        wait_bytes(vg.at[h, 1:NZ], v_send.at[h])
    for u in range(8):
        wait_bytes(xs.at[u, 1:NP], x_send.at[u])
        wait_bytes(zs.at[u, 1:NP], z_send.at[u])
    for k in range(NP):
        own = jnp.logical_and(k == 0, p // 2 == q)

        @pl.when(jnp.logical_not(own))
        def _():
            wait_bytes(rgp.at[k], g_send.at[k])

    for h in range(2):
        for n in range(2):
            rows = slice(n * 64, (n + 1) * 64)
            for s in range(4):
                wait_bytes(rbuf.at[h, s, rows], r_send.at[h, s, n])
            for s in range(3):
                wait_bytes(lbuf.at[h, s, rows], l_send.at[h, s, n])


def shards(receiver_spectra, reference_spectra, receiver_counts, reference_counts, column_station, lag_window, observed):
    table = lag_table()
    m = jnp.asarray(table, dtype=BF)
    mt = jnp.asarray(np.ascontiguousarray(table.T), dtype=BF)
    vmem = pl.BlockSpec(memory_space=pltpu.VMEM)
    hbm = pl.BlockSpec(memory_space=pl.ANY)
    dma = pltpu.SemaphoreType.DMA
    return pl.pallas_call(
        kernel,
        out_shape=(
            pltpu.VMEM((NI, 2048), F32),
            pltpu.VMEM((128, NJ), F32),
        ),
        in_specs=[vmem] * 6 + [hbm] * 3,
        out_specs=(pl.BlockSpec(memory_space=pltpu.MemorySpace.VMEM), pl.BlockSpec(memory_space=pltpu.MemorySpace.VMEM)),
        scratch_shapes=[
            pltpu.VMEM((2, NI, 1152), BF),
            pltpu.VMEM((NP, NI, 1152), BF),
            pltpu.VMEM((2, NZ, 128, 128), BF),
            pltpu.VMEM((NG, 4, 2, 128, 256), BF),
            pltpu.VMEM((NG, 2, 256, 512), BF),
            pltpu.VMEM((2, NP, NI, 128), F32),
            pltpu.VMEM((8, NJ), F32),
            pltpu.VMEM((8, NJ), F32),
            pltpu.VMEM((8, NJ), F32),
            pltpu.VMEM((NI, NJ, L), BF),
            pltpu.VMEM((2 * F, 2 * L), BF),
            pltpu.VMEM((2 * L, 2 * F), BF),
            pltpu.VMEM((8, L, NJ), BF),
            pltpu.VMEM((8, NP, 64, NJ), BF),
            pltpu.VMEM((8, NP, 64, NJ), BF),
            pltpu.VMEM((2 * L, NJ), BF),
            pltpu.VMEM((8, NP, NG, 16, NJ), BF),
            pltpu.VMEM((NG, 8, NP, 16, NJ), BF),
            pltpu.VMEM((2, NZ, 128, 128), F32),
            pltpu.VMEM((2, 4, 128, 128), F32),
            pltpu.VMEM((2, 3, 128, 128), F32),
            pltpu.VMEM((NP, NI, 1024), F32),
            pltpu.VMEM((4, 2, NI, 1024), F32),
            dma((NI + 2,)), dma((2, 4)), dma((NP,)), dma((2,)), dma((2, NZ)),
            dma((8,)), dma((8,)), dma((8,)), dma((8,)),
            dma((NP,)), dma((4, 2)), dma((2, 4, 2)), dma((2, 4, 2)), dma((2, 3, 2)), dma((2, 3, 2)),
        ],
        compiler_params=pltpu.CompilerParams(
            collective_id=0, has_side_effects=True, vmem_limit_bytes=60 * 1024 * 1024
        ),
    )(
        receiver_spectra,
        reference_spectra,
        receiver_counts.reshape(1, NI),
        reference_counts.reshape(1, NJ),
        column_station.reshape(1, NJ),
        lag_window,
        observed,
        m,
        mt,
    )


def solution(mesh):
    return jax.shard_map(
        shards,
        mesh=mesh,
        in_specs=(
            P("rcv", "ref"), P("rcv", "ref"), P("rcv"), P("ref"), P("ref"),
            P(None, "rcv", "ref"), P("rcv", "ref", None),
        ),
        out_specs=(P("rcv", "ref"), P("rcv", "ref")),
        check_vma=False,
    )
```

```python
import math

import jax
import jax.numpy as jnp
import numpy as np
from jax import lax
from jax.experimental import pallas as pl
from jax.experimental.pallas import tpu as pltpu
from jax.sharding import PartitionSpec as P

L = 512
S = 16
F = 256
NP = 8
NZ = 8
NI = 8
NJ = 256
NG = 4
MESH = pl.DeviceIdType.MESH
BF = jnp.bfloat16
F32 = jnp.float32

env_floor = 0.05
misfit_scale = 0.03125


def lag_table():
    freq_ids = np.arange(F, dtype=np.int64)[:, None]
    lag_ids = np.arange(L, dtype=np.int64)[None, :] - L // 2
    angle = ((freq_ids * lag_ids) % L).astype(np.float64) * (2.0 * math.pi / L)
    cosine = np.cos(angle) / math.sqrt(F)
    sine = np.sin(angle) / math.sqrt(F)
    real_rows = np.concatenate([cosine, sine], axis=1)
    imag_rows = np.concatenate([-sine, cosine], axis=1)
    stacked = np.stack([real_rows, imag_rows], axis=1).reshape(2 * F, 2 * L)
    return stacked.astype(np.float32)


def kernel(
    u_ref, v_ref, rc_ref, fc_ref, cs_ref, win_ref, obs_hbm, m_hbm, mq_hbm, mr_hbm,
    rg_out, wg_out,
    um, us, ur, uq, vr, vq, ucr, ucq, bw, scr, scq, bt, bb, ninv, first, last,
    obs, m_ref, mq_ref, mr_ref, obst, xsr, xrr, xsq, xrq, gs, zs, zr,
    w, rbuf, lbuf, rgp, rgr,
    in_sem, u_send, u_recv, ur_send, ur_recv, uq_send, uq_recv,
    vx_send, vx_recv, vy_send, vy_recv, vr_send, vr_recv, vq_send, vq_recv,
    xr_send, xr_recv, xq_send, xq_recv, z_send, z_recv,
    g_send, g_recv, r_send, r_recv, l_send, l_recv,
):
    r = lax.axis_index("rcv")
    q = lax.axis_index("ref")
    p = r // NZ
    z = r % NZ
    x = p // 4
    y = p % 4
    right = p * NZ + (z + 1) % NZ
    left = p * NZ + (z + NZ - 1) % NZ
    partner = ((p + 4) % NP) * NZ + z

    def signal(rr, qq):
        pl.semaphore_signal(barrier, inc=1, device_id=(rr, qq), device_id_type=MESH)

    def remote(src, dst, send, recv, rr, qq):
        return pltpu.make_async_remote_copy(
            src_ref=src, dst_ref=dst, send_sem=send, recv_sem=recv,
            device_id=(rr, qq), device_id_type=MESH,
        )

    def plane(k):
        return ((p + k) % NP) * NZ + z

    def wait_bytes(ref, sem):
        pltpu.make_async_copy(ref, ref, sem).wait()

    barrier = pltpu.get_barrier_semaphore()
    for k in range(NP):
        for dq in range(4):
            if k or dq:
                signal(plane(k), (q + dq) % 4)
    signal(right, q)
    signal(left, q)

    loads = [pltpu.make_async_copy(obs_hbm.at[i], obs.at[i], in_sem.at[i]) for i in range(NI)]
    loads.append(pltpu.make_async_copy(mr_hbm, mr_ref, in_sem.at[NI]))
    loads.append(pltpu.make_async_copy(m_hbm, m_ref, in_sem.at[NI + 1]))
    loads.append(pltpu.make_async_copy(mq_hbm, mq_ref, in_sem.at[NI + 2]))
    for load in loads:
        load.start()

    eye = lax.broadcasted_iota(jnp.int32, (NI, NI), 0) == lax.broadcasted_iota(jnp.int32, (NI, NI), 1)
    rcounts = jnp.sum(jnp.where(eye, rc_ref[...].astype(F32), 0.0), axis=1, keepdims=True)
    pc = fc_ref[...].astype(F32)
    row_mask = (lax.broadcasted_iota(jnp.int32, (128, NJ), 0) % S).astype(F32) < pc
    mine = jnp.where(row_mask, v_ref[...].astype(F32), 0.0).astype(BF)
    vq[z, y] = mine[:, 0:128]
    vr[z, x] = mine[:, 128:256]
    seg_lane = (lax.broadcasted_iota(jnp.int32, (NI, 1024), 1) % S).astype(F32)
    keep = seg_lane < rcounts
    for half in range(2):
        part = u_ref[:, half * 1024 : (half + 1) * 1024].astype(F32)
        um[half, :, 0:1024] = jnp.where(keep, part, 0.0).astype(BF)
        um[half, :, 1024:1152] = jnp.broadcast_to(rcounts, (NI, 128)).astype(BF)

    order = cs_ref[...] - q * NJ
    stations = lax.broadcasted_iota(jnp.int32, (NJ, NJ), 0)
    onehot = jnp.where(stations == order, 1.0, 0.0).astype(BF)
    nt = (((1,), (1,)), ((), ()))
    begin = lax.dot_general(win_ref[0].astype(F32).astype(BF), onehot, nt, preferred_element_type=F32)
    span = lax.dot_general(win_ref[1].astype(F32).astype(BF), onehot, nt, preferred_element_type=F32)
    inv = 1.0 / jnp.minimum(rcounts, pc)
    for h in range(2):
        for i in range(NI):
            u, lanes, side = 4 * h + i // 2, pl.ds((i % 2) * 128, 128), slice(h * 128, (h + 1) * 128)
            first[u : u + 1, lanes] = begin[i : i + 1, side]
            last[u : u + 1, lanes] = begin[i : i + 1, side] + span[i : i + 1, side]
            ninv[u : u + 1, lanes] = inv[i : i + 1, side]
    for i in range(NI):
        loads[i].wait()

    def turn(ii, c):
        for par in range(2):
            seen = jnp.dot(onehot, obs[2 * ii + par], preferred_element_type=F32)
            seen = jnp.transpose(seen, (1, 0)).astype(BF)
            for h in range(2):
                obst[4 * h + ii, :, par * 128 : (par + 1) * 128] = seen[:, h * 128 : (h + 1) * 128]
        return c

    lax.fori_loop(0, NI // 2, turn, 0)

    pl.semaphore_wait(barrier, 4 * NP - 1 + 2)

    def give(own, src, dst, send, recv, rr, qq):
        @pl.when(jnp.logical_not(own))
        def _():
            remote(src, dst, send, recv, rr, qq).start()

        @pl.when(own)
        def _():
            pltpu.make_async_copy(src, dst, recv).start()

    def pass_on(buf, send, recv, zz, sub, to):
        remote(buf.at[zz, sub], buf.at[zz, sub], send.at[0], recv.at[zz, sub], to, q).start()

    def pass_r(zz, sub, to):
        pass_on(vr, vr_send, vr_recv, zz, sub, to)

    def pass_q(zz, sub, to):
        pass_on(vq, vq_send, vq_recv, zz, sub, to)

    remote(vr.at[z, x], vr.at[z, x], vx_send.at[0], vx_recv.at[0], partner, q).start()
    for k in range(1, 4):
        remote(
            vq.at[z, y], vq.at[z, y], vy_send.at[0], vy_recv.at[y], (x * 4 + (y + k) % 4) * NZ + z, q
        ).start()
    pass_r(z, x, right)
    pass_r(z, x, left)
    pass_q(z, y, right)
    pass_q(z, y, left)
    for half in range(2):
        for qq in range(4):
            yd = 2 * (q % 2) + half
            own = jnp.logical_and(yd == y, qq == q)
            give(
                own, um.at[half], ur.at[(y - yd + 4) % 4, q // 2], ur_send.at[half, qq],
                ur_recv.at[(y - yd + 4) % 4, q // 2], (x * 4 + yd) * NZ + z, qq,
            )
    for qq in range(4):
        xd = q // 2
        own = jnp.logical_and(xd == x, qq == q)
        give(
            own, um, uq.at[(x - xd + 2) % 2, q % 2], uq_send.at[qq],
            uq_recv.at[(x - xd + 2) % 2, q % 2], (xd * 4 + y) * NZ + z, qq,
        )
    wait_bytes(vr.at[z, 1 - x], vx_recv.at[0])
    pass_r(z, 1 - x, right)
    pass_r(z, 1 - x, left)
    for k in (1, 3, 2):
        yy = (y + k) % 4
        wait_bytes(vq.at[z, yy], vy_recv.at[yy])
        pass_q(z, yy, right)
        pass_q(z, yy, left)
    for half in range(2):
        for qq in range(4):
            pp = 2 * q + half
            rr = pp * NZ + z
            own = jnp.logical_and(rr == r, qq == q)
            slot = (p - pp + NP) % NP
            give(own, um.at[half], us.at[slot], u_send.at[half, qq], u_recv.at[slot], rr, qq)

    def back(s):
        return (z + NZ - s) % NZ

    def ahead(s):
        return (z + s) % NZ

    def step_r(s):
        for k in range(2):
            sub = (x + k) % 2
            if s < 4:
                wait_bytes(vr.at[back(s), sub], vr_recv.at[back(s), sub])
                if s < 3:
                    pass_r(back(s), sub, right)
            wait_bytes(vr.at[ahead(s), sub], vr_recv.at[ahead(s), sub])
            if s < 4:
                pass_r(ahead(s), sub, left)

    def step_q(s):
        for k in (0, 1, 3, 2):
            sub = (y + k) % 4
            wait_bytes(vq.at[back(s), sub], vq_recv.at[back(s), sub])
            if s < 4:
                pass_q(back(s), sub, right)
                wait_bytes(vq.at[ahead(s), sub], vq_recv.at[ahead(s), sub])
                if s < 3:
                    pass_q(ahead(s), sub, left)

    row16 = lax.broadcasted_iota(jnp.int32, (16, 256), 0)
    lane256 = lax.broadcasted_iota(jnp.int32, (16, 256), 1)
    diag = (lane256 // 32) == (row16 // 2)
    mask0 = jnp.logical_and(diag, row16 % 2 == 0)
    mask1 = jnp.logical_and(diag, row16 % 2 == 1)

    def turned(uf):
        part = (lax.broadcasted_iota(jnp.int32, (NI, 1024), 1) // S) % 2
        return jnp.where(part == 0, pltpu.roll(uf, 1024 - S, 1), -pltpu.roll(uf, S, 1))

    def blocks(a, b, out):
        for i in range(NI):
            out(i, jnp.where(mask0, a[i : i + 1], jnp.where(mask1, b[i : i + 1], 0.0)).astype(BF))

    def ready_r(yk, c):
        for xx in range(2):
            wait_bytes(ur.at[yk, xx], ur_recv.at[yk, xx])
            uf = ur[yk, xx, :, 0:1024].astype(F32)
            ut = turned(uf)
            for zz in range(NZ):
                ucr[zz, yk, 0, :, xx * 128 : (xx + 1) * 128] = uf[:, zz * 128 : (zz + 1) * 128]
                ucr[zz, yk, 1, :, xx * 128 : (xx + 1) * 128] = ut[:, zz * 128 : (zz + 1) * 128]
        inverse = 1.0 / jnp.minimum(ur[yk, 0, :, 1024:1025].astype(F32), pc[:, 128:256])
        for i in range(NI):
            scr[yk, i] = jnp.broadcast_to(inverse[i : i + 1], (16, 128))
        return c

    def ready_q(xk, c):
        for b in range(2):
            wait_bytes(uq.at[xk, b], uq_recv.at[xk, b])
            for half in range(2):
                uf = uq[xk, b, half, :, 0:1024].astype(F32)
                ut = turned(uf)
                for zz in range(NZ):
                    ucq[zz, xk, b, 0, :, half * 128 : (half + 1) * 128] = uf[:, zz * 128 : (zz + 1) * 128]
                    ucq[zz, xk, b, 1, :, half * 128 : (half + 1) * 128] = ut[:, zz * 128 : (zz + 1) * 128]
        inverse = 1.0 / jnp.minimum(uq[xk, 0, 0, :, 1024:1025].astype(F32), pc[:, 0:128])
        for i in range(NI):
            scq[xk, i] = jnp.broadcast_to(inverse[i : i + 1], (16, 128))
        return c

    def cross_r(zz):
        for yk in range(4):
            def put(i, blk):
                bw[yk, i] = blk

            blocks(ucr[zz, yk, 0], ucr[zz, yk, 1], put)
        v = jnp.dot(bw[...].reshape(512, 256), vr[zz].reshape(256, 128), preferred_element_type=F32)
        v = (v * scr[...].reshape(512, 128)).astype(BF)
        for yk in range(4):
            for i in range(NI):
                rows = v[(yk * NI + i) * 16 : (yk * NI + i + 1) * 16]
                lanes = slice((i % 2) * 128, (i % 2 + 1) * 128)
                if yk:
                    xsr[zz, yk, i // 2, :, lanes] = rows
                else:
                    xrr[i // 2, y, zz, :, lanes] = rows
        for yk in range(1, 4):
            remote(
                xsr.at[zz, yk], xrr.at[:, y, zz], xr_send.at[zz], xr_recv.at[zz],
                (x * 4 + (y + yk) % 4) * NZ + z, q,
            ).start()

    def cross_q(zz):
        for b in range(2):
            for xk in range(2):
                def put(i, blk):
                    bw[2 * b + xk, i] = blk

                blocks(ucq[zz, xk, b, 0], ucq[zz, xk, b, 1], put)
        for b in range(2):
            v = jnp.dot(
                bw[2 * b : 2 * b + 2].reshape(256, 256), vq[zz, 2 * b : 2 * b + 2].reshape(256, 128),
                preferred_element_type=F32,
            )
            v = (v * scq[...].reshape(256, 128)).astype(BF)
            for xk in range(2):
                for i in range(NI):
                    rows = v[(xk * NI + i) * 16 : (xk * NI + i + 1) * 16]
                    lanes = slice((i % 2) * 128, (i % 2 + 1) * 128)
                    if xk:
                        xsq[zz, i // 2, b, :, lanes] = rows
                    else:
                        xrq[i // 2, x, zz, b, :, lanes] = rows
        remote(xsq.at[zz], xrq.at[:, x, zz], xq_send.at[zz], xq_recv.at[zz], partner, q).start()

    def crossings(cross, start, end):
        def one(j, c):
            cross((z + NZ + ((j + 1) // 2) * (2 * (j % 2) - 1)) % NZ)
            return c

        lax.fori_loop(start, end, one, 0)

    step_r(1)
    lax.fori_loop(0, 4, ready_r, 0)
    crossings(cross_r, 0, 1)
    step_q(1)
    step_r(2)
    crossings(cross_r, 1, 3)
    step_q(2)
    step_r(3)
    crossings(cross_r, 3, 5)
    step_q(3)
    step_r(4)
    crossings(cross_r, 5, 8)
    lax.fori_loop(0, 2, ready_q, 0)
    crossings(cross_q, 0, 7)
    step_q(4)
    crossings(cross_q, 7, 8)

    TB = 128
    for load in loads[NI:]:
        load.wait()

    def pairs(u, got, mt_ref):
        lo = first[pl.ds(u, 1), :]
        hi = last[pl.ds(u, 1), :]
        for b in range(L // TB):
            cor = jnp.dot(mt_ref[b * TB : (b + 1) * TB, :], got, preferred_element_type=F32)
            hil = jnp.dot(mt_ref[L + b * TB : L + (b + 1) * TB, :], got, preferred_element_type=F32)
            rs = lax.rsqrt(cor * cor + hil * hil + env_floor)
            lag = (lax.broadcasted_iota(jnp.int32, (TB, NJ), 0) + b * TB).astype(F32)
            inside = jnp.logical_and(lag >= lo, lag < hi)
            seen = obst[u, b * TB : (b + 1) * TB, :].astype(F32)
            wt = jnp.where(inside, (1.0 - seen * rs) * misfit_scale, 0.0)
            gs[b * TB : (b + 1) * TB, :] = (wt * cor).astype(BF)
            gs[L + b * TB : L + (b + 1) * TB, :] = (wt * hil).astype(BF)
        scale = ninv[pl.ds(u, 1), :]
        for b in range(4):
            back = jnp.dot(m_ref[b * 128 : (b + 1) * 128, :], gs[...], preferred_element_type=F32)
            zs[u, 2 * b : 2 * b + 2] = (back * scale).astype(BF).reshape(2, NG, 16, NJ)
        for k in range(1, NP):
            remote(
                zs.at[u, (p + k) % NP], zr.at[:, u, NP - k], z_send.at[u], z_recv.at[u], plane(k), q
            ).start()
        zr[:, u, 0] = zs[u, p]

    def pairs_r(ii, c):
        pairs(4 + ii, xrr[ii].reshape(2 * F, NJ), mr_ref)
        return c

    def pairs_q(ii, c):
        pairs(ii, xrq[ii].reshape(2 * F, NJ), mq_ref)
        return c

    for zz in range(NZ):
        wait_bytes(xsr.at[zz, 1:4], xr_recv.at[zz])
    lax.fori_loop(0, 4, pairs_r, 0)
    for zz in range(NZ):
        wait_bytes(xsq.at[zz], xq_recv.at[zz])
    lax.fori_loop(0, 4, pairs_q, 0)

    def operand(k, c):
        wait_bytes(us.at[k], u_recv.at[k])
        uf = us[k, :, 0:1024].astype(F32)
        ut = turned(uf)
        for g in range(NG):
            def put(i, blk):
                bt[g, i // 2, i % 2, pl.ds(k * 16, 16), :] = blk

            blocks(uf[:, g * 256 : (g + 1) * 256], ut[:, g * 256 : (g + 1) * 256], put)
        return c

    lax.fori_loop(0, NP, operand, 0)

    def flip(g, c):
        for ii in range(4):
            for par in range(2):
                bb[g, par, :, ii * 128 : (ii + 1) * 128] = jnp.transpose(
                    bt[g, ii, par].astype(F32), (1, 0)
                ).astype(BF)
        return c

    lax.fori_loop(0, NG, flip, 0)

    def arrived(u):
        wait_bytes(zs.at[u, 1:NP], z_recv.at[u])

    def sums(h):
        for g in range(NG):
            part = jnp.dot(
                bb[g, 0], zr[g, 4 * h : 4 * h + 4, :, :, 0:128].reshape(512, 128), preferred_element_type=F32
            ) + jnp.dot(
                bb[g, 1], zr[g, 4 * h : 4 * h + 4, :, :, 128:256].reshape(512, 128), preferred_element_type=F32
            )
            w[h, 2 * g : 2 * g + 2] = part.reshape(2, 128, 128)

    def ring(h, s):
        for n in range(2):
            rows = slice(n * 64, (n + 1) * 64)
            if s > 0:
                wait_bytes(rbuf.at[h, s - 1, rows], r_recv.at[h, s - 1, n])
                rbuf[h, s - 1, rows] = rbuf[h, s - 1, rows] + w[h, (z + 4 - s) % NZ, rows]
            src = rbuf.at[h, s - 1, rows] if s > 0 else w.at[h, (z + 4) % NZ, rows]
            remote(src, rbuf.at[h, s, rows], r_send.at[h, s, n], r_recv.at[h, s, n], right, q).start()
            if s > 2:
                continue
            if s > 0:
                wait_bytes(lbuf.at[h, s - 1, rows], l_recv.at[h, s - 1, n])
                lbuf[h, s - 1, rows] = lbuf[h, s - 1, rows] + w[h, (z + 5 + s) % NZ, rows]
            src = lbuf.at[h, s - 1, rows] if s > 0 else w.at[h, (z + 5) % NZ, rows]
            remote(src, lbuf.at[h, s, rows], l_send.at[h, s, n], l_recv.at[h, s, n], left, q).start()

    def ring_end(h):
        for n in range(2):
            rows = slice(n * 64, (n + 1) * 64)
            wait_bytes(rbuf.at[h, 3, rows], r_recv.at[h, 3, n])
            wait_bytes(lbuf.at[h, 2, rows], l_recv.at[h, 2, n])
            keep = row_mask[rows, h * 128 : (h + 1) * 128]
            done = w[h, z, rows] + rbuf[h, 3, rows] + lbuf[h, 2, rows]
            wg_out[rows, h * 128 : (h + 1) * 128] = jnp.where(keep, done, 0.0)

    lane8 = (lax.broadcasted_iota(jnp.int32, (NP, 256), 1) // S) % 2

    def receivers(ii):
        for g in range(NG):
            for par in range(2):
                t = None
                for h in range(2):
                    got = zr[g, 4 * h + ii, :, :, par * 128 : (par + 1) * 128].reshape(128, 128)
                    held = vr[2 * g : 2 * g + 2, x] if h else vq[2 * g : 2 * g + 2, y]
                    block = held.reshape(256, 128)
                    part = lax.dot_general(got, block, nt, preferred_element_type=F32)
                    t = part if t is None else t + part
                t = t.reshape(NP, 16, 256)
                a0 = jnp.sum(jnp.where(mask0[None], t, 0.0), axis=1)
                a1 = jnp.sum(jnp.where(mask1[None], t, 0.0), axis=1)
                rg = a0 + jnp.where(lane8 == 0, -pltpu.roll(a1, 256 - S, 1), pltpu.roll(a1, S, 1))
                i = 2 * ii + par
                for k in range(NP):
                    rgp[k, i : i + 1, g * 256 : (g + 1) * 256] = rg[k : k + 1]

    for u in range(4, 8):
        arrived(u)
    sums(1)
    ring(1, 0)
    for s in range(1, 4):
        arrived(s - 1)
        receivers(s - 1)
        ring(1, s)
    arrived(3)
    sums(0)
    ring(0, 0)
    receivers(3)
    for k in range(NP):
        own = jnp.logical_and(k == 0, p // 2 == q)

        @pl.when(jnp.logical_not(own))
        def _():
            remote(rgp.at[k], rgr.at[q, p % 2], g_send.at[k], g_recv.at[q, p % 2], plane(k), p // 2).start()

        @pl.when(own)
        def _():
            pltpu.make_async_copy(rgp.at[k], rgr.at[q, p % 2], g_recv.at[q, p % 2]).start()

    ring(0, 1)
    ring_end(1)
    ring(0, 2)
    ring(0, 3)
    for half in range(2):
        for qq in range(4):
            wait_bytes(rgr.at[qq, half], g_recv.at[qq, half])
        total = (rgr[0, half] + rgr[1, half]) + (rgr[2, half] + rgr[3, half])
        rg_out[:, half * 1024 : (half + 1) * 1024] = jnp.where(keep, total, 0.0)
    ring_end(0)

    for half in range(2):
        for qq in range(4):
            own = jnp.logical_and((2 * q + half) * NZ + z == r, qq == q)

            @pl.when(jnp.logical_not(own))
            def _():
                wait_bytes(um.at[half], u_send.at[half, qq])

    for half in range(2):
        for qq in range(4):
            own = jnp.logical_and(2 * (q % 2) + half == y, qq == q)

            @pl.when(jnp.logical_not(own))
            def _():
                wait_bytes(um.at[half], ur_send.at[half, qq])

    for qq in range(4):
        own = jnp.logical_and(q // 2 == x, qq == q)

        @pl.when(jnp.logical_not(own))
        def _():
            wait_bytes(um, uq_send.at[qq])

    wait_bytes(vr.at[z, x], vx_send.at[0])
    wait_bytes(vq.at[z, 1:4], vy_send.at[0])
    wait_bytes(vr.at[1:NZ], vr_send.at[0])
    wait_bytes(vq.at[1:NZ], vq_send.at[0])
    for zz in range(NZ):
        wait_bytes(xsr.at[zz, 1:4], xr_send.at[zz])
        wait_bytes(xsq.at[zz], xq_send.at[zz])
    for u in range(8):
        wait_bytes(zs.at[u, 1:NP], z_send.at[u])
    for k in range(NP):
        own = jnp.logical_and(k == 0, p // 2 == q)

        @pl.when(jnp.logical_not(own))
        def _():
            wait_bytes(rgp.at[k], g_send.at[k])

    for h in range(2):
        for n in range(2):
            rows = slice(n * 64, (n + 1) * 64)
            for s in range(4):
                wait_bytes(rbuf.at[h, s, rows], r_send.at[h, s, n])
            for s in range(3):
                wait_bytes(lbuf.at[h, s, rows], l_send.at[h, s, n])


def shards(receiver_spectra, reference_spectra, receiver_counts, reference_counts, column_station, lag_window, observed):
    table = lag_table()
    m = jnp.asarray(table, dtype=BF)
    places = np.arange(2 * F).reshape(2, 4, NZ, 4, 2)
    order_q = places.transpose(0, 2, 1, 3, 4).reshape(-1)
    order_r = places.transpose(1, 2, 0, 3, 4).reshape(-1)
    mq = jnp.asarray(np.ascontiguousarray(table[order_q].T), dtype=BF)
    mr = jnp.asarray(np.ascontiguousarray(table[order_r].T), dtype=BF)
    vmem = pl.BlockSpec(memory_space=pltpu.VMEM)
    hbm = pl.BlockSpec(memory_space=pl.ANY)
    dma = pltpu.SemaphoreType.DMA
    return pl.pallas_call(
        kernel,
        out_shape=(
            pltpu.VMEM((NI, 2048), F32),
            pltpu.VMEM((128, NJ), F32),
        ),
        in_specs=[vmem] * 6 + [hbm] * 4,
        out_specs=(pl.BlockSpec(memory_space=pltpu.MemorySpace.VMEM), pl.BlockSpec(memory_space=pltpu.MemorySpace.VMEM)),
        scratch_shapes=[
            pltpu.VMEM((2, NI, 1152), BF),
            pltpu.VMEM((NP, NI, 1152), BF),
            pltpu.VMEM((4, 2, NI, 1152), BF),
            pltpu.VMEM((2, 2, 2, NI, 1152), BF),
            pltpu.VMEM((NZ, 2, 128, 128), BF),
            pltpu.VMEM((NZ, 4, 128, 128), BF),
            pltpu.VMEM((NZ, 4, 2, NI, 256), F32),
            pltpu.VMEM((NZ, 2, 2, 2, NI, 256), F32),
            pltpu.VMEM((4, NI, 16, 256), BF),
            pltpu.VMEM((4, NI, 16, 128), F32),
            pltpu.VMEM((2, NI, 16, 128), F32),
            pltpu.VMEM((NG, 4, 2, 128, 256), BF),
            pltpu.VMEM((NG, 2, 256, 512), BF),
            pltpu.VMEM((8, NJ), F32),
            pltpu.VMEM((8, NJ), F32),
            pltpu.VMEM((8, NJ), F32),
            pltpu.VMEM((NI, NJ, L), BF),
            pltpu.VMEM((2 * F, 2 * L), BF),
            pltpu.VMEM((2 * L, 2 * F), BF),
            pltpu.VMEM((2 * L, 2 * F), BF),
            pltpu.VMEM((8, L, NJ), BF),
            pltpu.VMEM((NZ, 4, 4, 16, NJ), BF),
            pltpu.VMEM((4, 4, NZ, 16, NJ), BF),
            pltpu.VMEM((NZ, 4, 2, 16, NJ), BF),
            pltpu.VMEM((4, 2, NZ, 2, 16, NJ), BF),
            pltpu.VMEM((2 * L, NJ), BF),
            pltpu.VMEM((8, NP, NG, 16, NJ), BF),
            pltpu.VMEM((NG, 8, NP, 16, NJ), BF),
            pltpu.VMEM((2, NZ, 128, 128), F32),
            pltpu.VMEM((2, 4, 128, 128), F32),
            pltpu.VMEM((2, 3, 128, 128), F32),
            pltpu.VMEM((NP, NI, 1024), F32),
            pltpu.VMEM((4, 2, NI, 1024), F32),
            dma((NI + 3,)), dma((2, 4)), dma((NP,)), dma((2, 4)), dma((4, 2)), dma((4,)), dma((2, 2)),
            dma((1,)), dma((1,)), dma((1,)), dma((4,)), dma((1,)), dma((NZ, 2)), dma((1,)), dma((NZ, 4)),
            dma((NZ,)), dma((NZ,)), dma((NZ,)), dma((NZ,)), dma((8,)), dma((8,)),
            dma((NP,)), dma((4, 2)), dma((2, 4, 2)), dma((2, 4, 2)), dma((2, 3, 2)), dma((2, 3, 2)),
        ],
        compiler_params=pltpu.CompilerParams(
            collective_id=0, has_side_effects=True, vmem_limit_bytes=60 * 1024 * 1024
        ),
    )(
        receiver_spectra,
        reference_spectra,
        receiver_counts.reshape(1, NI),
        reference_counts.reshape(1, NJ),
        column_station.reshape(1, NJ),
        lag_window,
        observed,
        m,
        mq,
        mr,
    )


def solution(mesh):
    return jax.shard_map(
        shards,
        mesh=mesh,
        in_specs=(
            P("rcv", "ref"), P("rcv", "ref"), P("rcv"), P("ref"), P("ref"),
            P(None, "rcv", "ref"), P("rcv", "ref", None),
        ),
        out_specs=(P("rcv", "ref"), P("rcv", "ref")),
        check_vma=False,
    )
```

```python
import math

import jax
import jax.numpy as jnp
import numpy as np
from jax import lax
from jax.experimental import pallas as pl
from jax.experimental.pallas import tpu as pltpu
from jax.sharding import PartitionSpec as P

L = 512
S = 16
F = 256
NP = 8
NZ = 8
NI = 8
NJ = 256
NS = 4
NG = 4
MESH = pl.DeviceIdType.MESH
BF = jnp.bfloat16
F32 = jnp.float32

env_floor = 0.05
misfit_scale = 0.03125


def lag_table():
    freq_ids = np.arange(F, dtype=np.int64)[:, None]
    lag_ids = np.arange(L, dtype=np.int64)[None, :] - L // 2
    angle = ((freq_ids * lag_ids) % L).astype(np.float64) * (2.0 * math.pi / L)
    cosine = np.cos(angle) / math.sqrt(F)
    sine = np.sin(angle) / math.sqrt(F)
    real_rows = np.concatenate([cosine, sine], axis=1)
    imag_rows = np.concatenate([-sine, cosine], axis=1)
    stacked = np.stack([real_rows, imag_rows], axis=1).reshape(2 * F, 2 * L)
    return stacked.astype(np.float32)


def kernel(
    u_ref, v_ref, rc_ref, fc_ref, cs_ref, win_ref, obs_hbm, m_hbm, mt_hbm,
    rg_out, wg_out,
    um, us, ur, uq, vr, vq, ucr, ucq, bw, scr, scq, bt, bb, ninv, first, last,
    obs, m_ref, mt_ref, mq_ref, mr_ref, obst, xsr, xrr, xsq, xrq, gs, zs, zr,
    w, rbuf, lbuf, rgp, rgr,
    in_sem, u_send, u_recv, ur_send, ur_recv, uq_send, uq_recv,
    vx_send, vx_recv, vy_send, vy_recv, vr_send, vr_recv, vq_send, vq_recv,
    xr_send, xr_recv, xq_send, xq_recv, z_send, z_recv,
    g_send, g_recv, r_send, r_recv, l_send, l_recv,
):
    r = lax.axis_index("rcv")
    q = lax.axis_index("ref")
    p = r // NZ
    z = r % NZ
    x = p // 4
    y = p % 4
    right = p * NZ + (z + 1) % NZ
    left = p * NZ + (z + NZ - 1) % NZ
    partner = ((p + 4) % NP) * NZ + z

    def signal(rr, qq):
        pl.semaphore_signal(barrier, inc=1, device_id=(rr, qq), device_id_type=MESH)

    def remote(src, dst, send, recv, rr, qq):
        return pltpu.make_async_remote_copy(
            src_ref=src, dst_ref=dst, send_sem=send, recv_sem=recv,
            device_id=(rr, qq), device_id_type=MESH,
        )

    def plane(k):
        return ((p + k) % NP) * NZ + z

    def wait_bytes(ref, sem):
        pltpu.make_async_copy(ref, ref, sem).wait()

    barrier = pltpu.get_barrier_semaphore()
    for k in range(NP):
        for dq in range(4):
            if k or dq:
                signal(plane(k), (q + dq) % 4)
    signal(right, q)
    signal(left, q)

    loads = [pltpu.make_async_copy(obs_hbm.at[i], obs.at[i], in_sem.at[i]) for i in range(NI)]
    loads.append(pltpu.make_async_copy(mt_hbm, mt_ref, in_sem.at[NI]))
    loads.append(pltpu.make_async_copy(m_hbm, m_ref, in_sem.at[NI + 1]))
    for load in loads:
        load.start()

    eye = lax.broadcasted_iota(jnp.int32, (NI, NI), 0) == lax.broadcasted_iota(jnp.int32, (NI, NI), 1)
    rcounts = jnp.sum(jnp.where(eye, rc_ref[...].astype(F32), 0.0), axis=1, keepdims=True)
    pc = fc_ref[...].astype(F32)
    row_mask = (lax.broadcasted_iota(jnp.int32, (128, NJ), 0) % S).astype(F32) < pc
    mine = jnp.where(row_mask, v_ref[...].astype(F32), 0.0).astype(BF)
    vq[z, y] = mine[:, 0:128]
    vr[z, x] = mine[:, 128:256]
    seg_lane = (lax.broadcasted_iota(jnp.int32, (NI, 1024), 1) % S).astype(F32)
    keep = seg_lane < rcounts
    for half in range(2):
        part = u_ref[:, half * 1024 : (half + 1) * 1024].astype(F32)
        um[half, :, 0:1024] = jnp.where(keep, part, 0.0).astype(BF)
        um[half, :, 1024:1152] = jnp.broadcast_to(rcounts, (NI, 128)).astype(BF)

    pl.semaphore_wait(barrier, 4 * NP - 1 + 2)

    def give(own, src, dst, send, recv, rr, qq):
        @pl.when(jnp.logical_not(own))
        def _():
            remote(src, dst, send, recv, rr, qq).start()

        @pl.when(own)
        def _():
            pltpu.make_async_copy(src, dst, recv).start()

    def pass_on(buf, send, recv, zz, sub, to):
        remote(buf.at[zz, sub], buf.at[zz, sub], send.at[0], recv.at[zz, sub], to, q).start()

    def pass_r(zz, sub, to):
        pass_on(vr, vr_send, vr_recv, zz, sub, to)

    def pass_q(zz, sub, to):
        pass_on(vq, vq_send, vq_recv, zz, sub, to)

    remote(vr.at[z, x], vr.at[z, x], vx_send.at[0], vx_recv.at[0], partner, q).start()
    for k in range(1, 4):
        remote(
            vq.at[z, y], vq.at[z, y], vy_send.at[0], vy_recv.at[y], (x * 4 + (y + k) % 4) * NZ + z, q
        ).start()
    pass_r(z, x, right)
    pass_r(z, x, left)
    pass_q(z, y, right)
    pass_q(z, y, left)
    for half in range(2):
        for qq in range(4):
            yd = 2 * (q % 2) + half
            own = jnp.logical_and(yd == y, qq == q)
            give(
                own, um.at[half], ur.at[(y - yd + 4) % 4, q // 2], ur_send.at[half, qq],
                ur_recv.at[(y - yd + 4) % 4, q // 2], (x * 4 + yd) * NZ + z, qq,
            )
    for qq in range(4):
        xd = q // 2
        own = jnp.logical_and(xd == x, qq == q)
        give(
            own, um, uq.at[(x - xd + 2) % 2, q % 2], uq_send.at[qq],
            uq_recv.at[(x - xd + 2) % 2, q % 2], (xd * 4 + y) * NZ + z, qq,
        )
    order = cs_ref[...] - q * NJ
    stations = lax.broadcasted_iota(jnp.int32, (NJ, NJ), 0)
    onehot = jnp.where(stations == order, 1.0, 0.0).astype(BF)
    nt = (((1,), (1,)), ((), ()))
    begin = lax.dot_general(win_ref[0].astype(F32).astype(BF), onehot, nt, preferred_element_type=F32)
    span = lax.dot_general(win_ref[1].astype(F32).astype(BF), onehot, nt, preferred_element_type=F32)
    inv = 1.0 / jnp.minimum(rcounts, pc)
    for h in range(2):
        for i in range(NI):
            u, lanes, side = 4 * h + i // 2, pl.ds((i % 2) * 128, 128), slice(h * 128, (h + 1) * 128)
            first[u : u + 1, lanes] = begin[i : i + 1, side]
            last[u : u + 1, lanes] = begin[i : i + 1, side] + span[i : i + 1, side]
            ninv[u : u + 1, lanes] = inv[i : i + 1, side]
    def turn(ii, c):
        for par in range(2):
            seen = jnp.dot(onehot, obs[2 * ii + par], preferred_element_type=F32)
            seen = jnp.transpose(seen, (1, 0)).astype(BF)
            for h in range(2):
                obst[4 * h + ii, :, par * 128 : (par + 1) * 128] = seen[:, h * 128 : (h + 1) * 128]
        return c

    for i in range(NI):
        loads[i].wait()
    lax.fori_loop(0, 2, turn, 0)

    wait_bytes(vr.at[z, 1 - x], vx_recv.at[0])
    pass_r(z, 1 - x, right)
    pass_r(z, 1 - x, left)
    for k in (1, 3, 2):
        yy = (y + k) % 4
        wait_bytes(vq.at[z, yy], vy_recv.at[yy])
        pass_q(z, yy, right)
        pass_q(z, yy, left)
    for half in range(2):
        for qq in range(4):
            pp = 2 * q + half
            rr = pp * NZ + z
            own = jnp.logical_and(rr == r, qq == q)
            slot = (p - pp + NP) % NP
            give(own, um.at[half], us.at[slot], u_send.at[half, qq], u_recv.at[slot], rr, qq)

    def back(s):
        return (z + NZ - s) % NZ

    def ahead(s):
        return (z + s) % NZ

    def step_r(s):
        for k in range(2):
            sub = (x + k) % 2
            if s < 4:
                wait_bytes(vr.at[back(s), sub], vr_recv.at[back(s), sub])
                if s < 3:
                    pass_r(back(s), sub, right)
            wait_bytes(vr.at[ahead(s), sub], vr_recv.at[ahead(s), sub])
            if s < 4:
                pass_r(ahead(s), sub, left)

    def step_q(s):
        for k in (0, 1, 3, 2):
            sub = (y + k) % 4
            wait_bytes(vq.at[back(s), sub], vq_recv.at[back(s), sub])
            if s < 4:
                pass_q(back(s), sub, right)
                wait_bytes(vq.at[ahead(s), sub], vq_recv.at[ahead(s), sub])
                if s < 3:
                    pass_q(ahead(s), sub, left)

    row16 = lax.broadcasted_iota(jnp.int32, (16, 256), 0)
    lane256 = lax.broadcasted_iota(jnp.int32, (16, 256), 1)
    diag = (lane256 // 32) == (row16 // 2)
    mask0 = jnp.logical_and(diag, row16 % 2 == 0)
    mask1 = jnp.logical_and(diag, row16 % 2 == 1)

    def turned(uf):
        part = (lax.broadcasted_iota(jnp.int32, (NI, 1024), 1) // S) % 2
        return jnp.where(part == 0, pltpu.roll(uf, 1024 - S, 1), -pltpu.roll(uf, S, 1))

    def blocks(a, b, out):
        for i in range(NI):
            out(i, jnp.where(mask0, a[i : i + 1], jnp.where(mask1, b[i : i + 1], 0.0)).astype(BF))

    def ready_r(yk, c):
        for xx in range(2):
            wait_bytes(ur.at[yk, xx], ur_recv.at[yk, xx])
            uf = ur[yk, xx, :, 0:1024].astype(F32)
            ut = turned(uf)
            for zz in range(NZ):
                ucr[zz, yk, 0, :, xx * 128 : (xx + 1) * 128] = uf[:, zz * 128 : (zz + 1) * 128]
                ucr[zz, yk, 1, :, xx * 128 : (xx + 1) * 128] = ut[:, zz * 128 : (zz + 1) * 128]
        inverse = 1.0 / jnp.minimum(ur[yk, 0, :, 1024:1025].astype(F32), pc[:, 128:256])
        for i in range(NI):
            scr[yk, i] = jnp.broadcast_to(inverse[i : i + 1], (16, 128))
        return c

    def ready_q(xk, c):
        for b in range(2):
            wait_bytes(uq.at[xk, b], uq_recv.at[xk, b])
            for half in range(2):
                uf = uq[xk, b, half, :, 0:1024].astype(F32)
                ut = turned(uf)
                for zz in range(NZ):
                    ucq[zz, xk, b, 0, :, half * 128 : (half + 1) * 128] = uf[:, zz * 128 : (zz + 1) * 128]
                    ucq[zz, xk, b, 1, :, half * 128 : (half + 1) * 128] = ut[:, zz * 128 : (zz + 1) * 128]
        inverse = 1.0 / jnp.minimum(uq[xk, 0, 0, :, 1024:1025].astype(F32), pc[:, 0:128])
        for i in range(NI):
            scq[xk, i] = jnp.broadcast_to(inverse[i : i + 1], (16, 128))
        return c

    def cross_r(zz):
        for yk in range(4):
            def put(i, blk):
                bw[yk, i] = blk

            blocks(ucr[zz, yk, 0], ucr[zz, yk, 1], put)
        v = jnp.dot(bw[...].reshape(512, 256), vr[zz].reshape(256, 128), preferred_element_type=F32)
        v = (v * scr[...].reshape(512, 128)).astype(BF)
        for yk in range(4):
            for i in range(NI):
                rows = v[(yk * NI + i) * 16 : (yk * NI + i + 1) * 16]
                lanes = slice((i % 2) * 128, (i % 2 + 1) * 128)
                if yk:
                    xsr[zz, yk, i // 2, :, lanes] = rows
                else:
                    xrr[i // 2, y, zz, :, lanes] = rows
        for yk in range(1, 4):
            remote(
                xsr.at[zz, yk], xrr.at[:, y, zz], xr_send.at[zz], xr_recv.at[zz],
                (x * 4 + (y + yk) % 4) * NZ + z, q,
            ).start()

    def cross_q(zz):
        for b in range(2):
            for xk in range(2):
                def put(i, blk):
                    bw[2 * b + xk, i] = blk

                blocks(ucq[zz, xk, b, 0], ucq[zz, xk, b, 1], put)
        for b in range(2):
            v = jnp.dot(
                bw[2 * b : 2 * b + 2].reshape(256, 256), vq[zz, 2 * b : 2 * b + 2].reshape(256, 128),
                preferred_element_type=F32,
            )
            v = (v * scq[...].reshape(256, 128)).astype(BF)
            for xk in range(2):
                for i in range(NI):
                    rows = v[(xk * NI + i) * 16 : (xk * NI + i + 1) * 16]
                    lanes = slice((i % 2) * 128, (i % 2 + 1) * 128)
                    if xk:
                        xsq[zz, i // 2, b, :, lanes] = rows
                    else:
                        xrq[i // 2, x, zz, b, :, lanes] = rows
        remote(xsq.at[zz], xrq.at[:, x, zz], xq_send.at[zz], xq_recv.at[zz], partner, q).start()

    def crossings(cross, start, end):
        def one(j, c):
            cross((z + NZ + ((j + 1) // 2) * (2 * (j % 2) - 1)) % NZ)
            return c

        lax.fori_loop(start, end, one, 0)

    lax.fori_loop(2, 4, turn, 0)
    step_r(1)
    lax.fori_loop(0, 4, ready_r, 0)
    crossings(cross_r, 0, 3)
    step_q(1)
    lax.fori_loop(0, 2, ready_q, 0)
    crossings(cross_q, 0, 3)
    step_r(2)
    crossings(cross_r, 3, 5)
    step_q(2)
    crossings(cross_q, 3, 5)
    step_r(3)
    crossings(cross_r, 5, 7)
    step_q(3)
    crossings(cross_q, 5, 7)
    step_r(4)
    crossings(cross_r, 7, 8)

    for load in loads[NI:]:
        load.wait()
    here = lax.broadcasted_iota(jnp.int32, (2 * F, 2 * F), 0)
    n = lax.broadcasted_iota(jnp.int32, (2 * F, 2 * F), 1)
    from_r = n % 8 + 8 * ((n // 16) % 8) + 64 * (n // 128) + 256 * ((n // 8) % 2)
    from_q = n % 8 + 8 * ((n // 32) % 8) + 64 * ((n // 8) % 4) + 256 * (n // 256)
    for source, out in ((from_r, mr_ref), (from_q, mq_ref)):
        pick = jnp.where(here == source, 1.0, 0.0).astype(BF)
        for b in range(4):
            rows = slice(b * 256, (b + 1) * 256)
            out[rows, :] = jnp.dot(mt_ref[rows, :], pick, preferred_element_type=F32).astype(BF)

    step_q(4)
    crossings(cross_q, 7, 8)

    TB = 128
    def pairs(u, got, table):
        lo = first[pl.ds(u, 1), :]
        hi = last[pl.ds(u, 1), :]
        for b in range(L // TB):
            cor = jnp.dot(table[b * TB : (b + 1) * TB, :], got, preferred_element_type=F32)
            hil = jnp.dot(table[L + b * TB : L + (b + 1) * TB, :], got, preferred_element_type=F32)
            rs = lax.rsqrt(cor * cor + hil * hil + env_floor)
            lag = (lax.broadcasted_iota(jnp.int32, (TB, NJ), 0) + b * TB).astype(F32)
            inside = jnp.logical_and(lag >= lo, lag < hi)
            seen = obst[u, b * TB : (b + 1) * TB, :].astype(F32)
            wt = jnp.where(inside, (1.0 - seen * rs) * misfit_scale, 0.0)
            gs[b * TB : (b + 1) * TB, :] = (wt * cor).astype(BF)
            gs[L + b * TB : L + (b + 1) * TB, :] = (wt * hil).astype(BF)
        scale = ninv[pl.ds(u, 1), :]
        for b in range(4):
            back = jnp.dot(m_ref[b * 128 : (b + 1) * 128, :], gs[...], preferred_element_type=F32)
            zs[u, 2 * b : 2 * b + 2] = (back * scale).astype(BF).reshape(2, NG, 16, NJ)
        for k in range(1, NP):
            remote(
                zs.at[u, (p + k) % NP], zr.at[:, u, NP - k], z_send.at[u], z_recv.at[u], plane(k), q
            ).start()
        zr[:, u, 0] = zs[u, p]

    def pairs_r(ii, c):
        pairs(4 + ii, xrr[ii].reshape(2 * F, NJ), mr_ref)
        return c

    def pairs_q(ii, c):
        pairs(ii, xrq[ii].reshape(2 * F, NJ), mq_ref)
        return c

    for zz in range(NZ):
        wait_bytes(xsr.at[zz, 1:4], xr_recv.at[zz])
    lax.fori_loop(0, 4, pairs_r, 0)
    for zz in range(NZ):
        wait_bytes(xsq.at[zz], xq_recv.at[zz])
    lax.fori_loop(0, 4, pairs_q, 0)

    def operand(k, c):
        wait_bytes(us.at[k], u_recv.at[k])
        uf = us[k, :, 0:1024].astype(F32)
        ut = turned(uf)
        for g in range(NG):
            def put(i, blk):
                bt[g, i // 2, i % 2, pl.ds(k * 16, 16), :] = blk

            blocks(uf[:, g * 256 : (g + 1) * 256], ut[:, g * 256 : (g + 1) * 256], put)
        return c

    lax.fori_loop(0, NP, operand, 0)

    def flip(g, c):
        for ii in range(4):
            for par in range(2):
                bb[g, par, :, ii * 128 : (ii + 1) * 128] = jnp.transpose(
                    bt[g, ii, par].astype(F32), (1, 0)
                ).astype(BF)
        return c

    lax.fori_loop(0, NG, flip, 0)

    def arrived(u):
        wait_bytes(zs.at[u, 1:NP], z_recv.at[u])

    def sums(h, start, end):
        size = (end - start) * 128
        for g in range(NG):
            part = None
            for par in range(2):
                got = zr[g, 4 * h + start : 4 * h + end, :, :, par * 128 : (par + 1) * 128].reshape(size, 128)
                one = jnp.dot(bb[g, par, :, start * 128 : end * 128], got, preferred_element_type=F32)
                part = one if part is None else part + one
            part = part.reshape(2, 128, 128)
            if start:
                part = part + w[h, 2 * g : 2 * g + 2]
            w[h, 2 * g : 2 * g + 2] = part

    def ring(h, s):
        for n in range(NS):
            rows = slice(n * (128 // NS), (n + 1) * (128 // NS))
            if s > 0:
                wait_bytes(rbuf.at[h, s - 1, rows], r_recv.at[h, s - 1, n])
                rbuf[h, s - 1, rows] = rbuf[h, s - 1, rows] + w[h, (z + 4 - s) % NZ, rows]
            src = rbuf.at[h, s - 1, rows] if s > 0 else w.at[h, (z + 4) % NZ, rows]
            remote(src, rbuf.at[h, s, rows], r_send.at[h, s, n], r_recv.at[h, s, n], right, q).start()
            if s > 2:
                continue
            if s > 0:
                wait_bytes(lbuf.at[h, s - 1, rows], l_recv.at[h, s - 1, n])
                lbuf[h, s - 1, rows] = lbuf[h, s - 1, rows] + w[h, (z + 5 + s) % NZ, rows]
            src = lbuf.at[h, s - 1, rows] if s > 0 else w.at[h, (z + 5) % NZ, rows]
            remote(src, lbuf.at[h, s, rows], l_send.at[h, s, n], l_recv.at[h, s, n], left, q).start()

    def ring_end(h):
        for n in range(NS):
            rows = slice(n * (128 // NS), (n + 1) * (128 // NS))
            wait_bytes(rbuf.at[h, 3, rows], r_recv.at[h, 3, n])
            wait_bytes(lbuf.at[h, 2, rows], l_recv.at[h, 2, n])
            keep = row_mask[rows, h * 128 : (h + 1) * 128]
            done = w[h, z, rows] + rbuf[h, 3, rows] + lbuf[h, 2, rows]
            wg_out[rows, h * 128 : (h + 1) * 128] = jnp.where(keep, done, 0.0)

    lane8 = (lax.broadcasted_iota(jnp.int32, (NP, 256), 1) // S) % 2

    def receivers(ii):
        for g in range(NG):
            for par in range(2):
                t = None
                for h in range(2):
                    got = zr[g, 4 * h + ii, :, :, par * 128 : (par + 1) * 128].reshape(128, 128)
                    held = vr[2 * g : 2 * g + 2, x] if h else vq[2 * g : 2 * g + 2, y]
                    block = held.reshape(256, 128)
                    part = lax.dot_general(got, block, nt, preferred_element_type=F32)
                    t = part if t is None else t + part
                t = t.reshape(NP, 16, 256)
                a0 = jnp.sum(jnp.where(mask0[None], t, 0.0), axis=1)
                a1 = jnp.sum(jnp.where(mask1[None], t, 0.0), axis=1)
                rg = a0 + jnp.where(lane8 == 0, -pltpu.roll(a1, 256 - S, 1), pltpu.roll(a1, S, 1))
                i = 2 * ii + par
                for k in range(NP):
                    rgp[k, i : i + 1, g * 256 : (g + 1) * 256] = rg[k : k + 1]

    for u in range(4, 8):
        arrived(u)
    sums(1, 0, 4)
    ring(1, 0)
    for s in range(1, 4):
        arrived(s - 1)
        receivers(s - 1)
        ring(1, s)
    sums(0, 0, 3)
    arrived(3)
    sums(0, 3, 4)
    ring(0, 0)
    receivers(3)
    for k in range(NP):
        own = jnp.logical_and(k == 0, p // 2 == q)

        @pl.when(jnp.logical_not(own))
        def _():
            remote(rgp.at[k], rgr.at[q, p % 2], g_send.at[k], g_recv.at[q, p % 2], plane(k), p // 2).start()

        @pl.when(own)
        def _():
            pltpu.make_async_copy(rgp.at[k], rgr.at[q, p % 2], g_recv.at[q, p % 2]).start()

    ring(0, 1)
    ring_end(1)
    ring(0, 2)
    ring(0, 3)
    for half in range(2):
        for qq in range(4):
            wait_bytes(rgr.at[qq, half], g_recv.at[qq, half])
        total = (rgr[0, half] + rgr[1, half]) + (rgr[2, half] + rgr[3, half])
        rg_out[:, half * 1024 : (half + 1) * 1024] = jnp.where(keep, total, 0.0)
    ring_end(0)

    for half in range(2):
        for qq in range(4):
            own = jnp.logical_and((2 * q + half) * NZ + z == r, qq == q)

            @pl.when(jnp.logical_not(own))
            def _():
                wait_bytes(um.at[half], u_send.at[half, qq])

    for half in range(2):
        for qq in range(4):
            own = jnp.logical_and(2 * (q % 2) + half == y, qq == q)

            @pl.when(jnp.logical_not(own))
            def _():
                wait_bytes(um.at[half], ur_send.at[half, qq])

    for qq in range(4):
        own = jnp.logical_and(q // 2 == x, qq == q)

        @pl.when(jnp.logical_not(own))
        def _():
            wait_bytes(um, uq_send.at[qq])

    wait_bytes(vr.at[z, x], vx_send.at[0])
    wait_bytes(vq.at[z, 1:4], vy_send.at[0])
    wait_bytes(vr.at[1:NZ], vr_send.at[0])
    wait_bytes(vq.at[1:NZ], vq_send.at[0])
    for zz in range(NZ):
        wait_bytes(xsr.at[zz, 1:4], xr_send.at[zz])
        wait_bytes(xsq.at[zz], xq_send.at[zz])
    for u in range(8):
        wait_bytes(zs.at[u, 1:NP], z_send.at[u])
    for k in range(NP):
        own = jnp.logical_and(k == 0, p // 2 == q)

        @pl.when(jnp.logical_not(own))
        def _():
            wait_bytes(rgp.at[k], g_send.at[k])

    for h in range(2):
        for n in range(NS):
            rows = slice(n * (128 // NS), (n + 1) * (128 // NS))
            for s in range(4):
                wait_bytes(rbuf.at[h, s, rows], r_send.at[h, s, n])
            for s in range(3):
                wait_bytes(lbuf.at[h, s, rows], l_send.at[h, s, n])


def shards(receiver_spectra, reference_spectra, receiver_counts, reference_counts, column_station, lag_window, observed):
    table = lag_table()
    m = jnp.asarray(table, dtype=BF)
    mt = jnp.asarray(np.ascontiguousarray(table.T), dtype=BF)
    vmem = pl.BlockSpec(memory_space=pltpu.VMEM)
    hbm = pl.BlockSpec(memory_space=pl.ANY)
    dma = pltpu.SemaphoreType.DMA
    return pl.pallas_call(
        kernel,
        out_shape=(
            pltpu.VMEM((NI, 2048), F32),
            pltpu.VMEM((128, NJ), F32),
        ),
        in_specs=[vmem] * 6 + [hbm] * 3,
        out_specs=(pl.BlockSpec(memory_space=pltpu.MemorySpace.VMEM), pl.BlockSpec(memory_space=pltpu.MemorySpace.VMEM)),
        scratch_shapes=[
            pltpu.VMEM((2, NI, 1152), BF),
            pltpu.VMEM((NP, NI, 1152), BF),
            pltpu.VMEM((4, 2, NI, 1152), BF),
            pltpu.VMEM((2, 2, 2, NI, 1152), BF),
            pltpu.VMEM((NZ, 2, 128, 128), BF),
            pltpu.VMEM((NZ, 4, 128, 128), BF),
            pltpu.VMEM((NZ, 4, 2, NI, 256), F32),
            pltpu.VMEM((NZ, 2, 2, 2, NI, 256), F32),
            pltpu.VMEM((4, NI, 16, 256), BF),
            pltpu.VMEM((4, NI, 16, 128), F32),
            pltpu.VMEM((2, NI, 16, 128), F32),
            pltpu.VMEM((NG, 4, 2, 128, 256), BF),
            pltpu.VMEM((NG, 2, 256, 512), BF),
            pltpu.VMEM((8, NJ), F32),
            pltpu.VMEM((8, NJ), F32),
            pltpu.VMEM((8, NJ), F32),
            pltpu.VMEM((NI, NJ, L), BF),
            pltpu.VMEM((2 * F, 2 * L), BF),
            pltpu.VMEM((2 * L, 2 * F), BF),
            pltpu.VMEM((2 * L, 2 * F), BF),
            pltpu.VMEM((2 * L, 2 * F), BF),
            pltpu.VMEM((8, L, NJ), BF),
            pltpu.VMEM((NZ, 4, 4, 16, NJ), BF),
            pltpu.VMEM((4, 4, NZ, 16, NJ), BF),
            pltpu.VMEM((NZ, 4, 2, 16, NJ), BF),
            pltpu.VMEM((4, 2, NZ, 2, 16, NJ), BF),
            pltpu.VMEM((2 * L, NJ), BF),
            pltpu.VMEM((8, NP, NG, 16, NJ), BF),
            pltpu.VMEM((NG, 8, NP, 16, NJ), BF),
            pltpu.VMEM((2, NZ, 128, 128), F32),
            pltpu.VMEM((2, 4, 128, 128), F32),
            pltpu.VMEM((2, 3, 128, 128), F32),
            pltpu.VMEM((NP, NI, 1024), F32),
            pltpu.VMEM((4, 2, NI, 1024), F32),
            dma((NI + 2,)), dma((2, 4)), dma((NP,)), dma((2, 4)), dma((4, 2)), dma((4,)), dma((2, 2)),
            dma((1,)), dma((1,)), dma((1,)), dma((4,)), dma((1,)), dma((NZ, 2)), dma((1,)), dma((NZ, 4)),
            dma((NZ,)), dma((NZ,)), dma((NZ,)), dma((NZ,)), dma((8,)), dma((8,)),
            dma((NP,)), dma((4, 2)), dma((2, 4, NS)), dma((2, 4, NS)), dma((2, 3, NS)), dma((2, 3, NS)),
        ],
        compiler_params=pltpu.CompilerParams(
            collective_id=0, has_side_effects=True, vmem_limit_bytes=60 * 1024 * 1024
        ),
    )(
        receiver_spectra,
        reference_spectra,
        receiver_counts.reshape(1, NI),
        reference_counts.reshape(1, NJ),
        column_station.reshape(1, NJ),
        lag_window,
        observed,
        m,
        mt,
    )


def solution(mesh):
    return jax.shard_map(
        shards,
        mesh=mesh,
        in_specs=(
            P("rcv", "ref"), P("rcv", "ref"), P("rcv"), P("ref"), P("ref"),
            P(None, "rcv", "ref"), P("rcv", "ref", None),
        ),
        out_specs=(P("rcv", "ref"), P("rcv", "ref")),
        check_vma=False,
    )
```

```python
import math

import jax
import jax.numpy as jnp
import numpy as np
from jax import lax
from jax.experimental import pallas as pl
from jax.experimental.pallas import tpu as pltpu
from jax.sharding import PartitionSpec as P

L = 512
S = 16
F = 256
NP = 8
NZ = 8
NI = 8
NJ = 256
NG = 4
MESH = pl.DeviceIdType.MESH
BF = jnp.bfloat16
F32 = jnp.float32

env_floor = 0.05
misfit_scale = 0.03125


def lag_table():
    freq_ids = np.arange(F, dtype=np.int64)[:, None]
    lag_ids = np.arange(L, dtype=np.int64)[None, :] - L // 2
    angle = ((freq_ids * lag_ids) % L).astype(np.float64) * (2.0 * math.pi / L)
    cosine = np.cos(angle) / math.sqrt(F)
    sine = np.sin(angle) / math.sqrt(F)
    real_rows = np.concatenate([cosine, sine], axis=1)
    imag_rows = np.concatenate([-sine, cosine], axis=1)
    stacked = np.stack([real_rows, imag_rows], axis=1).reshape(2 * F, 2 * L)
    return stacked.astype(np.float32)


def kernel(
    u_ref, v_ref, rc_ref, fc_ref, cs_ref, win_ref, obs_hbm, m_hbm, mt_hbm,
    rg_out, wg_out,
    um, us, ur, uq, vr, vq, ucr, ucq, bw, scr, scq, bt, bb, ninv, first, last,
    obs, m_ref, mt_ref, mq_ref, mr_ref, obst, xsr, xrr, xsq, xrq, gs, zs, zr,
    w, tbuf, rgp, rgr,
    in_sem, u_send, u_recv, ur_send, ur_recv, uq_send, uq_recv,
    vx_send, vx_recv, vy_send, vy_recv, vr_send, vr_recv, vq_send, vq_recv,
    xr_send, xr_recv, xq_send, xq_recv, z_send, z_recv,
    g_send, g_recv, t_send, t_recv,
):
    r = lax.axis_index("rcv")
    q = lax.axis_index("ref")
    p = r // NZ
    z = r % NZ
    x = p // 4
    y = p % 4
    right = p * NZ + (z + 1) % NZ
    left = p * NZ + (z + NZ - 1) % NZ
    partner = ((p + 4) % NP) * NZ + z

    def signal(rr, qq):
        pl.semaphore_signal(barrier, inc=1, device_id=(rr, qq), device_id_type=MESH)

    def remote(src, dst, send, recv, rr, qq):
        return pltpu.make_async_remote_copy(
            src_ref=src, dst_ref=dst, send_sem=send, recv_sem=recv,
            device_id=(rr, qq), device_id_type=MESH,
        )

    def plane(k):
        return ((p + k) % NP) * NZ + z

    def wait_bytes(ref, sem):
        pltpu.make_async_copy(ref, ref, sem).wait()

    barrier = pltpu.get_barrier_semaphore()
    for k in range(NP):
        for dq in range(4):
            if k or dq:
                signal(plane(k), (q + dq) % 4)
    for k in (1, 2, 6, 7):
        signal(p * NZ + (z + k) % NZ, q)

    loads = [pltpu.make_async_copy(obs_hbm.at[i], obs.at[i], in_sem.at[0]) for i in range(NI)]
    loads.append(pltpu.make_async_copy(mt_hbm, mt_ref, in_sem.at[1]))
    loads.append(pltpu.make_async_copy(m_hbm, m_ref, in_sem.at[2]))
    for load in loads:
        load.start()

    eye = lax.broadcasted_iota(jnp.int32, (NI, NI), 0) == lax.broadcasted_iota(jnp.int32, (NI, NI), 1)
    rcounts = jnp.sum(jnp.where(eye, rc_ref[...].astype(F32), 0.0), axis=1, keepdims=True)
    pc = fc_ref[...].astype(F32)
    row_mask = (lax.broadcasted_iota(jnp.int32, (128, NJ), 0) % S).astype(F32) < pc
    mine = jnp.where(row_mask, v_ref[...].astype(F32), 0.0).astype(BF)
    vq[z, y] = mine[:, 0:128]
    vr[z, x] = mine[:, 128:256]
    seg_lane = (lax.broadcasted_iota(jnp.int32, (NI, 1024), 1) % S).astype(F32)
    keep = seg_lane < rcounts
    for half in range(2):
        part = u_ref[:, half * 1024 : (half + 1) * 1024].astype(F32)
        um[half, :, 0:1024] = jnp.where(keep, part, 0.0).astype(BF)
        um[half, :, 1024:1152] = jnp.broadcast_to(rcounts, (NI, 128)).astype(BF)

    pl.semaphore_wait(barrier, 4 * NP - 1 + 4)

    def give(own, src, dst, send, recv, rr, qq):
        @pl.when(jnp.logical_not(own))
        def _():
            remote(src, dst, send, recv, rr, qq).start()

        @pl.when(own)
        def _():
            pltpu.make_async_copy(src, dst, recv).start()

    def pass_on(buf, send, recv, zz, sub, to):
        remote(buf.at[zz, sub], buf.at[zz, sub], send.at[0], recv.at[zz, sub], to, q).start()

    def pass_r(zz, sub, to):
        pass_on(vr, vr_send, vr_recv, zz, sub, to)

    def pass_q(zz, sub, to):
        pass_on(vq, vq_send, vq_recv, zz, sub, to)

    remote(vr.at[z, x], vr.at[z, x], vx_send.at[0], vx_recv.at[0], partner, q).start()
    for k in range(1, 4):
        remote(
            vq.at[z, y], vq.at[z, y], vy_send.at[0], vy_recv.at[y], (x * 4 + (y + k) % 4) * NZ + z, q
        ).start()
    pass_r(z, x, right)
    pass_r(z, x, left)
    pass_q(z, y, right)
    pass_q(z, y, left)
    for half in range(2):
        for qq in range(4):
            yd = 2 * (q % 2) + half
            own = jnp.logical_and(yd == y, qq == q)
            give(
                own, um.at[half], ur.at[(y - yd + 4) % 4, q // 2], ur_send.at[0], ur_recv.at[0],
                (x * 4 + yd) * NZ + z, qq,
            )
    for qq in range(4):
        xd = q // 2
        own = jnp.logical_and(xd == x, qq == q)
        give(
            own, um, uq.at[2 * ((x - xd + 2) % 2) + q % 2], uq_send.at[0], uq_recv.at[0],
            (xd * 4 + y) * NZ + z, qq,
        )
    order = cs_ref[...] - q * NJ
    stations = lax.broadcasted_iota(jnp.int32, (NJ, NJ), 0)
    onehot = jnp.where(stations == order, 1.0, 0.0).astype(BF)
    nt = (((1,), (1,)), ((), ()))
    begin = lax.dot_general(win_ref[0].astype(F32).astype(BF), onehot, nt, preferred_element_type=F32)
    span = lax.dot_general(win_ref[1].astype(F32).astype(BF), onehot, nt, preferred_element_type=F32)
    inv = 1.0 / jnp.minimum(rcounts, pc)
    for h in range(2):
        for i in range(NI):
            u, lanes, side = 4 * h + i // 2, pl.ds((i % 2) * 128, 128), slice(h * 128, (h + 1) * 128)
            first[u : u + 1, lanes] = begin[i : i + 1, side]
            last[u : u + 1, lanes] = begin[i : i + 1, side] + span[i : i + 1, side]
            ninv[u : u + 1, lanes] = inv[i : i + 1, side]
    def turn(ii, c):
        for par in range(2):
            seen = jnp.dot(onehot, obs[2 * ii + par], preferred_element_type=F32)
            seen = jnp.transpose(seen, (1, 0)).astype(BF)
            for h in range(2):
                obst[4 * h + ii, :, par * 128 : (par + 1) * 128] = seen[:, h * 128 : (h + 1) * 128]
        return c

    wait_bytes(obs, in_sem.at[0])
    lax.fori_loop(0, 2, turn, 0)

    wait_bytes(vr.at[z, 1 - x], vx_recv.at[0])
    pass_r(z, 1 - x, right)
    pass_r(z, 1 - x, left)
    for k in (1, 3, 2):
        yy = (y + k) % 4
        wait_bytes(vq.at[z, yy], vy_recv.at[yy])
        pass_q(z, yy, right)
        pass_q(z, yy, left)
    for half in range(2):
        for qq in range(4):
            pp = 2 * q + half
            rr = pp * NZ + z
            own = jnp.logical_and(rr == r, qq == q)
            slot = (p - pp + NP) % NP
            give(own, um.at[half], us.at[slot], u_send.at[0], u_recv.at[0], rr, qq)

    def back(s):
        return (z + NZ - s) % NZ

    def ahead(s):
        return (z + s) % NZ

    def step_r(s):
        for k in range(2):
            sub = (x + k) % 2
            if s < 4:
                wait_bytes(vr.at[back(s), sub], vr_recv.at[back(s), sub])
                if s < 3:
                    pass_r(back(s), sub, right)
            wait_bytes(vr.at[ahead(s), sub], vr_recv.at[ahead(s), sub])
            if s < 4:
                pass_r(ahead(s), sub, left)

    def step_q(s):
        for k in (0, 1, 3, 2):
            sub = (y + k) % 4
            wait_bytes(vq.at[back(s), sub], vq_recv.at[back(s), sub])
            if s < 4:
                pass_q(back(s), sub, right)
                wait_bytes(vq.at[ahead(s), sub], vq_recv.at[ahead(s), sub])
                if s < 3:
                    pass_q(ahead(s), sub, left)

    row16 = lax.broadcasted_iota(jnp.int32, (16, 256), 0)
    lane256 = lax.broadcasted_iota(jnp.int32, (16, 256), 1)
    diag = (lane256 // 32) == (row16 // 2)
    mask0 = jnp.logical_and(diag, row16 % 2 == 0)
    mask1 = jnp.logical_and(diag, row16 % 2 == 1)

    def turned(uf):
        part = (lax.broadcasted_iota(jnp.int32, (NI, 1024), 1) // S) % 2
        return jnp.where(part == 0, pltpu.roll(uf, 1024 - S, 1), -pltpu.roll(uf, S, 1))

    def blocks(a, b, out):
        for i in range(NI):
            out(i, jnp.where(mask0, a[i : i + 1], jnp.where(mask1, b[i : i + 1], 0.0)).astype(BF))

    def ready_r(yk, c):
        for xx in range(2):
            uf = ur[yk, xx, :, 0:1024].astype(F32)
            ut = turned(uf)
            for zz in range(NZ):
                ucr[zz, yk, 0, :, xx * 128 : (xx + 1) * 128] = uf[:, zz * 128 : (zz + 1) * 128]
                ucr[zz, yk, 1, :, xx * 128 : (xx + 1) * 128] = ut[:, zz * 128 : (zz + 1) * 128]
        inverse = 1.0 / jnp.minimum(ur[yk, 0, :, 1024:1025].astype(F32), pc[:, 128:256])
        for i in range(NI):
            scr[yk, i] = jnp.broadcast_to(inverse[i : i + 1], (16, 128))
        return c

    def ready_q(xk, c):
        for b in range(2):
            for half in range(2):
                uf = uq[2 * xk + b, half, :, 0:1024].astype(F32)
                ut = turned(uf)
                for zz in range(NZ):
                    ucq[zz, xk, b, 0, :, half * 128 : (half + 1) * 128] = uf[:, zz * 128 : (zz + 1) * 128]
                    ucq[zz, xk, b, 1, :, half * 128 : (half + 1) * 128] = ut[:, zz * 128 : (zz + 1) * 128]
        inverse = 1.0 / jnp.minimum(uq[2 * xk, 0, :, 1024:1025].astype(F32), pc[:, 0:128])
        for i in range(NI):
            scq[xk, i] = jnp.broadcast_to(inverse[i : i + 1], (16, 128))
        return c

    def cross_r(zz):
        for yk in range(4):
            def put(i, blk):
                bw[yk, i] = blk

            blocks(ucr[zz, yk, 0], ucr[zz, yk, 1], put)
        v = jnp.dot(bw[...].reshape(512, 256), vr[zz].reshape(256, 128), preferred_element_type=F32)
        v = (v * scr[...].reshape(512, 128)).astype(BF)
        for yk in range(4):
            for i in range(NI):
                rows = v[(yk * NI + i) * 16 : (yk * NI + i + 1) * 16]
                lanes = slice((i % 2) * 128, (i % 2 + 1) * 128)
                if yk:
                    xsr[zz, yk, i // 2, :, lanes] = rows
                else:
                    xrr[i // 2, y, zz, :, lanes] = rows
        for yk in range(1, 4):
            remote(
                xsr.at[zz, yk], xrr.at[:, y, zz], xr_send.at[0], xr_recv.at[0],
                (x * 4 + (y + yk) % 4) * NZ + z, q,
            ).start()

    def cross_q(zz):
        for b in range(2):
            for xk in range(2):
                def put(i, blk):
                    bw[2 * b + xk, i] = blk

                blocks(ucq[zz, xk, b, 0], ucq[zz, xk, b, 1], put)
        for b in range(2):
            v = jnp.dot(
                bw[2 * b : 2 * b + 2].reshape(256, 256), vq[zz, 2 * b : 2 * b + 2].reshape(256, 128),
                preferred_element_type=F32,
            )
            v = (v * scq[...].reshape(256, 128)).astype(BF)
            for xk in range(2):
                for i in range(NI):
                    rows = v[(xk * NI + i) * 16 : (xk * NI + i + 1) * 16]
                    lanes = slice((i % 2) * 128, (i % 2 + 1) * 128)
                    if xk:
                        xsq[zz, i // 2, b, :, lanes] = rows
                    else:
                        xrq[i // 2, x, zz, b, :, lanes] = rows
        remote(xsq.at[zz], xrq.at[:, x, zz], xq_send.at[0], xq_recv.at[0], partner, q).start()

    def crossings(cross, start, end):
        def one(j, c):
            cross((z + NZ + ((j + 1) // 2) * (2 * (j % 2) - 1)) % NZ)
            return c

        lax.fori_loop(start, end, one, 0)

    lax.fori_loop(2, 4, turn, 0)
    step_r(1)
    wait_bytes(ur, ur_recv.at[0])
    lax.fori_loop(0, 4, ready_r, 0)
    crossings(cross_r, 0, 3)
    step_r(2)
    crossings(cross_r, 3, 5)
    step_q(1)
    wait_bytes(uq, uq_recv.at[0])
    lax.fori_loop(0, 2, ready_q, 0)
    crossings(cross_q, 0, 3)
    step_r(3)
    crossings(cross_r, 5, 7)
    step_q(2)
    crossings(cross_q, 3, 5)

    here = lax.broadcasted_iota(jnp.int32, (2 * F, 2 * F), 0)
    n = lax.broadcasted_iota(jnp.int32, (2 * F, 2 * F), 1)
    from_r = n % 8 + 8 * ((n // 16) % 8) + 64 * (n // 128) + 256 * ((n // 8) % 2)
    from_q = n % 8 + 8 * ((n // 32) % 8) + 64 * ((n // 8) % 4) + 256 * (n // 256)

    def reorder(source, out):
        pick = jnp.where(here == source, 1.0, 0.0).astype(BF)
        for b in range(4):
            rows = slice(b * 256, (b + 1) * 256)
            out[rows, :] = jnp.dot(mt_ref[rows, :], pick, preferred_element_type=F32).astype(BF)

    for load in loads[NI:]:
        load.wait()
    reorder(from_r, mr_ref)
    step_r(4)
    crossings(cross_r, 7, 8)
    step_q(3)
    crossings(cross_q, 5, 7)
    reorder(from_q, mq_ref)

    TB = 128
    def pairs(u, got, table):
        lo = first[pl.ds(u, 1), :]
        hi = last[pl.ds(u, 1), :]
        for b in range(L // TB):
            cor = jnp.dot(table[b * TB : (b + 1) * TB, :], got, preferred_element_type=F32)
            hil = jnp.dot(table[L + b * TB : L + (b + 1) * TB, :], got, preferred_element_type=F32)
            rs = lax.rsqrt(cor * cor + hil * hil + env_floor)
            lag = (lax.broadcasted_iota(jnp.int32, (TB, NJ), 0) + b * TB).astype(F32)
            inside = jnp.logical_and(lag >= lo, lag < hi)
            seen = obst[u, b * TB : (b + 1) * TB, :].astype(F32)
            wt = jnp.where(inside, (1.0 - seen * rs) * misfit_scale, 0.0)
            gs[b * TB : (b + 1) * TB, :] = (wt * cor).astype(BF)
            gs[L + b * TB : L + (b + 1) * TB, :] = (wt * hil).astype(BF)
        scale = ninv[pl.ds(u, 1), :]
        for b in range(4):
            back = jnp.dot(m_ref[b * 128 : (b + 1) * 128, :], gs[...], preferred_element_type=F32)
            zs[u, 2 * b : 2 * b + 2] = (back * scale).astype(BF).reshape(2, NG, 16, NJ)
        for k in (4, 5, 7, 6, 1, 3, 2):
            remote(
                zs.at[u, (p + k) % NP], zr.at[:, u, NP - k], z_send.at[u // 4], z_recv.at[u], plane(k), q
            ).start()
        zr[:, u, 0] = zs[u, p]

    def pairs_r(ii, c):
        pairs(4 + ii, xrr[ii].reshape(2 * F, NJ), mr_ref)
        return c

    def pairs_q(ii, c):
        pairs(ii, xrq[ii].reshape(2 * F, NJ), mq_ref)
        return c

    wait_bytes(xsr.at[:, 1:4], xr_recv.at[0])
    lax.fori_loop(0, 4, pairs_r, 0)
    step_q(4)
    crossings(cross_q, 7, 8)
    wait_bytes(xsq, xq_recv.at[0])
    lax.fori_loop(0, 4, pairs_q, 0)

    def operand(k, c):
        uf = us[k, :, 0:1024].astype(F32)
        ut = turned(uf)
        for g in range(NG):
            def put(i, blk):
                bt[g, i // 2, i % 2, pl.ds(k * 16, 16), :] = blk

            blocks(uf[:, g * 256 : (g + 1) * 256], ut[:, g * 256 : (g + 1) * 256], put)
        return c

    wait_bytes(us, u_recv.at[0])
    lax.fori_loop(0, NP, operand, 0)

    def flip(g, c):
        for ii in range(4):
            for par in range(2):
                bb[g, par, :, ii * 128 : (ii + 1) * 128] = jnp.transpose(
                    bt[g, ii, par].astype(F32), (1, 0)
                ).astype(BF)
        return c

    lax.fori_loop(0, NG, flip, 0)

    def arrived(u):
        wait_bytes(zs.at[u, 1:NP], z_recv.at[u])

    def sums(h, start, end):
        size = (end - start) * 128
        for g in range(NG):
            part = None
            for par in range(2):
                got = zr[g, 4 * h + start : 4 * h + end, :, :, par * 128 : (par + 1) * 128].reshape(size, 128)
                one = jnp.dot(bb[g, par, :, start * 128 : end * 128], got, preferred_element_type=F32)
                part = one if part is None else part + one
            part = part.reshape(2, 128, 128)
            if start:
                part = part + w[h, 2 * g : 2 * g + 2]
            w[h, 2 * g : 2 * g + 2] = part

    def toward(n, src, dst, h, to):
        remote(src, dst, t_send.at[h], t_recv.at[h, n], p * NZ + (z + NZ + to) % NZ, q).start()

    def tree_start(h):
        for n, m, to in ((0, 4, 2), (1, 3, 1), (2, 5, -1), (3, 1, 1), (4, 7, -1)):
            toward(n, w.at[h, (z + m) % NZ], tbuf.at[h, n], h, to)

    def tree_middle(h):
        wait_bytes(tbuf.at[h, 2], t_recv.at[h, 2])
        tbuf[h, 2] = tbuf[h, 2] + w[h, (z + 6) % NZ]
        toward(6, tbuf.at[h, 2], tbuf.at[h, 6], h, -2)
        wait_bytes(tbuf.at[h, 1], t_recv.at[h, 1])
        wait_bytes(tbuf.at[h, 0], t_recv.at[h, 0])
        tbuf[h, 0] = tbuf[h, 0] + (tbuf[h, 1] + w[h, (z + 2) % NZ])
        toward(5, tbuf.at[h, 0], tbuf.at[h, 5], h, 2)

    def tree_end(h):
        for n in (3, 4, 6, 5):
            wait_bytes(tbuf.at[h, n], t_recv.at[h, n])
        done = (w[h, z] + tbuf[h, 3]) + (tbuf[h, 4] + tbuf[h, 6]) + tbuf[h, 5]
        cols = slice(h * 128, (h + 1) * 128)
        wg_out[:, cols] = jnp.where(row_mask[:, cols], done, 0.0)

    lane8 = (lax.broadcasted_iota(jnp.int32, (NP, 256), 1) // S) % 2

    def receivers(ii):
        for g in range(NG):
            for par in range(2):
                t = None
                for h in range(2):
                    got = zr[g, 4 * h + ii, :, :, par * 128 : (par + 1) * 128].reshape(128, 128)
                    held = vr[2 * g : 2 * g + 2, x] if h else vq[2 * g : 2 * g + 2, y]
                    block = held.reshape(256, 128)
                    part = lax.dot_general(got, block, nt, preferred_element_type=F32)
                    t = part if t is None else t + part
                t = t.reshape(NP, 16, 256)
                a0 = jnp.sum(jnp.where(mask0[None], t, 0.0), axis=1)
                a1 = jnp.sum(jnp.where(mask1[None], t, 0.0), axis=1)
                rg = a0 + jnp.where(lane8 == 0, -pltpu.roll(a1, 256 - S, 1), pltpu.roll(a1, S, 1))
                i = 2 * ii + par
                for k in range(NP):
                    rgp[k, i : i + 1, g * 256 : (g + 1) * 256] = rg[k : k + 1]

    for u in range(4, 8):
        arrived(u)
    sums(1, 0, 4)
    tree_start(1)
    arrived(0)
    receivers(0)
    tree_middle(1)
    arrived(1)
    receivers(1)
    arrived(2)
    receivers(2)
    sums(0, 0, 3)
    tree_end(1)
    arrived(3)
    sums(0, 3, 4)
    tree_start(0)
    receivers(3)
    for k in range(NP):
        own = jnp.logical_and(k == 0, p // 2 == q)

        @pl.when(jnp.logical_not(own))
        def _():
            remote(rgp.at[k], rgr.at[q, p % 2], g_send.at[0], g_recv.at[0], plane(k), p // 2).start()

        @pl.when(own)
        def _():
            pltpu.make_async_copy(rgp.at[k], rgr.at[q, p % 2], g_recv.at[0]).start()

    tree_middle(0)
    wait_bytes(rgr, g_recv.at[0])
    for half in range(2):
        total = (rgr[0, half] + rgr[1, half]) + (rgr[2, half] + rgr[3, half])
        rg_out[:, half * 1024 : (half + 1) * 1024] = jnp.where(keep, total, 0.0)
    tree_end(0)

    def sent(own, every, others, sem):
        @pl.when(jnp.logical_not(own))
        def _():
            wait_bytes(every, sem)

        @pl.when(own)
        def _():
            wait_bytes(others, sem)

    home = q == p // 2
    sent(home, us, us.at[1:NP], u_send.at[0])
    sent(q % 2 == y // 2, us, us.at[1:NP], ur_send.at[0])
    sent(q // 2 == x, uq, uq.at[1:4], uq_send.at[0])
    sent(home, rgp, rgp.at[1:NP], g_send.at[0])
    wait_bytes(vr.at[z, x], vx_send.at[0])
    wait_bytes(vq.at[z, 1:4], vy_send.at[0])
    wait_bytes(vr.at[1:NZ], vr_send.at[0])
    wait_bytes(vq.at[1:NZ], vq_send.at[0])
    wait_bytes(xsr.at[:, 1:4], xr_send.at[0])
    wait_bytes(xsq, xq_send.at[0])
    for h in range(2):
        wait_bytes(zs.at[4 * h : 4 * h + 4, 1:NP], z_send.at[h])
    for h in range(2):
        wait_bytes(tbuf.at[h], t_send.at[h])


def shards(receiver_spectra, reference_spectra, receiver_counts, reference_counts, column_station, lag_window, observed):
    table = lag_table()
    m = jnp.asarray(table, dtype=BF)
    mt = jnp.asarray(np.ascontiguousarray(table.T), dtype=BF)
    vmem = pl.BlockSpec(memory_space=pltpu.VMEM)
    hbm = pl.BlockSpec(memory_space=pl.ANY)
    dma = pltpu.SemaphoreType.DMA
    return pl.pallas_call(
        kernel,
        out_shape=(
            pltpu.VMEM((NI, 2048), F32),
            pltpu.VMEM((128, NJ), F32),
        ),
        in_specs=[vmem] * 6 + [hbm] * 3,
        out_specs=(pl.BlockSpec(memory_space=pltpu.MemorySpace.VMEM), pl.BlockSpec(memory_space=pltpu.MemorySpace.VMEM)),
        scratch_shapes=[
            pltpu.VMEM((2, NI, 1152), BF),
            pltpu.VMEM((NP, NI, 1152), BF),
            pltpu.VMEM((4, 2, NI, 1152), BF),
            pltpu.VMEM((4, 2, NI, 1152), BF),
            pltpu.VMEM((NZ, 2, 128, 128), BF),
            pltpu.VMEM((NZ, 4, 128, 128), BF),
            pltpu.VMEM((NZ, 4, 2, NI, 256), F32),
            pltpu.VMEM((NZ, 2, 2, 2, NI, 256), F32),
            pltpu.VMEM((4, NI, 16, 256), BF),
            pltpu.VMEM((4, NI, 16, 128), F32),
            pltpu.VMEM((2, NI, 16, 128), F32),
            pltpu.VMEM((NG, 4, 2, 128, 256), BF),
            pltpu.VMEM((NG, 2, 256, 512), BF),
            pltpu.VMEM((8, NJ), F32),
            pltpu.VMEM((8, NJ), F32),
            pltpu.VMEM((8, NJ), F32),
            pltpu.VMEM((NI, NJ, L), BF),
            pltpu.VMEM((2 * F, 2 * L), BF),
            pltpu.VMEM((2 * L, 2 * F), BF),
            pltpu.VMEM((2 * L, 2 * F), BF),
            pltpu.VMEM((2 * L, 2 * F), BF),
            pltpu.VMEM((8, L, NJ), BF),
            pltpu.VMEM((NZ, 4, 4, 16, NJ), BF),
            pltpu.VMEM((4, 4, NZ, 16, NJ), BF),
            pltpu.VMEM((NZ, 4, 2, 16, NJ), BF),
            pltpu.VMEM((4, 2, NZ, 2, 16, NJ), BF),
            pltpu.VMEM((2 * L, NJ), BF),
            pltpu.VMEM((8, NP, NG, 16, NJ), BF),
            pltpu.VMEM((NG, 8, NP, 16, NJ), BF),
            pltpu.VMEM((2, NZ, 128, 128), F32),
            pltpu.VMEM((2, 7, 128, 128), F32),
            pltpu.VMEM((NP, NI, 1024), F32),
            pltpu.VMEM((4, 2, NI, 1024), F32),
            dma((3,)), dma((1,)), dma((1,)), dma((1,)), dma((1,)), dma((1,)), dma((1,)),
            dma((1,)), dma((1,)), dma((1,)), dma((4,)), dma((1,)), dma((NZ, 2)), dma((1,)), dma((NZ, 4)),
            dma((1,)), dma((1,)), dma((1,)), dma((1,)), dma((2,)), dma((8,)),
            dma((1,)), dma((1,)), dma((2,)), dma((2, 7)),
        ],
        compiler_params=pltpu.CompilerParams(
            collective_id=0, has_side_effects=True, vmem_limit_bytes=60 * 1024 * 1024
        ),
    )(
        receiver_spectra,
        reference_spectra,
        receiver_counts.reshape(1, NI),
        reference_counts.reshape(1, NJ),
        column_station.reshape(1, NJ),
        lag_window,
        observed,
        m,
        mt,
    )


def solution(mesh):
    return jax.shard_map(
        shards,
        mesh=mesh,
        in_specs=(
            P("rcv", "ref"), P("rcv", "ref"), P("rcv"), P("ref"), P("ref"),
            P(None, "rcv", "ref"), P("rcv", "ref", None),
        ),
        out_specs=(P("rcv", "ref"), P("rcv", "ref")),
        check_vma=False,
    )
```

```python
import math

import jax
import jax.numpy as jnp
import numpy as np
from jax import lax
from jax.experimental import pallas as pl
from jax.experimental.pallas import tpu as pltpu
from jax.sharding import PartitionSpec as P

L = 512
S = 16
F = 256
NP = 8
NZ = 8
NI = 8
NJ = 256
NG = 4
MESH = pl.DeviceIdType.MESH
BF = jnp.bfloat16
F32 = jnp.float32

env_floor = 0.05
misfit_scale = 0.03125


def lag_table():
    freq_ids = np.arange(F, dtype=np.int64)[:, None]
    lag_ids = np.arange(L, dtype=np.int64)[None, :] - L // 2
    angle = ((freq_ids * lag_ids) % L).astype(np.float64) * (2.0 * math.pi / L)
    cosine = np.cos(angle) / math.sqrt(F)
    sine = np.sin(angle) / math.sqrt(F)
    real_rows = np.concatenate([cosine, sine], axis=1)
    imag_rows = np.concatenate([-sine, cosine], axis=1)
    stacked = np.stack([real_rows, imag_rows], axis=1).reshape(2 * F, 2 * L)
    return stacked.astype(np.float32)


def kernel(
    u_ref, v_ref, rc_ref, fc_ref, cs_ref, win_ref, obs_hbm, m_hbm, mt_hbm,
    rg_out, wg_out,
    um, us, ur, uq, vr, vq, ucr, ucq, bw, scr, scq, bt, bb, ninv, first, last,
    obs, m_ref, mt_ref, mq_ref, mr_ref, obst, xsr, xrr, xsq, xrq, gs, zs, zr,
    w, tbuf, rgp, rgr,
    in_sem, u_send, u_recv, ur_send, ur_recv, uq_send, uq_recv,
    vx_send, vx_recv, vy_send, vy_recv, vr_send, vr_recv, vq_send, vq_recv,
    xr_send, xr_recv, xq_send, xq_recv, z_send, z_recv,
    g_send, g_recv, t_send, t_recv,
):
    r = lax.axis_index("rcv")
    q = lax.axis_index("ref")
    p = r // NZ
    z = r % NZ
    x = p // 4
    y = p % 4
    right = p * NZ + (z + 1) % NZ
    left = p * NZ + (z + NZ - 1) % NZ
    partner = ((p + 4) % NP) * NZ + z

    def signal(rr, qq):
        pl.semaphore_signal(barrier, inc=1, device_id=(rr, qq), device_id_type=MESH)

    def remote(src, dst, send, recv, rr, qq):
        return pltpu.make_async_remote_copy(
            src_ref=src, dst_ref=dst, send_sem=send, recv_sem=recv,
            device_id=(rr, qq), device_id_type=MESH,
        )

    def plane(k):
        return ((p + k) % NP) * NZ + z

    def wait_bytes(ref, sem):
        pltpu.make_async_copy(ref, ref, sem).wait()

    barrier = pltpu.get_barrier_semaphore()
    for k in range(NP):
        for dq in range(4):
            if k or dq:
                signal(plane(k), (q + dq) % 4)
    for k in (1, 2, 6, 7):
        signal(p * NZ + (z + k) % NZ, q)

    loads = [pltpu.make_async_copy(obs_hbm.at[i], obs.at[i], in_sem.at[0]) for i in range(NI)]
    loads.append(pltpu.make_async_copy(mt_hbm, mt_ref, in_sem.at[1]))
    loads.append(pltpu.make_async_copy(m_hbm, m_ref, in_sem.at[2]))
    for load in loads:
        load.start()

    eye = lax.broadcasted_iota(jnp.int32, (NI, NI), 0) == lax.broadcasted_iota(jnp.int32, (NI, NI), 1)
    rcounts = jnp.sum(jnp.where(eye, rc_ref[...].astype(F32), 0.0), axis=1, keepdims=True)
    pc = fc_ref[...].astype(F32)
    row_mask = (lax.broadcasted_iota(jnp.int32, (128, NJ), 0) % S).astype(F32) < pc
    mine = jnp.where(row_mask, v_ref[...].astype(F32), 0.0).astype(BF)
    vq[z, y] = mine[:, 0:128]
    vr[z, x] = mine[:, 128:256]
    seg_lane = (lax.broadcasted_iota(jnp.int32, (NI, 1024), 1) % S).astype(F32)
    keep = seg_lane < rcounts
    for half in range(2):
        part = u_ref[:, half * 1024 : (half + 1) * 1024].astype(F32)
        um[half, :, 0:1024] = jnp.where(keep, part, 0.0).astype(BF)
        um[half, :, 1024:1152] = jnp.broadcast_to(rcounts, (NI, 128)).astype(BF)

    pl.semaphore_wait(barrier, 4 * NP - 1 + 4)

    def give(own, src, dst, send, recv, rr, qq):
        @pl.when(jnp.logical_not(own))
        def _():
            remote(src, dst, send, recv, rr, qq).start()

        @pl.when(own)
        def _():
            pltpu.make_async_copy(src, dst, recv).start()

    def pass_on(buf, send, recv, zz, sub, to):
        remote(buf.at[zz, sub], buf.at[zz, sub], send.at[0], recv.at[zz, sub], to, q).start()

    def pass_r(zz, sub, to):
        pass_on(vr, vr_send, vr_recv, zz, sub, to)

    def pass_q(zz, sub, to):
        pass_on(vq, vq_send, vq_recv, zz, sub, to)

    remote(vr.at[z, x], vr.at[z, x], vx_send.at[0], vx_recv.at[0], partner, q).start()
    for k in range(1, 4):
        remote(
            vq.at[z, y], vq.at[z, y], vy_send.at[0], vy_recv.at[y], (x * 4 + (y + k) % 4) * NZ + z, q
        ).start()
    pass_r(z, x, right)
    pass_r(z, x, left)
    pass_q(z, y, right)
    pass_q(z, y, left)
    for half in range(2):
        for qq in range(4):
            yd = 2 * (q % 2) + half
            own = jnp.logical_and(yd == y, qq == q)
            give(
                own, um.at[half], ur.at[(y - yd + 4) % 4, q // 2], ur_send.at[0], ur_recv.at[0],
                (x * 4 + yd) * NZ + z, qq,
            )
    for qq in range(4):
        xd = q // 2
        own = jnp.logical_and(xd == x, qq == q)
        give(
            own, um, uq.at[2 * ((x - xd + 2) % 2) + q % 2], uq_send.at[0], uq_recv.at[0],
            (xd * 4 + y) * NZ + z, qq,
        )
    order = cs_ref[...] - q * NJ
    stations = lax.broadcasted_iota(jnp.int32, (NJ, NJ), 0)
    onehot = jnp.where(stations == order, 1.0, 0.0).astype(BF)
    nt = (((1,), (1,)), ((), ()))
    begin = lax.dot_general(win_ref[0].astype(F32).astype(BF), onehot, nt, preferred_element_type=F32)
    span = lax.dot_general(win_ref[1].astype(F32).astype(BF), onehot, nt, preferred_element_type=F32)
    inv = 1.0 / jnp.minimum(rcounts, pc)
    for h in range(2):
        for i in range(NI):
            u, lanes, side = 4 * h + i // 2, pl.ds((i % 2) * 128, 128), slice(h * 128, (h + 1) * 128)
            first[u : u + 1, lanes] = begin[i : i + 1, side]
            last[u : u + 1, lanes] = begin[i : i + 1, side] + span[i : i + 1, side]
            ninv[u : u + 1, lanes] = inv[i : i + 1, side]
    def turn(ii, c):
        for par in range(2):
            seen = jnp.dot(onehot, obs[2 * ii + par], preferred_element_type=F32)
            seen = jnp.transpose(seen, (1, 0)).astype(BF)
            for h in range(2):
                obst[4 * h + ii, :, par * 128 : (par + 1) * 128] = seen[:, h * 128 : (h + 1) * 128]
        return c

    wait_bytes(obs, in_sem.at[0])
    lax.fori_loop(0, 2, turn, 0)

    wait_bytes(vr.at[z, 1 - x], vx_recv.at[0])
    pass_r(z, 1 - x, right)
    pass_r(z, 1 - x, left)
    for k in (1, 3, 2):
        yy = (y + k) % 4
        wait_bytes(vq.at[z, yy], vy_recv.at[yy])
        pass_q(z, yy, right)
        pass_q(z, yy, left)
    for half in range(2):
        for qq in range(4):
            pp = 2 * q + half
            rr = pp * NZ + z
            own = jnp.logical_and(rr == r, qq == q)
            slot = (p - pp + NP) % NP
            give(own, um.at[half], us.at[slot], u_send.at[0], u_recv.at[0], rr, qq)

    def back(s):
        return (z + NZ - s) % NZ

    def ahead(s):
        return (z + s) % NZ

    def step(s, buf, recv, pass_to, sub, up):
        if s <= up:
            wait_bytes(buf.at[back(s), sub], recv.at[back(s), sub])
            if s < up:
                pass_to(back(s), sub, right)
        if s <= 7 - up:
            wait_bytes(buf.at[ahead(s), sub], recv.at[ahead(s), sub])
            if s < 7 - up:
                pass_to(ahead(s), sub, left)

    def step_r(s):
        for k in range(2):
            step(s, vr, vr_recv, pass_r, (x + k) % 2, 4 - k)

    def step_q(s):
        for k in (0, 1, 3, 2):
            step(s, vq, vq_recv, pass_q, (y + k) % 4, 4 if k < 2 else 3)

    row16 = lax.broadcasted_iota(jnp.int32, (16, 256), 0)
    lane256 = lax.broadcasted_iota(jnp.int32, (16, 256), 1)
    diag = (lane256 // 32) == (row16 // 2)
    mask0 = jnp.logical_and(diag, row16 % 2 == 0)
    mask1 = jnp.logical_and(diag, row16 % 2 == 1)

    def turned(uf):
        part = (lax.broadcasted_iota(jnp.int32, (NI, 1024), 1) // S) % 2
        return jnp.where(part == 0, pltpu.roll(uf, 1024 - S, 1), -pltpu.roll(uf, S, 1))

    def blocks(a, b, out):
        for i in range(NI):
            out(i, jnp.where(mask0, a[i : i + 1], jnp.where(mask1, b[i : i + 1], 0.0)).astype(BF))

    def ready_r(yk, c):
        for xx in range(2):
            uf = ur[yk, xx, :, 0:1024].astype(F32)
            ut = turned(uf)
            for zz in range(NZ):
                ucr[zz, yk, 0, :, xx * 128 : (xx + 1) * 128] = uf[:, zz * 128 : (zz + 1) * 128]
                ucr[zz, yk, 1, :, xx * 128 : (xx + 1) * 128] = ut[:, zz * 128 : (zz + 1) * 128]
        inverse = 1.0 / jnp.minimum(ur[yk, 0, :, 1024:1025].astype(F32), pc[:, 128:256])
        for i in range(NI):
            scr[yk, i] = jnp.broadcast_to(inverse[i : i + 1], (16, 128))
        return c

    def ready_q(xk, c):
        for b in range(2):
            for half in range(2):
                uf = uq[2 * xk + b, half, :, 0:1024].astype(F32)
                ut = turned(uf)
                for zz in range(NZ):
                    ucq[zz, xk, b, 0, :, half * 128 : (half + 1) * 128] = uf[:, zz * 128 : (zz + 1) * 128]
                    ucq[zz, xk, b, 1, :, half * 128 : (half + 1) * 128] = ut[:, zz * 128 : (zz + 1) * 128]
        inverse = 1.0 / jnp.minimum(uq[2 * xk, 0, :, 1024:1025].astype(F32), pc[:, 0:128])
        for i in range(NI):
            scq[xk, i] = jnp.broadcast_to(inverse[i : i + 1], (16, 128))
        return c

    def cross_r(zz):
        for yk in range(4):
            def put(i, blk):
                bw[yk, i] = blk

            blocks(ucr[zz, yk, 0], ucr[zz, yk, 1], put)
        v = jnp.dot(bw[...].reshape(512, 256), vr[zz].reshape(256, 128), preferred_element_type=F32)
        v = (v * scr[...].reshape(512, 128)).astype(BF)
        for yk in range(4):
            for i in range(NI):
                rows = v[(yk * NI + i) * 16 : (yk * NI + i + 1) * 16]
                lanes = slice((i % 2) * 128, (i % 2 + 1) * 128)
                if yk:
                    xsr[zz, yk, i // 2, :, lanes] = rows
                else:
                    xrr[i // 2, y, zz, :, lanes] = rows
        for yk in range(1, 4):
            remote(
                xsr.at[zz, yk], xrr.at[:, y, zz], xr_send.at[0], xr_recv.at[0],
                (x * 4 + (y + yk) % 4) * NZ + z, q,
            ).start()

    def cross_q(zz):
        for b in range(2):
            for xk in range(2):
                def put(i, blk):
                    bw[2 * b + xk, i] = blk

                blocks(ucq[zz, xk, b, 0], ucq[zz, xk, b, 1], put)
        for b in range(2):
            v = jnp.dot(
                bw[2 * b : 2 * b + 2].reshape(256, 256), vq[zz, 2 * b : 2 * b + 2].reshape(256, 128),
                preferred_element_type=F32,
            )
            v = (v * scq[...].reshape(256, 128)).astype(BF)
            for xk in range(2):
                for i in range(NI):
                    rows = v[(xk * NI + i) * 16 : (xk * NI + i + 1) * 16]
                    lanes = slice((i % 2) * 128, (i % 2 + 1) * 128)
                    if xk:
                        xsq[zz, i // 2, b, :, lanes] = rows
                    else:
                        xrq[i // 2, x, zz, b, :, lanes] = rows
        remote(xsq.at[zz], xrq.at[:, x, zz], xq_send.at[0], xq_recv.at[0], partner, q).start()

    def crossings(cross, start, end):
        def one(j, c):
            cross((z + NZ + ((j + 1) // 2) * (2 * (j % 2) - 1)) % NZ)
            return c

        lax.fori_loop(start, end, one, 0)

    lax.fori_loop(2, 4, turn, 0)
    step_r(1)
    wait_bytes(ur, ur_recv.at[0])
    lax.fori_loop(0, 4, ready_r, 0)
    crossings(cross_r, 0, 3)
    step_r(2)
    crossings(cross_r, 3, 5)
    step_q(1)
    wait_bytes(uq, uq_recv.at[0])
    lax.fori_loop(0, 2, ready_q, 0)
    crossings(cross_q, 0, 3)
    step_r(3)
    crossings(cross_r, 5, 7)
    step_q(2)
    crossings(cross_q, 3, 5)

    here = lax.broadcasted_iota(jnp.int32, (2 * F, 2 * F), 0)
    n = lax.broadcasted_iota(jnp.int32, (2 * F, 2 * F), 1)
    from_r = n % 8 + 8 * ((n // 16) % 8) + 64 * (n // 128) + 256 * ((n // 8) % 2)
    from_q = n % 8 + 8 * ((n // 32) % 8) + 64 * ((n // 8) % 4) + 256 * (n // 256)

    def reorder(source, out):
        pick = jnp.where(here == source, 1.0, 0.0).astype(BF)
        for b in range(4):
            rows = slice(b * 256, (b + 1) * 256)
            out[rows, :] = jnp.dot(mt_ref[rows, :], pick, preferred_element_type=F32).astype(BF)

    for load in loads[NI:]:
        load.wait()
    reorder(from_r, mr_ref)
    step_r(4)
    crossings(cross_r, 7, 8)
    step_q(3)
    crossings(cross_q, 5, 7)
    reorder(from_q, mq_ref)
    step_q(4)
    crossings(cross_q, 7, 8)

    TB = 128
    def pairs(u, got, table):
        lo = first[pl.ds(u, 1), :]
        hi = last[pl.ds(u, 1), :]
        for b in range(L // TB):
            cor = jnp.dot(table[b * TB : (b + 1) * TB, :], got, preferred_element_type=F32)
            hil = jnp.dot(table[L + b * TB : L + (b + 1) * TB, :], got, preferred_element_type=F32)
            rs = lax.rsqrt(cor * cor + hil * hil + env_floor)
            lag = (lax.broadcasted_iota(jnp.int32, (TB, NJ), 0) + b * TB).astype(F32)
            inside = jnp.logical_and(lag >= lo, lag < hi)
            seen = obst[u, b * TB : (b + 1) * TB, :].astype(F32)
            wt = jnp.where(inside, (1.0 - seen * rs) * misfit_scale, 0.0)
            gs[b * TB : (b + 1) * TB, :] = (wt * cor).astype(BF)
            gs[L + b * TB : L + (b + 1) * TB, :] = (wt * hil).astype(BF)
        scale = ninv[pl.ds(u, 1), :]
        for b in range(4):
            back = jnp.dot(m_ref[b * 128 : (b + 1) * 128, :], gs[...], preferred_element_type=F32)
            zs[u, 2 * b : 2 * b + 2] = (back * scale).astype(BF).reshape(2, NG, 16, NJ)
        for k in (4, 5, 7, 6, 1, 3, 2):
            remote(
                zs.at[u, (p + k) % NP], zr.at[:, u, NP - k], z_send.at[u // 4], z_recv.at[u], plane(k), q
            ).start()
        zr[:, u, 0] = zs[u, p]

    def pairs_r(ii, c):
        pairs(4 + ii, xrr[ii].reshape(2 * F, NJ), mr_ref)
        return c

    def pairs_q(ii, c):
        pairs(ii, xrq[ii].reshape(2 * F, NJ), mq_ref)
        return c

    wait_bytes(xsr.at[:, 1:4], xr_recv.at[0])
    lax.fori_loop(0, 4, pairs_r, 0)
    wait_bytes(xsq, xq_recv.at[0])
    lax.fori_loop(0, 4, pairs_q, 0)

    def operand(k, c):
        uf = us[k, :, 0:1024].astype(F32)
        ut = turned(uf)
        for g in range(NG):
            def put(i, blk):
                bt[g, i // 2, i % 2, pl.ds(k * 16, 16), :] = blk

            blocks(uf[:, g * 256 : (g + 1) * 256], ut[:, g * 256 : (g + 1) * 256], put)
        return c

    wait_bytes(us, u_recv.at[0])
    lax.fori_loop(0, NP, operand, 0)

    def flip(g, c):
        for ii in range(4):
            for par in range(2):
                bb[g, par, :, ii * 128 : (ii + 1) * 128] = jnp.transpose(
                    bt[g, ii, par].astype(F32), (1, 0)
                ).astype(BF)
        return c

    lax.fori_loop(0, NG, flip, 0)

    def arrived(u):
        wait_bytes(zs.at[u, 1:NP], z_recv.at[u])

    def sums(h, start, end):
        size = (end - start) * 128
        for g in range(NG):
            part = None
            for par in range(2):
                got = zr[g, 4 * h + start : 4 * h + end, :, :, par * 128 : (par + 1) * 128].reshape(size, 128)
                one = jnp.dot(bb[g, par, :, start * 128 : end * 128], got, preferred_element_type=F32)
                part = one if part is None else part + one
            part = part.reshape(2, 128, 128)
            if start:
                part = part + w[h, 2 * g : 2 * g + 2]
            w[h, 2 * g : 2 * g + 2] = part

    def toward(n, src, h, part, to):
        rows = slice(part * 64, (part + 1) * 64)
        remote(
            src.at[rows], tbuf.at[h, n, rows], t_send.at[h], t_recv.at[h, n, part],
            p * NZ + (z + NZ + to) % NZ, q,
        ).start()

    def landed(n, h, part):
        wait_bytes(tbuf.at[h, n, part * 64 : (part + 1) * 64], t_recv.at[h, n, part])

    def tree_start(h):
        for part in range(2):
            for n, m, to in ((0, 4, 2), (2, 5, -1), (1, 3, 1)):
                toward(n, w.at[h, (z + m) % NZ], h, part, to)
        for part in range(2):
            for n, m, to in ((3, 1, 1), (4, 7, -1)):
                toward(n, w.at[h, (z + m) % NZ], h, part, to)

    def tree_middle(h):
        for part in range(2):
            rows = slice(part * 64, (part + 1) * 64)
            landed(2, h, part)
            tbuf[h, 2, rows] = tbuf[h, 2, rows] + w[h, (z + 6) % NZ, rows]
            toward(6, tbuf.at[h, 2], h, part, -2)
            landed(1, h, part)
            landed(0, h, part)
            tbuf[h, 0, rows] = tbuf[h, 0, rows] + (tbuf[h, 1, rows] + w[h, (z + 2) % NZ, rows])
            toward(5, tbuf.at[h, 0], h, part, 2)

    def tree_end(h):
        for n in (3, 4, 6, 5):
            for part in range(2):
                landed(n, h, part)
        done = (w[h, z] + tbuf[h, 3]) + (tbuf[h, 4] + tbuf[h, 6]) + tbuf[h, 5]
        cols = slice(h * 128, (h + 1) * 128)
        wg_out[:, cols] = jnp.where(row_mask[:, cols], done, 0.0)

    lane8 = (lax.broadcasted_iota(jnp.int32, (NP, 256), 1) // S) % 2

    def receivers(ii):
        for g in range(NG):
            for par in range(2):
                t = None
                for h in range(2):
                    got = zr[g, 4 * h + ii, :, :, par * 128 : (par + 1) * 128].reshape(128, 128)
                    held = vr[2 * g : 2 * g + 2, x] if h else vq[2 * g : 2 * g + 2, y]
                    block = held.reshape(256, 128)
                    part = lax.dot_general(got, block, nt, preferred_element_type=F32)
                    t = part if t is None else t + part
                t = t.reshape(NP, 16, 256)
                a0 = jnp.sum(jnp.where(mask0[None], t, 0.0), axis=1)
                a1 = jnp.sum(jnp.where(mask1[None], t, 0.0), axis=1)
                rg = a0 + jnp.where(lane8 == 0, -pltpu.roll(a1, 256 - S, 1), pltpu.roll(a1, S, 1))
                i = 2 * ii + par
                for k in range(NP):
                    rgp[k, i : i + 1, g * 256 : (g + 1) * 256] = rg[k : k + 1]

    for u in range(4, 8):
        arrived(u)
    sums(1, 0, 4)
    tree_start(1)
    arrived(0)
    receivers(0)
    tree_middle(1)
    arrived(1)
    receivers(1)
    arrived(2)
    receivers(2)
    sums(0, 0, 3)
    tree_end(1)
    arrived(3)
    sums(0, 3, 4)
    tree_start(0)
    receivers(3)
    for k in range(NP):
        own = jnp.logical_and(k == 0, p // 2 == q)

        @pl.when(jnp.logical_not(own))
        def _():
            remote(rgp.at[k], rgr.at[q, p % 2], g_send.at[0], g_recv.at[0], plane(k), p // 2).start()

        @pl.when(own)
        def _():
            pltpu.make_async_copy(rgp.at[k], rgr.at[q, p % 2], g_recv.at[0]).start()

    tree_middle(0)
    wait_bytes(rgr, g_recv.at[0])
    for half in range(2):
        total = (rgr[0, half] + rgr[1, half]) + (rgr[2, half] + rgr[3, half])
        rg_out[:, half * 1024 : (half + 1) * 1024] = jnp.where(keep, total, 0.0)
    tree_end(0)

    def sent(own, every, others, sem):
        @pl.when(jnp.logical_not(own))
        def _():
            wait_bytes(every, sem)

        @pl.when(own)
        def _():
            wait_bytes(others, sem)

    home = q == p // 2
    sent(home, us, us.at[1:NP], u_send.at[0])
    sent(q % 2 == y // 2, us, us.at[1:NP], ur_send.at[0])
    sent(q // 2 == x, uq, uq.at[1:4], uq_send.at[0])
    sent(home, rgp, rgp.at[1:NP], g_send.at[0])
    wait_bytes(vr.at[z, x], vx_send.at[0])
    wait_bytes(vq.at[z, 1:4], vy_send.at[0])
    wait_bytes(vr.at[1:NZ], vr_send.at[0])
    wait_bytes(vq.at[1:NZ], vq_send.at[0])
    wait_bytes(xsr.at[:, 1:4], xr_send.at[0])
    wait_bytes(xsq, xq_send.at[0])
    for h in range(2):
        wait_bytes(zs.at[4 * h : 4 * h + 4, 1:NP], z_send.at[h])
    for h in range(2):
        wait_bytes(tbuf.at[h], t_send.at[h])


def shards(receiver_spectra, reference_spectra, receiver_counts, reference_counts, column_station, lag_window, observed):
    table = lag_table()
    m = jnp.asarray(table, dtype=BF)
    mt = jnp.asarray(np.ascontiguousarray(table.T), dtype=BF)
    vmem = pl.BlockSpec(memory_space=pltpu.VMEM)
    hbm = pl.BlockSpec(memory_space=pl.ANY)
    dma = pltpu.SemaphoreType.DMA
    return pl.pallas_call(
        kernel,
        out_shape=(
            pltpu.VMEM((NI, 2048), F32),
            pltpu.VMEM((128, NJ), F32),
        ),
        in_specs=[vmem] * 6 + [hbm] * 3,
        out_specs=(pl.BlockSpec(memory_space=pltpu.MemorySpace.VMEM), pl.BlockSpec(memory_space=pltpu.MemorySpace.VMEM)),
        scratch_shapes=[
            pltpu.VMEM((2, NI, 1152), BF),
            pltpu.VMEM((NP, NI, 1152), BF),
            pltpu.VMEM((4, 2, NI, 1152), BF),
            pltpu.VMEM((4, 2, NI, 1152), BF),
            pltpu.VMEM((NZ, 2, 128, 128), BF),
            pltpu.VMEM((NZ, 4, 128, 128), BF),
            pltpu.VMEM((NZ, 4, 2, NI, 256), F32),
            pltpu.VMEM((NZ, 2, 2, 2, NI, 256), F32),
            pltpu.VMEM((4, NI, 16, 256), BF),
            pltpu.VMEM((4, NI, 16, 128), F32),
            pltpu.VMEM((2, NI, 16, 128), F32),
            pltpu.VMEM((NG, 4, 2, 128, 256), BF),
            pltpu.VMEM((NG, 2, 256, 512), BF),
            pltpu.VMEM((8, NJ), F32),
            pltpu.VMEM((8, NJ), F32),
            pltpu.VMEM((8, NJ), F32),
            pltpu.VMEM((NI, NJ, L), BF),
            pltpu.VMEM((2 * F, 2 * L), BF),
            pltpu.VMEM((2 * L, 2 * F), BF),
            pltpu.VMEM((2 * L, 2 * F), BF),
            pltpu.VMEM((2 * L, 2 * F), BF),
            pltpu.VMEM((8, L, NJ), BF),
            pltpu.VMEM((NZ, 4, 4, 16, NJ), BF),
            pltpu.VMEM((4, 4, NZ, 16, NJ), BF),
            pltpu.VMEM((NZ, 4, 2, 16, NJ), BF),
            pltpu.VMEM((4, 2, NZ, 2, 16, NJ), BF),
            pltpu.VMEM((2 * L, NJ), BF),
            pltpu.VMEM((8, NP, NG, 16, NJ), BF),
            pltpu.VMEM((NG, 8, NP, 16, NJ), BF),
            pltpu.VMEM((2, NZ, 128, 128), F32),
            pltpu.VMEM((2, 7, 128, 128), F32),
            pltpu.VMEM((NP, NI, 1024), F32),
            pltpu.VMEM((4, 2, NI, 1024), F32),
            dma((3,)), dma((1,)), dma((1,)), dma((1,)), dma((1,)), dma((1,)), dma((1,)),
            dma((1,)), dma((1,)), dma((1,)), dma((4,)), dma((1,)), dma((NZ, 2)), dma((1,)), dma((NZ, 4)),
            dma((1,)), dma((1,)), dma((1,)), dma((1,)), dma((2,)), dma((8,)),
            dma((1,)), dma((1,)), dma((2,)), dma((2, 7, 2)),
        ],
        compiler_params=pltpu.CompilerParams(
            collective_id=0, has_side_effects=True, vmem_limit_bytes=60 * 1024 * 1024
        ),
    )(
        receiver_spectra,
        reference_spectra,
        receiver_counts.reshape(1, NI),
        reference_counts.reshape(1, NJ),
        column_station.reshape(1, NJ),
        lag_window,
        observed,
        m,
        mt,
    )


def solution(mesh):
    return jax.shard_map(
        shards,
        mesh=mesh,
        in_specs=(
            P("rcv", "ref"), P("rcv", "ref"), P("rcv"), P("ref"), P("ref"),
            P(None, "rcv", "ref"), P("rcv", "ref", None),
        ),
        out_specs=(P("rcv", "ref"), P("rcv", "ref")),
        check_vma=False,
    )
```

```python
import math

import jax
import jax.numpy as jnp
import numpy as np
from jax import lax
from jax.experimental import pallas as pl
from jax.experimental.pallas import tpu as pltpu
from jax.sharding import PartitionSpec as P

L = 512
S = 16
F = 256
NP = 8
NZ = 8
NI = 8
NJ = 256
NG = 4
MESH = pl.DeviceIdType.MESH
BF = jnp.bfloat16
F32 = jnp.float32

env_floor = 0.05
misfit_scale = 0.03125


def lag_table():
    freq_ids = np.arange(F, dtype=np.int64)[:, None]
    lag_ids = np.arange(L, dtype=np.int64)[None, :] - L // 2
    angle = ((freq_ids * lag_ids) % L).astype(np.float64) * (2.0 * math.pi / L)
    cosine = np.cos(angle) / math.sqrt(F)
    sine = np.sin(angle) / math.sqrt(F)
    real_rows = np.concatenate([cosine, sine], axis=1)
    imag_rows = np.concatenate([-sine, cosine], axis=1)
    stacked = np.stack([real_rows, imag_rows], axis=1).reshape(2 * F, 2 * L)
    return stacked.astype(np.float32)


def kernel(
    u_hbm, v_hbm, rc_hbm, fc_hbm, cs_hbm, win_hbm, obs_hbm, m_hbm, mt_hbm,
    rg_out, wg_out,
    u_ref, v_ref, rc_ref, fc_ref, cs_ref, win_ref,
    um, us, ur, uq, vr, vq, ucr, ucq, bw, scr, scq, bt, bb, ninv, first, last,
    obs, m_ref, mt_ref, mq_ref, mr_ref, obst, xsr, xrr, xsq, xrq, gs, zs, zr,
    w, tbuf, rgp, rgr,
    in_sem, u_send, u_recv, ur_send, ur_recv, uq_send, uq_recv,
    vx_send, vx_recv, vy_send, vy_recv, vr_send, vr_recv, vq_send, vq_recv,
    xr_send, xr_recv, xq_send, xq_recv, z_send, z_recv,
    g_send, g_recv, t_send, t_recv,
):
    r = lax.axis_index("rcv")
    q = lax.axis_index("ref")
    p = r // NZ
    z = r % NZ
    x = p // 4
    y = p % 4
    right = p * NZ + (z + 1) % NZ
    left = p * NZ + (z + NZ - 1) % NZ
    partner = ((p + 4) % NP) * NZ + z

    def signal(rr, qq):
        pl.semaphore_signal(barrier, inc=1, device_id=(rr, qq), device_id_type=MESH)

    def remote(src, dst, send, recv, rr, qq):
        return pltpu.make_async_remote_copy(
            src_ref=src, dst_ref=dst, send_sem=send, recv_sem=recv,
            device_id=(rr, qq), device_id_type=MESH,
        )

    def plane(k):
        return ((p + k) % NP) * NZ + z

    def wait_bytes(ref, sem):
        pltpu.make_async_copy(ref, ref, sem).wait()

    small = ((u_hbm, u_ref), (v_hbm, v_ref), (rc_hbm, rc_ref), (fc_hbm, fc_ref), (cs_hbm, cs_ref), (win_hbm, win_ref))
    firsts = [pltpu.make_async_copy(src, dst, in_sem.at[3 + n]) for n, (src, dst) in enumerate(small)]
    for load in firsts:
        load.start()

    barrier = pltpu.get_barrier_semaphore()
    for k in range(NP):
        for dq in range(4):
            if k or dq:
                signal(plane(k), (q + dq) % 4)
    for k in (1, 2, 6, 7):
        signal(p * NZ + (z + k) % NZ, q)

    loads = [pltpu.make_async_copy(obs_hbm.at[i], obs.at[i], in_sem.at[0]) for i in range(NI)]
    loads.append(pltpu.make_async_copy(mt_hbm, mt_ref, in_sem.at[1]))
    loads.append(pltpu.make_async_copy(m_hbm, m_ref, in_sem.at[2]))
    for load in loads:
        load.start()

    for load in firsts:
        load.wait()

    eye = lax.broadcasted_iota(jnp.int32, (NI, NI), 0) == lax.broadcasted_iota(jnp.int32, (NI, NI), 1)
    rcounts = jnp.sum(jnp.where(eye, rc_ref[...].astype(F32), 0.0), axis=1, keepdims=True)
    pc = fc_ref[...].astype(F32)
    row_mask = (lax.broadcasted_iota(jnp.int32, (128, NJ), 0) % S).astype(F32) < pc
    mine = jnp.where(row_mask, v_ref[...].astype(F32), 0.0).astype(BF)
    vq[z, y] = mine[:, 0:128]
    vr[z, x] = mine[:, 128:256]
    seg_lane = (lax.broadcasted_iota(jnp.int32, (NI, 1024), 1) % S).astype(F32)
    keep = seg_lane < rcounts
    for half in range(2):
        part = u_ref[:, half * 1024 : (half + 1) * 1024].astype(F32)
        um[half, :, 0:1024] = jnp.where(keep, part, 0.0).astype(BF)
        um[half, :, 1024:1152] = jnp.broadcast_to(rcounts, (NI, 128)).astype(BF)

    pl.semaphore_wait(barrier, 4 * NP - 1 + 4)

    def give(own, src, dst, send, recv, rr, qq):
        @pl.when(jnp.logical_not(own))
        def _():
            remote(src, dst, send, recv, rr, qq).start()

        @pl.when(own)
        def _():
            pltpu.make_async_copy(src, dst, recv).start()

    def pass_on(buf, send, recv, zz, sub, to):
        remote(buf.at[zz, sub], buf.at[zz, sub], send.at[0], recv.at[zz, sub], to, q).start()

    def pass_r(zz, sub, to):
        pass_on(vr, vr_send, vr_recv, zz, sub, to)

    def pass_q(zz, sub, to):
        pass_on(vq, vq_send, vq_recv, zz, sub, to)

    remote(vr.at[z, x], vr.at[z, x], vx_send.at[0], vx_recv.at[0], partner, q).start()
    for k in range(1, 4):
        remote(
            vq.at[z, y], vq.at[z, y], vy_send.at[0], vy_recv.at[y], (x * 4 + (y + k) % 4) * NZ + z, q
        ).start()
    pass_r(z, x, right)
    pass_r(z, x, left)
    pass_q(z, y, right)
    pass_q(z, y, left)
    for half in range(2):
        for qq in range(4):
            yd = 2 * (q % 2) + half
            own = jnp.logical_and(yd == y, qq == q)
            give(
                own, um.at[half], ur.at[(y - yd + 4) % 4, q // 2], ur_send.at[0], ur_recv.at[0],
                (x * 4 + yd) * NZ + z, qq,
            )
    for qq in range(4):
        xd = q // 2
        own = jnp.logical_and(xd == x, qq == q)
        give(
            own, um, uq.at[2 * ((x - xd + 2) % 2) + q % 2], uq_send.at[0], uq_recv.at[0],
            (xd * 4 + y) * NZ + z, qq,
        )
    order = cs_ref[...] - q * NJ
    stations = lax.broadcasted_iota(jnp.int32, (NJ, NJ), 0)
    onehot = jnp.where(stations == order, 1.0, 0.0).astype(BF)
    nt = (((1,), (1,)), ((), ()))
    begin = lax.dot_general(win_ref[0].astype(F32).astype(BF), onehot, nt, preferred_element_type=F32)
    span = lax.dot_general(win_ref[1].astype(F32).astype(BF), onehot, nt, preferred_element_type=F32)
    inv = 1.0 / jnp.minimum(rcounts, pc)
    for h in range(2):
        for i in range(NI):
            u, lanes, side = 4 * h + i // 2, pl.ds((i % 2) * 128, 128), slice(h * 128, (h + 1) * 128)
            first[u : u + 1, lanes] = begin[i : i + 1, side]
            last[u : u + 1, lanes] = begin[i : i + 1, side] + span[i : i + 1, side]
            ninv[u : u + 1, lanes] = inv[i : i + 1, side]
    def turn(ii, c):
        for par in range(2):
            seen = jnp.dot(onehot, obs[2 * ii + par], preferred_element_type=F32)
            seen = jnp.transpose(seen, (1, 0)).astype(BF)
            for h in range(2):
                obst[4 * h + ii, :, par * 128 : (par + 1) * 128] = seen[:, h * 128 : (h + 1) * 128]
        return c

    wait_bytes(obs, in_sem.at[0])
    lax.fori_loop(0, 2, turn, 0)

    wait_bytes(vr.at[z, 1 - x], vx_recv.at[0])
    pass_r(z, 1 - x, right)
    pass_r(z, 1 - x, left)
    for k in (1, 3, 2):
        yy = (y + k) % 4
        wait_bytes(vq.at[z, yy], vy_recv.at[yy])
        pass_q(z, yy, right)
        pass_q(z, yy, left)
    for half in range(2):
        for qq in range(4):
            pp = 2 * q + half
            rr = pp * NZ + z
            own = jnp.logical_and(rr == r, qq == q)
            slot = (p - pp + NP) % NP
            give(own, um.at[half], us.at[slot], u_send.at[0], u_recv.at[0], rr, qq)

    def back(s):
        return (z + NZ - s) % NZ

    def ahead(s):
        return (z + s) % NZ

    def step(s, buf, recv, pass_to, sub, up, down, beside=False):
        for zz, most, to in ((back(s), up, right), (ahead(s), down, left)):
            if s == 4 and most < 4 and (to is left or down == 4):
                continue
            wait_bytes(buf.at[zz, sub], recv.at[zz, sub])
            if s < most:
                pass_to(zz, sub, to)
            if beside and s > 2:
                for k in (1, 3):
                    pass_to(zz, sub, (x * 4 + (y + k) % 4) * NZ + z)

    def step_r(s):
        for k in range(2):
            step(s, vr, vr_recv, pass_r, (x + k) % 2, 4 - k, 3 + k)

    def step_q(s):
        for k, up, down in ((0, 4, 3), (2, 3, 4), (1, 2, 2), (3, 2, 2)):
            step(s, vq, vq_recv, pass_q, (y + k) % 4, up, down, k == 0)

    row16 = lax.broadcasted_iota(jnp.int32, (16, 256), 0)
    lane256 = lax.broadcasted_iota(jnp.int32, (16, 256), 1)
    diag = (lane256 // 32) == (row16 // 2)
    mask0 = jnp.logical_and(diag, row16 % 2 == 0)
    mask1 = jnp.logical_and(diag, row16 % 2 == 1)

    def turned(uf):
        part = (lax.broadcasted_iota(jnp.int32, (NI, 1024), 1) // S) % 2
        return jnp.where(part == 0, pltpu.roll(uf, 1024 - S, 1), -pltpu.roll(uf, S, 1))

    def blocks(a, b, out):
        for i in range(NI):
            out(i, jnp.where(mask0, a[i : i + 1], jnp.where(mask1, b[i : i + 1], 0.0)).astype(BF))

    def ready_r(yk, c):
        for xx in range(2):
            uf = ur[yk, xx, :, 0:1024].astype(F32)
            ut = turned(uf)
            for zz in range(NZ):
                ucr[zz, yk, 0, :, xx * 128 : (xx + 1) * 128] = uf[:, zz * 128 : (zz + 1) * 128]
                ucr[zz, yk, 1, :, xx * 128 : (xx + 1) * 128] = ut[:, zz * 128 : (zz + 1) * 128]
        inverse = 1.0 / jnp.minimum(ur[yk, 0, :, 1024:1025].astype(F32), pc[:, 128:256])
        for i in range(NI):
            scr[yk, i] = jnp.broadcast_to(inverse[i : i + 1], (16, 128))
        return c

    def ready_q(xk, c):
        for b in range(2):
            for half in range(2):
                uf = uq[2 * xk + b, half, :, 0:1024].astype(F32)
                ut = turned(uf)
                for zz in range(NZ):
                    ucq[zz, xk, b, 0, :, half * 128 : (half + 1) * 128] = uf[:, zz * 128 : (zz + 1) * 128]
                    ucq[zz, xk, b, 1, :, half * 128 : (half + 1) * 128] = ut[:, zz * 128 : (zz + 1) * 128]
        inverse = 1.0 / jnp.minimum(uq[2 * xk, 0, :, 1024:1025].astype(F32), pc[:, 0:128])
        for i in range(NI):
            scq[xk, i] = jnp.broadcast_to(inverse[i : i + 1], (16, 128))
        return c

    def cross_r(zz):
        for yk in range(4):
            def put(i, blk):
                bw[yk, i] = blk

            blocks(ucr[zz, yk, 0], ucr[zz, yk, 1], put)
        v = jnp.dot(bw[...].reshape(512, 256), vr[zz].reshape(256, 128), preferred_element_type=F32)
        v = (v * scr[...].reshape(512, 128)).astype(BF)
        for yk in range(4):
            for i in range(NI):
                rows = v[(yk * NI + i) * 16 : (yk * NI + i + 1) * 16]
                lanes = slice((i % 2) * 128, (i % 2 + 1) * 128)
                if yk:
                    xsr[zz, yk, i // 2, :, lanes] = rows
                else:
                    xrr[i // 2, y, zz, :, lanes] = rows
        for yk in range(1, 4):
            remote(
                xsr.at[zz, yk], xrr.at[:, y, zz], xr_send.at[0], xr_recv.at[0],
                (x * 4 + (y + yk) % 4) * NZ + z, q,
            ).start()

    def cross_q(zz):
        for b in range(2):
            for xk in range(2):
                def put(i, blk):
                    bw[2 * b + xk, i] = blk

                blocks(ucq[zz, xk, b, 0], ucq[zz, xk, b, 1], put)
        for b in range(2):
            v = jnp.dot(
                bw[2 * b : 2 * b + 2].reshape(256, 256), vq[zz, 2 * b : 2 * b + 2].reshape(256, 128),
                preferred_element_type=F32,
            )
            v = (v * scq[...].reshape(256, 128)).astype(BF)
            for xk in range(2):
                for i in range(NI):
                    rows = v[(xk * NI + i) * 16 : (xk * NI + i + 1) * 16]
                    lanes = slice((i % 2) * 128, (i % 2 + 1) * 128)
                    if xk:
                        xsq[zz, i // 2, b, :, lanes] = rows
                    else:
                        xrq[i // 2, x, zz, b, :, lanes] = rows
        remote(xsq.at[zz], xrq.at[:, x, zz], xq_send.at[0], xq_recv.at[0], partner, q).start()

    def crossings(cross, start, end):
        def one(j, c):
            cross((z + NZ + ((j + 1) // 2) * (2 * (j % 2) - 1)) % NZ)
            return c

        lax.fori_loop(start, end, one, 0)

    lax.fori_loop(2, 4, turn, 0)
    step_r(1)
    wait_bytes(ur, ur_recv.at[0])
    lax.fori_loop(0, 4, ready_r, 0)
    crossings(cross_r, 0, 3)
    step_r(2)
    crossings(cross_r, 3, 5)
    step_q(1)
    wait_bytes(uq, uq_recv.at[0])
    lax.fori_loop(0, 2, ready_q, 0)
    crossings(cross_q, 0, 3)
    step_r(3)
    crossings(cross_r, 5, 7)
    step_q(2)
    crossings(cross_q, 3, 5)

    here = lax.broadcasted_iota(jnp.int32, (2 * F, 2 * F), 0)
    n = lax.broadcasted_iota(jnp.int32, (2 * F, 2 * F), 1)
    from_r = n % 8 + 8 * ((n // 16) % 8) + 64 * (n // 128) + 256 * ((n // 8) % 2)
    from_q = n % 8 + 8 * ((n // 32) % 8) + 64 * ((n // 8) % 4) + 256 * (n // 256)

    def reorder(source, out):
        pick = jnp.where(here == source, 1.0, 0.0).astype(BF)
        for b in range(4):
            rows = slice(b * 256, (b + 1) * 256)
            out[rows, :] = jnp.dot(mt_ref[rows, :], pick, preferred_element_type=F32).astype(BF)

    for load in loads[NI:]:
        load.wait()
    reorder(from_r, mr_ref)
    step_r(4)
    crossings(cross_r, 7, 8)
    step_q(3)
    crossings(cross_q, 5, 7)
    reorder(from_q, mq_ref)
    step_q(4)
    crossings(cross_q, 7, 8)

    TB = 128
    def pairs(u, got, table):
        lo = first[pl.ds(u, 1), :]
        hi = last[pl.ds(u, 1), :]
        for b in range(L // TB):
            cor = jnp.dot(table[b * TB : (b + 1) * TB, :], got, preferred_element_type=F32)
            hil = jnp.dot(table[L + b * TB : L + (b + 1) * TB, :], got, preferred_element_type=F32)
            rs = lax.rsqrt(cor * cor + hil * hil + env_floor)
            lag = (lax.broadcasted_iota(jnp.int32, (TB, NJ), 0) + b * TB).astype(F32)
            inside = jnp.logical_and(lag >= lo, lag < hi)
            seen = obst[u, b * TB : (b + 1) * TB, :].astype(F32)
            wt = jnp.where(inside, (1.0 - seen * rs) * misfit_scale, 0.0)
            gs[b * TB : (b + 1) * TB, :] = (wt * cor).astype(BF)
            gs[L + b * TB : L + (b + 1) * TB, :] = (wt * hil).astype(BF)
        scale = ninv[pl.ds(u, 1), :]
        for b in range(4):
            back = jnp.dot(m_ref[b * 128 : (b + 1) * 128, :], gs[...], preferred_element_type=F32)
            zs[u, 2 * b : 2 * b + 2] = (back * scale).astype(BF).reshape(2, NG, 16, NJ)
        for k in (4, 5, 7, 6, 1, 3, 2):
            remote(
                zs.at[u, (p + k) % NP], zr.at[:, u, NP - k], z_send.at[u // 4], z_recv.at[u], plane(k), q
            ).start()
        zr[:, u, 0] = zs[u, p]

    def pairs_r(ii, c):
        pairs(4 + ii, xrr[ii].reshape(2 * F, NJ), mr_ref)
        return c

    def pairs_q(ii, c):
        pairs(ii, xrq[ii].reshape(2 * F, NJ), mq_ref)
        return c

    wait_bytes(xsr.at[:, 1:4], xr_recv.at[0])
    lax.fori_loop(0, 4, pairs_r, 0)
    wait_bytes(xsq, xq_recv.at[0])
    lax.fori_loop(0, 4, pairs_q, 0)

    def operand(k, c):
        uf = us[k, :, 0:1024].astype(F32)
        ut = turned(uf)
        for g in range(NG):
            def put(i, blk):
                bt[g, i // 2, i % 2, pl.ds(k * 16, 16), :] = blk

            blocks(uf[:, g * 256 : (g + 1) * 256], ut[:, g * 256 : (g + 1) * 256], put)
        return c

    wait_bytes(us, u_recv.at[0])
    lax.fori_loop(0, NP, operand, 0)

    def flip(g, c):
        for ii in range(4):
            for par in range(2):
                bb[g, par, :, ii * 128 : (ii + 1) * 128] = jnp.transpose(
                    bt[g, ii, par].astype(F32), (1, 0)
                ).astype(BF)
        return c

    lax.fori_loop(0, NG, flip, 0)

    def arrived(u):
        wait_bytes(zs.at[u, 1:NP], z_recv.at[u])

    def sums(h, start, end):
        size = (end - start) * 128
        for g in range(NG):
            part = None
            for par in range(2):
                got = zr[g, 4 * h + start : 4 * h + end, :, :, par * 128 : (par + 1) * 128].reshape(size, 128)
                one = jnp.dot(bb[g, par, :, start * 128 : end * 128], got, preferred_element_type=F32)
                part = one if part is None else part + one
            part = part.reshape(2, 128, 128)
            if start:
                part = part + w[h, 2 * g : 2 * g + 2]
            w[h, 2 * g : 2 * g + 2] = part

    def toward(n, src, h, part, to):
        rows = slice(part * 64, (part + 1) * 64)
        remote(
            src.at[rows], tbuf.at[h, n, rows], t_send.at[h], t_recv.at[h, n, part],
            p * NZ + (z + NZ + to) % NZ, q,
        ).start()

    def landed(n, h, part):
        wait_bytes(tbuf.at[h, n, part * 64 : (part + 1) * 64], t_recv.at[h, n, part])

    def tree_start(h):
        for part in range(2):
            for n, m, to in ((0, 4, 2), (2, 5, -1), (1, 3, 1)):
                toward(n, w.at[h, (z + m) % NZ], h, part, to)
        for part in range(2):
            for n, m, to in ((3, 1, 1), (4, 7, -1)):
                toward(n, w.at[h, (z + m) % NZ], h, part, to)

    def tree_middle(h):
        for part in range(2):
            rows = slice(part * 64, (part + 1) * 64)
            landed(2, h, part)
            tbuf[h, 2, rows] = tbuf[h, 2, rows] + w[h, (z + 6) % NZ, rows]
            toward(6, tbuf.at[h, 2], h, part, -2)
            landed(1, h, part)
            landed(0, h, part)
            tbuf[h, 0, rows] = tbuf[h, 0, rows] + (tbuf[h, 1, rows] + w[h, (z + 2) % NZ, rows])
            toward(5, tbuf.at[h, 0], h, part, 2)

    def tree_end(h):
        for n in (3, 4, 6, 5):
            for part in range(2):
                landed(n, h, part)
        done = (w[h, z] + tbuf[h, 3]) + (tbuf[h, 4] + tbuf[h, 6]) + tbuf[h, 5]
        cols = slice(h * 128, (h + 1) * 128)
        wg_out[:, cols] = jnp.where(row_mask[:, cols], done, 0.0)

    lane8 = (lax.broadcasted_iota(jnp.int32, (NP, 256), 1) // S) % 2

    def receivers(ii):
        for g in range(NG):
            for par in range(2):
                t = None
                for h in range(2):
                    got = zr[g, 4 * h + ii, :, :, par * 128 : (par + 1) * 128].reshape(128, 128)
                    held = vr[2 * g : 2 * g + 2, x] if h else vq[2 * g : 2 * g + 2, y]
                    block = held.reshape(256, 128)
                    part = lax.dot_general(got, block, nt, preferred_element_type=F32)
                    t = part if t is None else t + part
                t = t.reshape(NP, 16, 256)
                a0 = jnp.sum(jnp.where(mask0[None], t, 0.0), axis=1)
                a1 = jnp.sum(jnp.where(mask1[None], t, 0.0), axis=1)
                rg = a0 + jnp.where(lane8 == 0, -pltpu.roll(a1, 256 - S, 1), pltpu.roll(a1, S, 1))
                i = 2 * ii + par
                for k in range(NP):
                    rgp[k, i : i + 1, g * 256 : (g + 1) * 256] = rg[k : k + 1]

    for u in range(4, 8):
        arrived(u)
    sums(1, 0, 4)
    tree_start(1)
    arrived(0)
    receivers(0)
    tree_middle(1)
    arrived(1)
    receivers(1)
    arrived(2)
    receivers(2)
    sums(0, 0, 3)
    tree_end(1)
    arrived(3)
    sums(0, 3, 4)
    tree_start(0)
    receivers(3)
    for k in range(NP):
        own = jnp.logical_and(k == 0, p // 2 == q)

        @pl.when(jnp.logical_not(own))
        def _():
            remote(rgp.at[k], rgr.at[q, p % 2], g_send.at[0], g_recv.at[0], plane(k), p // 2).start()

        @pl.when(own)
        def _():
            pltpu.make_async_copy(rgp.at[k], rgr.at[q, p % 2], g_recv.at[0]).start()

    tree_middle(0)
    wait_bytes(rgr, g_recv.at[0])
    for half in range(2):
        total = (rgr[0, half] + rgr[1, half]) + (rgr[2, half] + rgr[3, half])
        rg_out[:, half * 1024 : (half + 1) * 1024] = jnp.where(keep, total, 0.0)
    tree_end(0)

    def sent(own, every, others, sem):
        @pl.when(jnp.logical_not(own))
        def _():
            wait_bytes(every, sem)

        @pl.when(own)
        def _():
            wait_bytes(others, sem)

    home = q == p // 2
    sent(home, us, us.at[1:NP], u_send.at[0])
    sent(q % 2 == y // 2, us, us.at[1:NP], ur_send.at[0])
    sent(q // 2 == x, uq, uq.at[1:4], uq_send.at[0])
    sent(home, rgp, rgp.at[1:NP], g_send.at[0])
    wait_bytes(vr.at[z, x], vx_send.at[0])
    wait_bytes(vq.at[z, 1:4], vy_send.at[0])
    wait_bytes(vr.at[1:NZ], vr_send.at[0])
    wait_bytes(vq.at[1:NZ], vq_send.at[0])
    wait_bytes(xsr.at[:, 1:4], xr_send.at[0])
    wait_bytes(xsq, xq_send.at[0])
    for h in range(2):
        wait_bytes(zs.at[4 * h : 4 * h + 4, 1:NP], z_send.at[h])
    for h in range(2):
        wait_bytes(tbuf.at[h], t_send.at[h])


def shards(receiver_spectra, reference_spectra, receiver_counts, reference_counts, column_station, lag_window, observed):
    table = lag_table()
    m = jnp.asarray(table, dtype=BF)
    mt = jnp.asarray(np.ascontiguousarray(table.T), dtype=BF)
    vmem = pl.BlockSpec(memory_space=pltpu.VMEM)
    hbm = pl.BlockSpec(memory_space=pl.ANY)
    dma = pltpu.SemaphoreType.DMA
    return pl.pallas_call(
        kernel,
        out_shape=(
            pltpu.VMEM((NI, 2048), F32),
            pltpu.VMEM((128, NJ), F32),
        ),
        in_specs=[hbm] * 9,
        out_specs=(pl.BlockSpec(memory_space=pltpu.MemorySpace.VMEM), pl.BlockSpec(memory_space=pltpu.MemorySpace.VMEM)),
        scratch_shapes=[
            pltpu.VMEM((NI, 2048), BF),
            pltpu.VMEM((128, NJ), BF),
            pltpu.VMEM((1, NI), jnp.int32),
            pltpu.VMEM((1, NJ), jnp.int32),
            pltpu.VMEM((1, NJ), jnp.int32),
            pltpu.VMEM((2, NI, NJ), jnp.int32),
            pltpu.VMEM((2, NI, 1152), BF),
            pltpu.VMEM((NP, NI, 1152), BF),
            pltpu.VMEM((4, 2, NI, 1152), BF),
            pltpu.VMEM((4, 2, NI, 1152), BF),
            pltpu.VMEM((NZ, 2, 128, 128), BF),
            pltpu.VMEM((NZ, 4, 128, 128), BF),
            pltpu.VMEM((NZ, 4, 2, NI, 256), F32),
            pltpu.VMEM((NZ, 2, 2, 2, NI, 256), F32),
            pltpu.VMEM((4, NI, 16, 256), BF),
            pltpu.VMEM((4, NI, 16, 128), F32),
            pltpu.VMEM((2, NI, 16, 128), F32),
            pltpu.VMEM((NG, 4, 2, 128, 256), BF),
            pltpu.VMEM((NG, 2, 256, 512), BF),
            pltpu.VMEM((8, NJ), F32),
            pltpu.VMEM((8, NJ), F32),
            pltpu.VMEM((8, NJ), F32),
            pltpu.VMEM((NI, NJ, L), BF),
            pltpu.VMEM((2 * F, 2 * L), BF),
            pltpu.VMEM((2 * L, 2 * F), BF),
            pltpu.VMEM((2 * L, 2 * F), BF),
            pltpu.VMEM((2 * L, 2 * F), BF),
            pltpu.VMEM((8, L, NJ), BF),
            pltpu.VMEM((NZ, 4, 4, 16, NJ), BF),
            pltpu.VMEM((4, 4, NZ, 16, NJ), BF),
            pltpu.VMEM((NZ, 4, 2, 16, NJ), BF),
            pltpu.VMEM((4, 2, NZ, 2, 16, NJ), BF),
            pltpu.VMEM((2 * L, NJ), BF),
            pltpu.VMEM((8, NP, NG, 16, NJ), BF),
            pltpu.VMEM((NG, 8, NP, 16, NJ), BF),
            pltpu.VMEM((2, NZ, 128, 128), F32),
            pltpu.VMEM((2, 7, 128, 128), F32),
            pltpu.VMEM((NP, NI, 1024), F32),
            pltpu.VMEM((4, 2, NI, 1024), F32),
            dma((9,)), dma((1,)), dma((1,)), dma((1,)), dma((1,)), dma((1,)), dma((1,)),
            dma((1,)), dma((1,)), dma((1,)), dma((4,)), dma((1,)), dma((NZ, 2)), dma((1,)), dma((NZ, 4)),
            dma((1,)), dma((1,)), dma((1,)), dma((1,)), dma((2,)), dma((8,)),
            dma((1,)), dma((1,)), dma((2,)), dma((2, 7, 2)),
        ],
        compiler_params=pltpu.CompilerParams(
            collective_id=0, has_side_effects=True, vmem_limit_bytes=60 * 1024 * 1024
        ),
    )(
        receiver_spectra,
        reference_spectra,
        receiver_counts.reshape(1, NI),
        reference_counts.reshape(1, NJ),
        column_station.reshape(1, NJ),
        lag_window,
        observed,
        m,
        mt,
    )


def solution(mesh):
    return jax.shard_map(
        shards,
        mesh=mesh,
        in_specs=(
            P("rcv", "ref"), P("rcv", "ref"), P("rcv"), P("ref"), P("ref"),
            P(None, "rcv", "ref"), P("rcv", "ref", None),
        ),
        out_specs=(P("rcv", "ref"), P("rcv", "ref")),
        check_vma=False,
    )
```

```python
import math

import jax
import jax.numpy as jnp
import numpy as np
from jax import lax
from jax.experimental import pallas as pl
from jax.experimental.pallas import tpu as pltpu
from jax.sharding import PartitionSpec as P

L = 512
S = 16
F = 256
NP = 8
NZ = 8
NI = 8
NJ = 256
NG = 4
MESH = pl.DeviceIdType.MESH
BF = jnp.bfloat16
F32 = jnp.float32

env_floor = 0.05
misfit_scale = 0.03125


def lag_table():
    freq_ids = np.arange(F, dtype=np.int64)[:, None]
    lag_ids = np.arange(L, dtype=np.int64)[None, :] - L // 2
    angle = ((freq_ids * lag_ids) % L).astype(np.float64) * (2.0 * math.pi / L)
    cosine = np.cos(angle) / math.sqrt(F)
    sine = np.sin(angle) / math.sqrt(F)
    real_rows = np.concatenate([cosine, sine], axis=1)
    imag_rows = np.concatenate([-sine, cosine], axis=1)
    stacked = np.stack([real_rows, imag_rows], axis=1).reshape(2 * F, 2 * L)
    return stacked.astype(np.float32)


def kernel(
    u_hbm, v_hbm, rc_hbm, fc_hbm, cs_hbm, win_hbm, obs_hbm, m_hbm, mt_hbm,
    rg_out, wg_out,
    u_ref, v_ref, rc_ref, fc_ref, cs_ref, win_ref,
    um, us, ur, uq, vr, vq, ucr, ucq, bw, scr, scq, bt, bb, ninv, first, last,
    obs, m_ref, mt_ref, mq_ref, mr_ref, obst, xsr, xrr, xsq, xrq, gs, zs, zr,
    w, tbuf, rgp, rgr,
    in_sem, u_send, u_recv, ur_send, ur_recv, uq_send, uq_recv,
    vx_send, vx_recv, vy_send, vy_recv, vr_send, vr_recv, vq_send, vq_recv,
    xr_send, xr_recv, xq_send, xq_recv, z_send, z_recv,
    g_send, g_recv, t_send, t_recv,
):
    r = lax.axis_index("rcv")
    q = lax.axis_index("ref")
    p = r // NZ
    z = r % NZ
    x = p // 4
    y = p % 4
    right = p * NZ + (z + 1) % NZ
    left = p * NZ + (z + NZ - 1) % NZ
    partner = ((p + 4) % NP) * NZ + z

    def signal(rr, qq):
        pl.semaphore_signal(barrier, inc=1, device_id=(rr, qq), device_id_type=MESH)

    def remote(src, dst, send, recv, rr, qq):
        return pltpu.make_async_remote_copy(
            src_ref=src, dst_ref=dst, send_sem=send, recv_sem=recv,
            device_id=(rr, qq), device_id_type=MESH,
        )

    def plane(k):
        return ((p + k) % NP) * NZ + z

    def wait_bytes(ref, sem):
        pltpu.make_async_copy(ref, ref, sem).wait()

    small = ((u_hbm, u_ref), (v_hbm, v_ref), (rc_hbm, rc_ref), (fc_hbm, fc_ref), (cs_hbm, cs_ref), (win_hbm, win_ref))
    firsts = [pltpu.make_async_copy(src, dst, in_sem.at[3 + n]) for n, (src, dst) in enumerate(small)]
    for load in firsts:
        load.start()

    barrier = pltpu.get_barrier_semaphore()
    for k in range(NP):
        for dq in range(4):
            if k or dq:
                signal(plane(k), (q + dq) % 4)
    for k in (1, 2, 6, 7):
        signal(p * NZ + (z + k) % NZ, q)

    loads = [pltpu.make_async_copy(obs_hbm.at[i], obs.at[i], in_sem.at[0]) for i in range(NI)]
    loads.append(pltpu.make_async_copy(mt_hbm, mt_ref, in_sem.at[1]))
    loads.append(pltpu.make_async_copy(m_hbm, m_ref, in_sem.at[2]))
    for load in loads:
        load.start()

    for load in firsts:
        load.wait()

    eye = lax.broadcasted_iota(jnp.int32, (NI, NI), 0) == lax.broadcasted_iota(jnp.int32, (NI, NI), 1)
    rcounts = jnp.sum(jnp.where(eye, rc_ref[...].astype(F32), 0.0), axis=1, keepdims=True)
    pc = fc_ref[...].astype(F32)
    row_mask = (lax.broadcasted_iota(jnp.int32, (128, NJ), 0) % S).astype(F32) < pc
    mine = jnp.where(row_mask, v_ref[...].astype(F32), 0.0).astype(BF)
    vq[z, y] = mine[:, 0:128]
    vr[z, x] = mine[:, 128:256]
    seg_lane = (lax.broadcasted_iota(jnp.int32, (NI, 1024), 1) % S).astype(F32)
    keep = seg_lane < rcounts
    for half in range(2):
        part = u_ref[:, half * 1024 : (half + 1) * 1024].astype(F32)
        um[half, :, 0:1024] = jnp.where(keep, part, 0.0).astype(BF)
        um[half, :, 1024:1152] = jnp.broadcast_to(rcounts, (NI, 128)).astype(BF)

    pl.semaphore_wait(barrier, 4 * NP - 1 + 4)

    def give(own, src, dst, send, recv, rr, qq):
        @pl.when(jnp.logical_not(own))
        def _():
            remote(src, dst, send, recv, rr, qq).start()

        @pl.when(own)
        def _():
            pltpu.make_async_copy(src, dst, recv).start()

    def pass_on(buf, send, recv, zz, sub, to):
        remote(buf.at[zz, sub], buf.at[zz, sub], send.at[0], recv.at[zz, sub], to, q).start()

    def pass_r(zz, sub, to):
        pass_on(vr, vr_send, vr_recv, zz, sub, to)

    def pass_q(zz, sub, to):
        pass_on(vq, vq_send, vq_recv, zz, sub, to)

    remote(vr.at[z, x], vr.at[z, x], vx_send.at[0], vx_recv.at[0], partner, q).start()
    for k in range(1, 4):
        remote(
            vq.at[z, y], vq.at[z, y], vy_send.at[0], vy_recv.at[y], (x * 4 + (y + k) % 4) * NZ + z, q
        ).start()
    pass_r(z, x, right)
    pass_r(z, x, left)
    pass_q(z, y, right)
    pass_q(z, y, left)
    for half in range(2):
        for qq in range(4):
            yd = 2 * (q % 2) + half
            own = jnp.logical_and(yd == y, qq == q)
            give(
                own, um.at[half], ur.at[(y - yd + 4) % 4, q // 2], ur_send.at[0], ur_recv.at[0],
                (x * 4 + yd) * NZ + z, qq,
            )
    for qq in range(4):
        xd = q // 2
        own = jnp.logical_and(xd == x, qq == q)
        give(
            own, um, uq.at[2 * ((x - xd + 2) % 2) + q % 2], uq_send.at[0], uq_recv.at[0],
            (xd * 4 + y) * NZ + z, qq,
        )
    order = cs_ref[...] - q * NJ
    stations = lax.broadcasted_iota(jnp.int32, (NJ, NJ), 0)
    onehot = jnp.where(stations == order, 1.0, 0.0).astype(BF)
    nt = (((1,), (1,)), ((), ()))
    begin = lax.dot_general(win_ref[0].astype(F32).astype(BF), onehot, nt, preferred_element_type=F32)
    span = lax.dot_general(win_ref[1].astype(F32).astype(BF), onehot, nt, preferred_element_type=F32)
    inv = 1.0 / jnp.minimum(rcounts, pc)
    for h in range(2):
        for i in range(NI):
            u, lanes, side = 4 * h + i // 2, pl.ds((i % 2) * 128, 128), slice(h * 128, (h + 1) * 128)
            first[u : u + 1, lanes] = begin[i : i + 1, side]
            last[u : u + 1, lanes] = begin[i : i + 1, side] + span[i : i + 1, side]
            ninv[u : u + 1, lanes] = inv[i : i + 1, side]
    def turn(ii, c):
        for par in range(2):
            seen = jnp.dot(onehot, obs[2 * ii + par], preferred_element_type=F32)
            seen = jnp.transpose(seen, (1, 0)).astype(BF)
            for h in range(2):
                obst[4 * h + ii, :, par * 128 : (par + 1) * 128] = seen[:, h * 128 : (h + 1) * 128]
        return c

    wait_bytes(obs, in_sem.at[0])
    lax.fori_loop(0, 2, turn, 0)

    wait_bytes(vr.at[z, 1 - x], vx_recv.at[0])
    pass_r(z, 1 - x, right)
    pass_r(z, 1 - x, left)
    for k in (1, 3, 2):
        yy = (y + k) % 4
        wait_bytes(vq.at[z, yy], vy_recv.at[yy])
        pass_q(z, yy, right)
        pass_q(z, yy, left)
    for half in range(2):
        for qq in range(4):
            pp = 2 * q + half
            rr = pp * NZ + z
            own = jnp.logical_and(rr == r, qq == q)
            slot = (p - pp + NP) % NP
            give(own, um.at[half], us.at[slot], u_send.at[0], u_recv.at[0], rr, qq)

    def back(s):
        return (z + NZ - s) % NZ

    def ahead(s):
        return (z + s) % NZ

    def step(s, buf, recv, pass_to, sub, up):
        if s <= up:
            wait_bytes(buf.at[back(s), sub], recv.at[back(s), sub])
            if s < up:
                pass_to(back(s), sub, right)
        if s <= 7 - up:
            wait_bytes(buf.at[ahead(s), sub], recv.at[ahead(s), sub])
            if s < 7 - up:
                pass_to(ahead(s), sub, left)

    def step_r(s):
        for k in range(2):
            step(s, vr, vr_recv, pass_r, (x + k) % 2, 4 - k)

    def step_q(s):
        for k in (0, 1, 3, 2):
            step(s, vq, vq_recv, pass_q, (y + k) % 4, 4 if k < 2 else 3)

    row16 = lax.broadcasted_iota(jnp.int32, (16, 256), 0)
    lane256 = lax.broadcasted_iota(jnp.int32, (16, 256), 1)
    diag = (lane256 // 32) == (row16 // 2)
    mask0 = jnp.logical_and(diag, row16 % 2 == 0)
    mask1 = jnp.logical_and(diag, row16 % 2 == 1)

    def turned(uf):
        part = (lax.broadcasted_iota(jnp.int32, (NI, 1024), 1) // S) % 2
        return jnp.where(part == 0, pltpu.roll(uf, 1024 - S, 1), -pltpu.roll(uf, S, 1))

    def blocks(a, b, out):
        for i in range(NI):
            out(i, jnp.where(mask0, a[i : i + 1], jnp.where(mask1, b[i : i + 1], 0.0)).astype(BF))

    def ready_r(yk, c):
        for xx in range(2):
            uf = ur[yk, xx, :, 0:1024].astype(F32)
            ut = turned(uf)
            for zz in range(NZ):
                ucr[zz, yk, 0, :, xx * 128 : (xx + 1) * 128] = uf[:, zz * 128 : (zz + 1) * 128]
                ucr[zz, yk, 1, :, xx * 128 : (xx + 1) * 128] = ut[:, zz * 128 : (zz + 1) * 128]
        inverse = 1.0 / jnp.minimum(ur[yk, 0, :, 1024:1025].astype(F32), pc[:, 128:256])
        for i in range(NI):
            scr[yk, i] = jnp.broadcast_to(inverse[i : i + 1], (16, 128))
        return c

    def ready_q(xk, c):
        for b in range(2):
            for half in range(2):
                uf = uq[2 * xk + b, half, :, 0:1024].astype(F32)
                ut = turned(uf)
                for zz in range(NZ):
                    ucq[zz, xk, b, 0, :, half * 128 : (half + 1) * 128] = uf[:, zz * 128 : (zz + 1) * 128]
                    ucq[zz, xk, b, 1, :, half * 128 : (half + 1) * 128] = ut[:, zz * 128 : (zz + 1) * 128]
        inverse = 1.0 / jnp.minimum(uq[2 * xk, 0, :, 1024:1025].astype(F32), pc[:, 0:128])
        for i in range(NI):
            scq[xk, i] = jnp.broadcast_to(inverse[i : i + 1], (16, 128))
        return c

    def cross_r(zz):
        for yk in range(4):
            def put(i, blk):
                bw[yk, i] = blk

            blocks(ucr[zz, yk, 0], ucr[zz, yk, 1], put)
        v = jnp.dot(bw[...].reshape(512, 256), vr[zz].reshape(256, 128), preferred_element_type=F32)
        v = (v * scr[...].reshape(512, 128)).astype(BF)
        for yk in range(4):
            for i in range(NI):
                rows = v[(yk * NI + i) * 16 : (yk * NI + i + 1) * 16]
                lanes = slice((i % 2) * 128, (i % 2 + 1) * 128)
                if yk:
                    xsr[zz, yk, i // 2, :, lanes] = rows
                else:
                    xrr[i // 2, y, zz, :, lanes] = rows
        for yk in range(1, 4):
            remote(
                xsr.at[zz, yk], xrr.at[:, y, zz], xr_send.at[0], xr_recv.at[0],
                (x * 4 + (y + yk) % 4) * NZ + z, q,
            ).start()

    def cross_q(zz):
        for b in range(2):
            for xk in range(2):
                def put(i, blk):
                    bw[2 * b + xk, i] = blk

                blocks(ucq[zz, xk, b, 0], ucq[zz, xk, b, 1], put)
        for b in range(2):
            v = jnp.dot(
                bw[2 * b : 2 * b + 2].reshape(256, 256), vq[zz, 2 * b : 2 * b + 2].reshape(256, 128),
                preferred_element_type=F32,
            )
            v = (v * scq[...].reshape(256, 128)).astype(BF)
            for xk in range(2):
                for i in range(NI):
                    rows = v[(xk * NI + i) * 16 : (xk * NI + i + 1) * 16]
                    lanes = slice((i % 2) * 128, (i % 2 + 1) * 128)
                    if xk:
                        xsq[zz, i // 2, b, :, lanes] = rows
                    else:
                        xrq[i // 2, x, zz, b, :, lanes] = rows
        remote(xsq.at[zz], xrq.at[:, x, zz], xq_send.at[0], xq_recv.at[0], partner, q).start()

    def crossings(cross, start, end):
        def one(j, c):
            cross((z + NZ + ((j + 1) // 2) * (2 * (j % 2) - 1)) % NZ)
            return c

        lax.fori_loop(start, end, one, 0)

    lax.fori_loop(2, 4, turn, 0)
    step_r(1)
    wait_bytes(ur, ur_recv.at[0])
    lax.fori_loop(0, 4, ready_r, 0)
    crossings(cross_r, 0, 3)
    step_r(2)
    crossings(cross_r, 3, 5)
    step_q(1)
    wait_bytes(uq, uq_recv.at[0])
    lax.fori_loop(0, 2, ready_q, 0)
    crossings(cross_q, 0, 3)
    step_r(3)
    crossings(cross_r, 5, 7)
    step_q(2)
    crossings(cross_q, 3, 5)

    here = lax.broadcasted_iota(jnp.int32, (2 * F, 2 * F), 0)
    n = lax.broadcasted_iota(jnp.int32, (2 * F, 2 * F), 1)
    from_r = n % 8 + 8 * ((n // 16) % 8) + 64 * (n // 128) + 256 * ((n // 8) % 2)
    from_q = n % 8 + 8 * ((n // 32) % 8) + 64 * ((n // 8) % 4) + 256 * (n // 256)

    def reorder(source, out):
        pick = jnp.where(here == source, 1.0, 0.0).astype(BF)
        for b in range(4):
            rows = slice(b * 256, (b + 1) * 256)
            out[rows, :] = jnp.dot(mt_ref[rows, :], pick, preferred_element_type=F32).astype(BF)

    for load in loads[NI:]:
        load.wait()
    reorder(from_r, mr_ref)
    step_r(4)
    crossings(cross_r, 7, 8)
    step_q(3)
    crossings(cross_q, 5, 7)
    reorder(from_q, mq_ref)

    TB = 128
    def pairs(u, got, table):
        lo = first[pl.ds(u, 1), :]
        hi = last[pl.ds(u, 1), :]
        for b in range(L // TB):
            cor = jnp.dot(table[b * TB : (b + 1) * TB, :], got, preferred_element_type=F32)
            hil = jnp.dot(table[L + b * TB : L + (b + 1) * TB, :], got, preferred_element_type=F32)
            rs = lax.rsqrt(cor * cor + hil * hil + env_floor)
            lag = (lax.broadcasted_iota(jnp.int32, (TB, NJ), 0) + b * TB).astype(F32)
            inside = jnp.logical_and(lag >= lo, lag < hi)
            seen = obst[u, b * TB : (b + 1) * TB, :].astype(F32)
            wt = jnp.where(inside, (1.0 - seen * rs) * misfit_scale, 0.0)
            gs[b * TB : (b + 1) * TB, :] = (wt * cor).astype(BF)
            gs[L + b * TB : L + (b + 1) * TB, :] = (wt * hil).astype(BF)
        scale = ninv[pl.ds(u, 1), :]
        for b in range(4):
            back = jnp.dot(m_ref[b * 128 : (b + 1) * 128, :], gs[...], preferred_element_type=F32)
            zs[u, 2 * b : 2 * b + 2] = (back * scale).astype(BF).reshape(2, NG, 16, NJ)
        zr[:, u, 0] = zs[u, p]

    def hand_out(u, across, beside):
        todo = [(1, k) for k in (0, 1, 3, 2) if across] + [(0, k) for k in (1, 3, 2) if beside]
        for xx, k in todo:
            peer = ((x + xx) % 2) * 4 + (y + k) % 4
            remote(
                zs.at[u, peer], zr.at[:, u, (p - peer + NP) % NP], z_send.at[u // 4], z_recv.at[u],
                peer * NZ + z, q,
            ).start()

    def pairs_r(ii, c):
        pairs(4 + ii, xrr[ii].reshape(2 * F, NJ), mr_ref)
        hand_out(4 + ii, True, True)
        return c

    def pairs_y(ii, c):
        pairs(4 + ii, xrr[ii].reshape(2 * F, NJ), mr_ref)
        hand_out(4 + ii, False, True)
        return c

    def hand_x(ii, c):
        hand_out(4 + ii, True, False)
        return c

    def pairs_q(ii, c):
        pairs(ii, xrq[ii].reshape(2 * F, NJ), mq_ref)
        hand_out(ii, True, True)
        return c

    wait_bytes(xsr.at[:, 1:4], xr_recv.at[0])
    lax.fori_loop(0, 2, pairs_y, 0)
    step_q(4)
    crossings(cross_q, 7, 8)
    lax.fori_loop(0, 2, hand_x, 0)
    lax.fori_loop(2, 4, pairs_r, 0)
    wait_bytes(xsq, xq_recv.at[0])
    lax.fori_loop(0, 4, pairs_q, 0)

    def operand(k, c):
        uf = us[k, :, 0:1024].astype(F32)
        ut = turned(uf)
        for g in range(NG):
            def put(i, blk):
                bt[g, i // 2, i % 2, pl.ds(k * 16, 16), :] = blk

            blocks(uf[:, g * 256 : (g + 1) * 256], ut[:, g * 256 : (g + 1) * 256], put)
        return c

    wait_bytes(us, u_recv.at[0])
    lax.fori_loop(0, NP, operand, 0)

    def flip(g, c):
        for ii in range(4):
            for par in range(2):
                bb[g, par, :, ii * 128 : (ii + 1) * 128] = jnp.transpose(
                    bt[g, ii, par].astype(F32), (1, 0)
                ).astype(BF)
        return c

    lax.fori_loop(0, NG, flip, 0)

    def arrived(u):
        wait_bytes(zs.at[u, 1:NP], z_recv.at[u])

    def sums(h, start, end):
        size = (end - start) * 128
        for g in range(NG):
            part = None
            for par in range(2):
                got = zr[g, 4 * h + start : 4 * h + end, :, :, par * 128 : (par + 1) * 128].reshape(size, 128)
                one = jnp.dot(bb[g, par, :, start * 128 : end * 128], got, preferred_element_type=F32)
                part = one if part is None else part + one
            part = part.reshape(2, 128, 128)
            if start:
                part = part + w[h, 2 * g : 2 * g + 2]
            w[h, 2 * g : 2 * g + 2] = part

    def toward(n, src, h, part, to):
        rows = slice(part * 64, (part + 1) * 64)
        remote(
            src.at[rows], tbuf.at[h, n, rows], t_send.at[h], t_recv.at[h, n, part],
            p * NZ + (z + NZ + to) % NZ, q,
        ).start()

    def landed(n, h, part):
        wait_bytes(tbuf.at[h, n, part * 64 : (part + 1) * 64], t_recv.at[h, n, part])

    def tree_start(h):
        for part in range(2):
            for n, m, to in ((0, 4, 2), (2, 5, -1), (1, 3, 1)):
                toward(n, w.at[h, (z + m) % NZ], h, part, to)
        for part in range(2):
            for n, m, to in ((3, 1, 1), (4, 7, -1)):
                toward(n, w.at[h, (z + m) % NZ], h, part, to)

    def tree_middle(h):
        for part in range(2):
            rows = slice(part * 64, (part + 1) * 64)
            landed(2, h, part)
            tbuf[h, 2, rows] = tbuf[h, 2, rows] + w[h, (z + 6) % NZ, rows]
            toward(6, tbuf.at[h, 2], h, part, -2)
            landed(1, h, part)
            landed(0, h, part)
            tbuf[h, 0, rows] = tbuf[h, 0, rows] + (tbuf[h, 1, rows] + w[h, (z + 2) % NZ, rows])
            toward(5, tbuf.at[h, 0], h, part, 2)

    def tree_end(h):
        for n in (3, 4, 6, 5):
            for part in range(2):
                landed(n, h, part)
        done = (w[h, z] + tbuf[h, 3]) + (tbuf[h, 4] + tbuf[h, 6]) + tbuf[h, 5]
        cols = slice(h * 128, (h + 1) * 128)
        wg_out[:, cols] = jnp.where(row_mask[:, cols], done, 0.0)

    lane8 = (lax.broadcasted_iota(jnp.int32, (NP, 256), 1) // S) % 2

    def receivers(ii):
        for g in range(NG):
            for par in range(2):
                t = None
                for h in range(2):
                    got = zr[g, 4 * h + ii, :, :, par * 128 : (par + 1) * 128].reshape(128, 128)
                    held = vr[2 * g : 2 * g + 2, x] if h else vq[2 * g : 2 * g + 2, y]
                    block = held.reshape(256, 128)
                    part = lax.dot_general(got, block, nt, preferred_element_type=F32)
                    t = part if t is None else t + part
                t = t.reshape(NP, 16, 256)
                a0 = jnp.sum(jnp.where(mask0[None], t, 0.0), axis=1)
                a1 = jnp.sum(jnp.where(mask1[None], t, 0.0), axis=1)
                rg = a0 + jnp.where(lane8 == 0, -pltpu.roll(a1, 256 - S, 1), pltpu.roll(a1, S, 1))
                i = 2 * ii + par
                for k in range(NP):
                    rgp[k, i : i + 1, g * 256 : (g + 1) * 256] = rg[k : k + 1]

    for u in range(4, 8):
        arrived(u)
    sums(1, 0, 4)
    tree_start(1)
    arrived(0)
    receivers(0)
    tree_middle(1)
    arrived(1)
    receivers(1)
    arrived(2)
    receivers(2)
    sums(0, 0, 3)
    tree_end(1)
    arrived(3)
    sums(0, 3, 4)
    tree_start(0)
    receivers(3)
    for k in range(NP):
        own = jnp.logical_and(k == 0, p // 2 == q)

        @pl.when(jnp.logical_not(own))
        def _():
            remote(rgp.at[k], rgr.at[q, p % 2], g_send.at[0], g_recv.at[0], plane(k), p // 2).start()

        @pl.when(own)
        def _():
            pltpu.make_async_copy(rgp.at[k], rgr.at[q, p % 2], g_recv.at[0]).start()

    tree_middle(0)
    wait_bytes(rgr, g_recv.at[0])
    for half in range(2):
        total = (rgr[0, half] + rgr[1, half]) + (rgr[2, half] + rgr[3, half])
        rg_out[:, half * 1024 : (half + 1) * 1024] = jnp.where(keep, total, 0.0)
    tree_end(0)

    def sent(own, every, others, sem):
        @pl.when(jnp.logical_not(own))
        def _():
            wait_bytes(every, sem)

        @pl.when(own)
        def _():
            wait_bytes(others, sem)

    home = q == p // 2
    sent(home, us, us.at[1:NP], u_send.at[0])
    sent(q % 2 == y // 2, us, us.at[1:NP], ur_send.at[0])
    sent(q // 2 == x, uq, uq.at[1:4], uq_send.at[0])
    sent(home, rgp, rgp.at[1:NP], g_send.at[0])
    wait_bytes(vr.at[z, x], vx_send.at[0])
    wait_bytes(vq.at[z, 1:4], vy_send.at[0])
    wait_bytes(vr.at[1:NZ], vr_send.at[0])
    wait_bytes(vq.at[1:NZ], vq_send.at[0])
    wait_bytes(xsr.at[:, 1:4], xr_send.at[0])
    wait_bytes(xsq, xq_send.at[0])
    for h in range(2):
        wait_bytes(zs.at[4 * h : 4 * h + 4, 1:NP], z_send.at[h])
    for h in range(2):
        wait_bytes(tbuf.at[h], t_send.at[h])


def shards(receiver_spectra, reference_spectra, receiver_counts, reference_counts, column_station, lag_window, observed):
    table = lag_table()
    m = jnp.asarray(table, dtype=BF)
    mt = jnp.asarray(np.ascontiguousarray(table.T), dtype=BF)
    vmem = pl.BlockSpec(memory_space=pltpu.VMEM)
    hbm = pl.BlockSpec(memory_space=pl.ANY)
    dma = pltpu.SemaphoreType.DMA
    return pl.pallas_call(
        kernel,
        out_shape=(
            pltpu.VMEM((NI, 2048), F32),
            pltpu.VMEM((128, NJ), F32),
        ),
        in_specs=[hbm] * 9,
        out_specs=(pl.BlockSpec(memory_space=pltpu.MemorySpace.VMEM), pl.BlockSpec(memory_space=pltpu.MemorySpace.VMEM)),
        scratch_shapes=[
            pltpu.VMEM((NI, 2048), BF),
            pltpu.VMEM((128, NJ), BF),
            pltpu.VMEM((1, NI), jnp.int32),
            pltpu.VMEM((1, NJ), jnp.int32),
            pltpu.VMEM((1, NJ), jnp.int32),
            pltpu.VMEM((2, NI, NJ), jnp.int32),
            pltpu.VMEM((2, NI, 1152), BF),
            pltpu.VMEM((NP, NI, 1152), BF),
            pltpu.VMEM((4, 2, NI, 1152), BF),
            pltpu.VMEM((4, 2, NI, 1152), BF),
            pltpu.VMEM((NZ, 2, 128, 128), BF),
            pltpu.VMEM((NZ, 4, 128, 128), BF),
            pltpu.VMEM((NZ, 4, 2, NI, 256), F32),
            pltpu.VMEM((NZ, 2, 2, 2, NI, 256), F32),
            pltpu.VMEM((4, NI, 16, 256), BF),
            pltpu.VMEM((4, NI, 16, 128), F32),
            pltpu.VMEM((2, NI, 16, 128), F32),
            pltpu.VMEM((NG, 4, 2, 128, 256), BF),
            pltpu.VMEM((NG, 2, 256, 512), BF),
            pltpu.VMEM((8, NJ), F32),
            pltpu.VMEM((8, NJ), F32),
            pltpu.VMEM((8, NJ), F32),
            pltpu.VMEM((NI, NJ, L), BF),
            pltpu.VMEM((2 * F, 2 * L), BF),
            pltpu.VMEM((2 * L, 2 * F), BF),
            pltpu.VMEM((2 * L, 2 * F), BF),
            pltpu.VMEM((2 * L, 2 * F), BF),
            pltpu.VMEM((8, L, NJ), BF),
            pltpu.VMEM((NZ, 4, 4, 16, NJ), BF),
            pltpu.VMEM((4, 4, NZ, 16, NJ), BF),
            pltpu.VMEM((NZ, 4, 2, 16, NJ), BF),
            pltpu.VMEM((4, 2, NZ, 2, 16, NJ), BF),
            pltpu.VMEM((2 * L, NJ), BF),
            pltpu.VMEM((8, NP, NG, 16, NJ), BF),
            pltpu.VMEM((NG, 8, NP, 16, NJ), BF),
            pltpu.VMEM((2, NZ, 128, 128), F32),
            pltpu.VMEM((2, 7, 128, 128), F32),
            pltpu.VMEM((NP, NI, 1024), F32),
            pltpu.VMEM((4, 2, NI, 1024), F32),
            dma((9,)), dma((1,)), dma((1,)), dma((1,)), dma((1,)), dma((1,)), dma((1,)),
            dma((1,)), dma((1,)), dma((1,)), dma((4,)), dma((1,)), dma((NZ, 2)), dma((1,)), dma((NZ, 4)),
            dma((1,)), dma((1,)), dma((1,)), dma((1,)), dma((2,)), dma((8,)),
            dma((1,)), dma((1,)), dma((2,)), dma((2, 7, 2)),
        ],
        compiler_params=pltpu.CompilerParams(
            collective_id=0, has_side_effects=True, vmem_limit_bytes=60 * 1024 * 1024
        ),
    )(
        receiver_spectra,
        reference_spectra,
        receiver_counts.reshape(1, NI),
        reference_counts.reshape(1, NJ),
        column_station.reshape(1, NJ),
        lag_window,
        observed,
        m,
        mt,
    )


def solution(mesh):
    return jax.shard_map(
        shards,
        mesh=mesh,
        in_specs=(
            P("rcv", "ref"), P("rcv", "ref"), P("rcv"), P("ref"), P("ref"),
            P(None, "rcv", "ref"), P("rcv", "ref", None),
        ),
        out_specs=(P("rcv", "ref"), P("rcv", "ref")),
        check_vma=False,
    )
```

```python
import math

import jax
import jax.numpy as jnp
import numpy as np
from jax import lax
from jax.experimental import pallas as pl
from jax.experimental.pallas import tpu as pltpu
from jax.sharding import PartitionSpec as P

L = 512
S = 16
F = 256
NP = 8
NZ = 8
NI = 8
NJ = 256
NG = 4
MESH = pl.DeviceIdType.MESH
BF = jnp.bfloat16
F32 = jnp.float32

env_floor = 0.05
misfit_scale = 0.03125


def lag_table():
    freq_ids = np.arange(F, dtype=np.int64)[:, None]
    lag_ids = np.arange(L, dtype=np.int64)[None, :] - L // 2
    angle = ((freq_ids * lag_ids) % L).astype(np.float64) * (2.0 * math.pi / L)
    cosine = np.cos(angle) / math.sqrt(F)
    sine = np.sin(angle) / math.sqrt(F)
    real_rows = np.concatenate([cosine, sine], axis=1)
    imag_rows = np.concatenate([-sine, cosine], axis=1)
    stacked = np.stack([real_rows, imag_rows], axis=1).reshape(2 * F, 2 * L)
    return stacked.astype(np.float32)


def kernel(
    u_hbm, v_hbm, rc_hbm, fc_hbm, cs_hbm, win_hbm, obs_hbm, m_hbm, mt_hbm,
    rg_out, wg_out,
    u_ref, v_ref, rc_ref, fc_ref, cs_ref, win_ref,
    um, us, ur, uq, vr, vq, ucr, ucq, bw, scr, scq, bt, bb, ninv, first, last,
    obs, m_ref, mt_ref, mq_ref, mr_ref, obst, xsr, xrr, xsq, xrq, gs, zs, zr,
    w, tbuf, rgp, rgr,
    in_sem, u_send, u_recv, ur_send, ur_recv, uq_send, uq_recv,
    vx_send, vx_recv, vy_send, vy_recv, vr_send, vr_recv, vq_send, vq_recv,
    xr_send, xr_recv, xq_send, xq_recv, z_send, z_recv,
    g_send, g_recv, t_send, t_recv,
):
    r = lax.axis_index("rcv")
    q = lax.axis_index("ref")
    p = r // NZ
    z = r % NZ
    x = p // 4
    y = p % 4
    right = p * NZ + (z + 1) % NZ
    left = p * NZ + (z + NZ - 1) % NZ
    partner = ((p + 4) % NP) * NZ + z

    def signal(rr, qq):
        pl.semaphore_signal(barrier, inc=1, device_id=(rr, qq), device_id_type=MESH)

    def remote(src, dst, send, recv, rr, qq):
        return pltpu.make_async_remote_copy(
            src_ref=src, dst_ref=dst, send_sem=send, recv_sem=recv,
            device_id=(rr, qq), device_id_type=MESH,
        )

    def plane(k):
        return ((p + k) % NP) * NZ + z

    def wait_bytes(ref, sem):
        pltpu.make_async_copy(ref, ref, sem).wait()

    small = ((u_hbm, u_ref), (v_hbm, v_ref), (rc_hbm, rc_ref), (fc_hbm, fc_ref), (cs_hbm, cs_ref), (win_hbm, win_ref))
    firsts = [pltpu.make_async_copy(src, dst, in_sem.at[3 + n]) for n, (src, dst) in enumerate(small)]
    for load in firsts:
        load.start()

    barrier = pltpu.get_barrier_semaphore()
    for k in range(NP):
        for dq in range(4):
            if k or dq:
                signal(plane(k), (q + dq) % 4)
    for k in (1, 2, 6, 7):
        signal(p * NZ + (z + k) % NZ, q)

    loads = [pltpu.make_async_copy(obs_hbm.at[i], obs.at[i], in_sem.at[0]) for i in range(NI)]
    loads.append(pltpu.make_async_copy(mt_hbm, mt_ref, in_sem.at[1]))
    loads.append(pltpu.make_async_copy(m_hbm, m_ref, in_sem.at[2]))
    for load in loads:
        load.start()

    for load in firsts:
        load.wait()

    eye = lax.broadcasted_iota(jnp.int32, (NI, NI), 0) == lax.broadcasted_iota(jnp.int32, (NI, NI), 1)
    rcounts = jnp.sum(jnp.where(eye, rc_ref[...].astype(F32), 0.0), axis=1, keepdims=True)
    pc = fc_ref[...].astype(F32)
    row_mask = (lax.broadcasted_iota(jnp.int32, (128, NJ), 0) % S).astype(F32) < pc
    mine = jnp.where(row_mask, v_ref[...].astype(F32), 0.0).astype(BF)
    vq[z, y] = mine[:, 0:128]
    vr[z, x] = mine[:, 128:256]
    seg_lane = (lax.broadcasted_iota(jnp.int32, (NI, 1024), 1) % S).astype(F32)
    keep = seg_lane < rcounts
    for half in range(2):
        part = u_ref[:, half * 1024 : (half + 1) * 1024].astype(F32)
        um[half, :, 0:1024] = jnp.where(keep, part, 0.0).astype(BF)
        um[half, :, 1024:1152] = jnp.broadcast_to(rcounts, (NI, 128)).astype(BF)

    pl.semaphore_wait(barrier, 4 * NP - 1 + 4)

    def give(own, src, dst, send, recv, rr, qq):
        @pl.when(jnp.logical_not(own))
        def _():
            remote(src, dst, send, recv, rr, qq).start()

        @pl.when(own)
        def _():
            pltpu.make_async_copy(src, dst, recv).start()

    def pass_on(buf, send, recv, zz, sub, to):
        remote(buf.at[zz, sub], buf.at[zz, sub], send.at[0], recv.at[zz, sub], to, q).start()

    def pass_r(zz, sub, to):
        pass_on(vr, vr_send, vr_recv, zz, sub, to)

    def pass_q(zz, sub, to):
        pass_on(vq, vq_send, vq_recv, zz, sub, to)

    remote(vr.at[z, x], vr.at[z, x], vx_send.at[0], vx_recv.at[0], partner, q).start()
    for k in range(1, 4):
        remote(
            vq.at[z, y], vq.at[z, y], vy_send.at[0], vy_recv.at[y], (x * 4 + (y + k) % 4) * NZ + z, q
        ).start()
    pass_r(z, x, right)
    pass_r(z, x, left)
    pass_q(z, y, right)
    pass_q(z, y, left)
    for half in range(2):
        for qq in range(4):
            yd = 2 * (q % 2) + half
            own = jnp.logical_and(yd == y, qq == q)
            give(
                own, um.at[half], ur.at[(y - yd + 4) % 4, q // 2], ur_send.at[0], ur_recv.at[0],
                (x * 4 + yd) * NZ + z, qq,
            )
    for qq in range(4):
        xd = q // 2
        own = jnp.logical_and(xd == x, qq == q)
        give(
            own, um, uq.at[2 * ((x - xd + 2) % 2) + q % 2], uq_send.at[0], uq_recv.at[0],
            (xd * 4 + y) * NZ + z, qq,
        )
    order = cs_ref[...] - q * NJ
    stations = lax.broadcasted_iota(jnp.int32, (NJ, NJ), 0)
    onehot = jnp.where(stations == order, 1.0, 0.0).astype(BF)
    nt = (((1,), (1,)), ((), ()))
    begin = lax.dot_general(win_ref[0].astype(F32).astype(BF), onehot, nt, preferred_element_type=F32)
    span = lax.dot_general(win_ref[1].astype(F32).astype(BF), onehot, nt, preferred_element_type=F32)
    inv = 1.0 / jnp.minimum(rcounts, pc)
    for h in range(2):
        for i in range(NI):
            u, lanes, side = 4 * h + i // 2, pl.ds((i % 2) * 128, 128), slice(h * 128, (h + 1) * 128)
            first[u : u + 1, lanes] = begin[i : i + 1, side]
            last[u : u + 1, lanes] = begin[i : i + 1, side] + span[i : i + 1, side]
            ninv[u : u + 1, lanes] = inv[i : i + 1, side]
    def turn(ii, c):
        for par in range(2):
            seen = jnp.dot(onehot, obs[2 * ii + par], preferred_element_type=F32)
            seen = jnp.transpose(seen, (1, 0)).astype(BF)
            for h in range(2):
                obst[4 * h + ii, :, par * 128 : (par + 1) * 128] = seen[:, h * 128 : (h + 1) * 128]
        return c

    wait_bytes(obs, in_sem.at[0])
    lax.fori_loop(0, 2, turn, 0)

    wait_bytes(vr.at[z, 1 - x], vx_recv.at[0])
    pass_r(z, 1 - x, right)
    pass_r(z, 1 - x, left)
    for k in (1, 3, 2):
        yy = (y + k) % 4
        wait_bytes(vq.at[z, yy], vy_recv.at[yy])
        pass_q(z, yy, right)
        pass_q(z, yy, left)
    for half in range(2):
        for qq in range(4):
            pp = 2 * q + half
            rr = pp * NZ + z
            own = jnp.logical_and(rr == r, qq == q)
            slot = (p - pp + NP) % NP
            give(own, um.at[half], us.at[slot], u_send.at[0], u_recv.at[0], rr, qq)

    def back(s):
        return (z + NZ - s) % NZ

    def ahead(s):
        return (z + s) % NZ

    def step(s, buf, recv, pass_to, sub, up):
        if s <= up:
            wait_bytes(buf.at[back(s), sub], recv.at[back(s), sub])
            if s < up:
                pass_to(back(s), sub, right)
        if s <= 7 - up:
            wait_bytes(buf.at[ahead(s), sub], recv.at[ahead(s), sub])
            if s < 7 - up:
                pass_to(ahead(s), sub, left)

    def step_r(s):
        for k in range(2):
            step(s, vr, vr_recv, pass_r, (x + k) % 2, 4 - k)

    def step_q(s):
        for k in (0, 1, 3, 2):
            step(s, vq, vq_recv, pass_q, (y + k) % 4, 4 if k < 2 else 3)

    row16 = lax.broadcasted_iota(jnp.int32, (16, 256), 0)
    lane256 = lax.broadcasted_iota(jnp.int32, (16, 256), 1)
    diag = (lane256 // 32) == (row16 // 2)
    mask0 = jnp.logical_and(diag, row16 % 2 == 0)
    mask1 = jnp.logical_and(diag, row16 % 2 == 1)

    def turned(uf):
        part = (lax.broadcasted_iota(jnp.int32, (NI, 1024), 1) // S) % 2
        return jnp.where(part == 0, pltpu.roll(uf, 1024 - S, 1), -pltpu.roll(uf, S, 1))

    def blocks(a, b, out):
        for i in range(NI):
            out(i, jnp.where(mask0, a[i : i + 1], jnp.where(mask1, b[i : i + 1], 0.0)).astype(BF))

    def ready_r(yk, c):
        for xx in range(2):
            uf = ur[yk, xx, :, 0:1024].astype(F32)
            ut = turned(uf)
            for zz in range(NZ):
                ucr[zz, yk, 0, :, xx * 128 : (xx + 1) * 128] = uf[:, zz * 128 : (zz + 1) * 128]
                ucr[zz, yk, 1, :, xx * 128 : (xx + 1) * 128] = ut[:, zz * 128 : (zz + 1) * 128]
        inverse = 1.0 / jnp.minimum(ur[yk, 0, :, 1024:1025].astype(F32), pc[:, 128:256])
        for i in range(NI):
            scr[yk, i] = jnp.broadcast_to(inverse[i : i + 1], (16, 128))
        return c

    def ready_q(xk, c):
        for b in range(2):
            for half in range(2):
                uf = uq[2 * xk + b, half, :, 0:1024].astype(F32)
                ut = turned(uf)
                for zz in range(NZ):
                    ucq[zz, xk, b, 0, :, half * 128 : (half + 1) * 128] = uf[:, zz * 128 : (zz + 1) * 128]
                    ucq[zz, xk, b, 1, :, half * 128 : (half + 1) * 128] = ut[:, zz * 128 : (zz + 1) * 128]
        inverse = 1.0 / jnp.minimum(uq[2 * xk, 0, :, 1024:1025].astype(F32), pc[:, 0:128])
        for i in range(NI):
            scq[xk, i] = jnp.broadcast_to(inverse[i : i + 1], (16, 128))
        return c

    def cross_r(zz):
        for yk in range(4):
            def put(i, blk):
                bw[yk, i] = blk

            blocks(ucr[zz, yk, 0], ucr[zz, yk, 1], put)
        v = jnp.dot(bw[...].reshape(512, 256), vr[zz].reshape(256, 128), preferred_element_type=F32)
        v = (v * scr[...].reshape(512, 128)).astype(BF)
        for yk in range(4):
            for i in range(NI):
                rows = v[(yk * NI + i) * 16 : (yk * NI + i + 1) * 16]
                lanes = slice((i % 2) * 128, (i % 2 + 1) * 128)
                if yk:
                    xsr[zz, yk, i // 2, :, lanes] = rows
                else:
                    xrr[i // 2, y, zz, :, lanes] = rows
        for yk in range(1, 4):
            remote(
                xsr.at[zz, yk], xrr.at[:, y, zz], xr_send.at[0], xr_recv.at[0],
                (x * 4 + (y + yk) % 4) * NZ + z, q,
            ).start()

    def cross_q(zz):
        for b in range(2):
            for xk in range(2):
                def put(i, blk):
                    bw[2 * b + xk, i] = blk

                blocks(ucq[zz, xk, b, 0], ucq[zz, xk, b, 1], put)
        for b in range(2):
            v = jnp.dot(
                bw[2 * b : 2 * b + 2].reshape(256, 256), vq[zz, 2 * b : 2 * b + 2].reshape(256, 128),
                preferred_element_type=F32,
            )
            v = (v * scq[...].reshape(256, 128)).astype(BF)
            for xk in range(2):
                for i in range(NI):
                    rows = v[(xk * NI + i) * 16 : (xk * NI + i + 1) * 16]
                    lanes = slice((i % 2) * 128, (i % 2 + 1) * 128)
                    if xk:
                        xsq[zz, i // 2, b, :, lanes] = rows
                    else:
                        xrq[i // 2, x, zz, b, :, lanes] = rows
        remote(xsq.at[zz], xrq.at[:, x, zz], xq_send.at[0], xq_recv.at[0], partner, q).start()

    def crossings(cross, start, end):
        def one(j, c):
            cross((z + NZ + ((j + 1) // 2) * (2 * (j % 2) - 1)) % NZ)
            return c

        lax.fori_loop(start, end, one, 0)

    lax.fori_loop(2, 4, turn, 0)
    step_r(1)
    wait_bytes(ur, ur_recv.at[0])
    lax.fori_loop(0, 4, ready_r, 0)
    crossings(cross_r, 0, 3)
    step_r(2)
    crossings(cross_r, 3, 5)
    step_q(1)
    wait_bytes(uq, uq_recv.at[0])
    lax.fori_loop(0, 2, ready_q, 0)
    crossings(cross_q, 0, 3)
    step_r(3)
    crossings(cross_r, 5, 7)
    step_q(2)
    crossings(cross_q, 3, 5)

    here = lax.broadcasted_iota(jnp.int32, (2 * F, 2 * F), 0)
    n = lax.broadcasted_iota(jnp.int32, (2 * F, 2 * F), 1)
    from_r = n % 8 + 8 * ((n // 16) % 8) + 64 * (n // 128) + 256 * ((n // 8) % 2)
    from_q = n % 8 + 8 * ((n // 32) % 8) + 64 * ((n // 8) % 4) + 256 * (n // 256)

    def reorder(source, out):
        pick = jnp.where(here == source, 1.0, 0.0).astype(BF)
        for b in range(4):
            rows = slice(b * 256, (b + 1) * 256)
            out[rows, :] = jnp.dot(mt_ref[rows, :], pick, preferred_element_type=F32).astype(BF)

    for load in loads[NI:]:
        load.wait()
    reorder(from_r, mr_ref)
    step_r(4)
    crossings(cross_r, 7, 8)
    step_q(3)
    crossings(cross_q, 5, 7)
    reorder(from_q, mq_ref)
    step_q(4)
    crossings(cross_q, 7, 8)

    TB = 128
    def pairs(u, got, table):
        lo = first[pl.ds(u, 1), :]
        hi = last[pl.ds(u, 1), :]
        for b in range(L // TB):
            cor = jnp.dot(table[b * TB : (b + 1) * TB, :], got, preferred_element_type=F32)
            hil = jnp.dot(table[L + b * TB : L + (b + 1) * TB, :], got, preferred_element_type=F32)
            rs = lax.rsqrt(cor * cor + hil * hil + env_floor)
            lag = (lax.broadcasted_iota(jnp.int32, (TB, NJ), 0) + b * TB).astype(F32)
            inside = jnp.logical_and(lag >= lo, lag < hi)
            seen = obst[u, b * TB : (b + 1) * TB, :].astype(F32)
            wt = jnp.where(inside, (1.0 - seen * rs) * misfit_scale, 0.0)
            gs[b * TB : (b + 1) * TB, :] = (wt * cor).astype(BF)
            gs[L + b * TB : L + (b + 1) * TB, :] = (wt * hil).astype(BF)
        scale = ninv[pl.ds(u, 1), :]
        for b in range(4):
            back = jnp.dot(m_ref[b * 128 : (b + 1) * 128, :], gs[...], preferred_element_type=F32)
            zs[u, 2 * b : 2 * b + 2] = (back * scale).astype(BF).reshape(2, NG, 16, NJ)
        for k in range(1, NP):
            remote(
                zs.at[u, (p + k) % NP], zr.at[:, u, NP - k], z_send.at[u // 4], z_recv.at[u], plane(k), q
            ).start()
        zr[:, u, 0] = zs[u, p]

    def pairs_r(ii, c):
        pairs(4 + ii, xrr[ii].reshape(2 * F, NJ), mr_ref)
        return c

    def pairs_q(ii, c):
        pairs(ii, xrq[ii].reshape(2 * F, NJ), mq_ref)
        return c

    wait_bytes(xsr.at[:, 1:4], xr_recv.at[0])
    lax.fori_loop(0, 4, pairs_r, 0)
    wait_bytes(xsq, xq_recv.at[0])
    lax.fori_loop(0, 4, pairs_q, 0)

    def operand(k, c):
        uf = us[k, :, 0:1024].astype(F32)
        ut = turned(uf)
        for g in range(NG):
            def put(i, blk):
                bt[g, i // 2, i % 2, pl.ds(k * 16, 16), :] = blk

            blocks(uf[:, g * 256 : (g + 1) * 256], ut[:, g * 256 : (g + 1) * 256], put)
        return c

    wait_bytes(us, u_recv.at[0])
    lax.fori_loop(0, NP, operand, 0)

    def flip(g, c):
        for ii in range(4):
            for par in range(2):
                bb[g, par, :, ii * 128 : (ii + 1) * 128] = jnp.transpose(
                    bt[g, ii, par].astype(F32), (1, 0)
                ).astype(BF)
        return c

    lax.fori_loop(0, NG, flip, 0)

    def arrived(u):
        wait_bytes(zs.at[u, 1:NP], z_recv.at[u])

    def sums(h, start, end):
        size = (end - start) * 128
        for g in range(NG):
            part = None
            for par in range(2):
                got = zr[g, 4 * h + start : 4 * h + end, :, :, par * 128 : (par + 1) * 128].reshape(size, 128)
                one = jnp.dot(bb[g, par, :, start * 128 : end * 128], got, preferred_element_type=F32)
                part = one if part is None else part + one
            part = part.reshape(2, 128, 128)
            if start:
                part = part + w[h, 2 * g : 2 * g + 2]
            w[h, 2 * g : 2 * g + 2] = part

    def toward(n, src, h, part, to):
        rows = slice(part * 64, (part + 1) * 64)
        remote(
            src.at[rows], tbuf.at[h, n, rows], t_send.at[h], t_recv.at[h, n, part],
            p * NZ + (z + NZ + to) % NZ, q,
        ).start()

    def landed(n, h, part):
        wait_bytes(tbuf.at[h, n, part * 64 : (part + 1) * 64], t_recv.at[h, n, part])

    def tree_start(h):
        for part in range(2):
            for n, m, to in ((0, 4, 2), (2, 5, -1), (1, 3, 1)):
                toward(n, w.at[h, (z + m) % NZ], h, part, to)
        for part in range(2):
            for n, m, to in ((3, 1, 1), (4, 7, -1)):
                toward(n, w.at[h, (z + m) % NZ], h, part, to)

    def tree_middle(h):
        for part in range(2):
            rows = slice(part * 64, (part + 1) * 64)
            landed(2, h, part)
            tbuf[h, 2, rows] = tbuf[h, 2, rows] + w[h, (z + 6) % NZ, rows]
            toward(6, tbuf.at[h, 2], h, part, -2)
            landed(1, h, part)
            landed(0, h, part)
            tbuf[h, 0, rows] = tbuf[h, 0, rows] + (tbuf[h, 1, rows] + w[h, (z + 2) % NZ, rows])
            toward(5, tbuf.at[h, 0], h, part, 2)

    def tree_end(h):
        for n in (3, 4, 6, 5):
            for part in range(2):
                landed(n, h, part)
        done = (w[h, z] + tbuf[h, 3]) + (tbuf[h, 4] + tbuf[h, 6]) + tbuf[h, 5]
        cols = slice(h * 128, (h + 1) * 128)
        wg_out[:, cols] = jnp.where(row_mask[:, cols], done, 0.0)

    lane8 = (lax.broadcasted_iota(jnp.int32, (NP, 256), 1) // S) % 2

    def receivers(ii):
        for g in range(NG):
            for par in range(2):
                t = None
                for h in range(2):
                    got = zr[g, 4 * h + ii, :, :, par * 128 : (par + 1) * 128].reshape(128, 128)
                    held = vr[2 * g : 2 * g + 2, x] if h else vq[2 * g : 2 * g + 2, y]
                    block = held.reshape(256, 128)
                    part = lax.dot_general(got, block, nt, preferred_element_type=F32)
                    t = part if t is None else t + part
                t = t.reshape(NP, 16, 256)
                a0 = jnp.sum(jnp.where(mask0[None], t, 0.0), axis=1)
                a1 = jnp.sum(jnp.where(mask1[None], t, 0.0), axis=1)
                rg = a0 + jnp.where(lane8 == 0, -pltpu.roll(a1, 256 - S, 1), pltpu.roll(a1, S, 1))
                i = 2 * ii + par
                for k in range(NP):
                    rgp[k, i : i + 1, g * 256 : (g + 1) * 256] = rg[k : k + 1]

    for u in range(4, 8):
        arrived(u)
    sums(1, 0, 4)
    tree_start(1)
    arrived(0)
    receivers(0)
    tree_middle(1)
    arrived(1)
    receivers(1)
    arrived(2)
    receivers(2)
    sums(0, 0, 3)
    tree_end(1)
    arrived(3)
    sums(0, 3, 4)
    tree_start(0)
    receivers(3)
    for k in range(NP):
        own = jnp.logical_and(k == 0, p // 2 == q)

        @pl.when(jnp.logical_not(own))
        def _():
            remote(rgp.at[k], rgr.at[q, p % 2], g_send.at[0], g_recv.at[0], plane(k), p // 2).start()

        @pl.when(own)
        def _():
            pltpu.make_async_copy(rgp.at[k], rgr.at[q, p % 2], g_recv.at[0]).start()

    tree_middle(0)
    wait_bytes(rgr, g_recv.at[0])
    for half in range(2):
        total = (rgr[0, half] + rgr[1, half]) + (rgr[2, half] + rgr[3, half])
        rg_out[:, half * 1024 : (half + 1) * 1024] = jnp.where(keep, total, 0.0)
    tree_end(0)

    def sent(own, every, others, sem):
        @pl.when(jnp.logical_not(own))
        def _():
            wait_bytes(every, sem)

        @pl.when(own)
        def _():
            wait_bytes(others, sem)

    home = q == p // 2
    sent(home, us, us.at[1:NP], u_send.at[0])
    sent(q % 2 == y // 2, us, us.at[1:NP], ur_send.at[0])
    sent(q // 2 == x, uq, uq.at[1:4], uq_send.at[0])
    sent(home, rgp, rgp.at[1:NP], g_send.at[0])
    wait_bytes(vr.at[z, x], vx_send.at[0])
    wait_bytes(vq.at[z, 1:4], vy_send.at[0])
    wait_bytes(vr.at[1:NZ], vr_send.at[0])
    wait_bytes(vq.at[1:NZ], vq_send.at[0])
    wait_bytes(xsr.at[:, 1:4], xr_send.at[0])
    wait_bytes(xsq, xq_send.at[0])
    for h in range(2):
        wait_bytes(zs.at[4 * h : 4 * h + 4, 1:NP], z_send.at[h])
    for h in range(2):
        wait_bytes(tbuf.at[h], t_send.at[h])


def shards(receiver_spectra, reference_spectra, receiver_counts, reference_counts, column_station, lag_window, observed):
    table = lag_table()
    m = jnp.asarray(table, dtype=BF)
    mt = jnp.asarray(np.ascontiguousarray(table.T), dtype=BF)
    vmem = pl.BlockSpec(memory_space=pltpu.VMEM)
    hbm = pl.BlockSpec(memory_space=pl.ANY)
    dma = pltpu.SemaphoreType.DMA
    return pl.pallas_call(
        kernel,
        out_shape=(
            pltpu.VMEM((NI, 2048), F32),
            pltpu.VMEM((128, NJ), F32),
        ),
        in_specs=[hbm] * 9,
        out_specs=(pl.BlockSpec(memory_space=pltpu.MemorySpace.VMEM), pl.BlockSpec(memory_space=pltpu.MemorySpace.VMEM)),
        scratch_shapes=[
            pltpu.VMEM((NI, 2048), BF),
            pltpu.VMEM((128, NJ), BF),
            pltpu.VMEM((1, NI), jnp.int32),
            pltpu.VMEM((1, NJ), jnp.int32),
            pltpu.VMEM((1, NJ), jnp.int32),
            pltpu.VMEM((2, NI, NJ), jnp.int32),
            pltpu.VMEM((2, NI, 1152), BF),
            pltpu.VMEM((NP, NI, 1152), BF),
            pltpu.VMEM((4, 2, NI, 1152), BF),
            pltpu.VMEM((4, 2, NI, 1152), BF),
            pltpu.VMEM((NZ, 2, 128, 128), BF),
            pltpu.VMEM((NZ, 4, 128, 128), BF),
            pltpu.VMEM((NZ, 4, 2, NI, 256), F32),
            pltpu.VMEM((NZ, 2, 2, 2, NI, 256), F32),
            pltpu.VMEM((4, NI, 16, 256), BF),
            pltpu.VMEM((4, NI, 16, 128), F32),
            pltpu.VMEM((2, NI, 16, 128), F32),
            pltpu.VMEM((NG, 4, 2, 128, 256), BF),
            pltpu.VMEM((NG, 2, 256, 512), BF),
            pltpu.VMEM((8, NJ), F32),
            pltpu.VMEM((8, NJ), F32),
            pltpu.VMEM((8, NJ), F32),
            pltpu.VMEM((NI, NJ, L), BF),
            pltpu.VMEM((2 * F, 2 * L), BF),
            pltpu.VMEM((2 * L, 2 * F), BF),
            pltpu.VMEM((2 * L, 2 * F), BF),
            pltpu.VMEM((2 * L, 2 * F), BF),
            pltpu.VMEM((8, L, NJ), BF),
            pltpu.VMEM((NZ, 4, 4, 16, NJ), BF),
            pltpu.VMEM((4, 4, NZ, 16, NJ), BF),
            pltpu.VMEM((NZ, 4, 2, 16, NJ), BF),
            pltpu.VMEM((4, 2, NZ, 2, 16, NJ), BF),
            pltpu.VMEM((2 * L, NJ), BF),
            pltpu.VMEM((8, NP, NG, 16, NJ), BF),
            pltpu.VMEM((NG, 8, NP, 16, NJ), BF),
            pltpu.VMEM((2, NZ, 128, 128), F32),
            pltpu.VMEM((2, 7, 128, 128), F32),
            pltpu.VMEM((NP, NI, 1024), F32),
            pltpu.VMEM((4, 2, NI, 1024), F32),
            dma((9,)), dma((1,)), dma((1,)), dma((1,)), dma((1,)), dma((1,)), dma((1,)),
            dma((1,)), dma((1,)), dma((1,)), dma((4,)), dma((1,)), dma((NZ, 2)), dma((1,)), dma((NZ, 4)),
            dma((1,)), dma((1,)), dma((1,)), dma((1,)), dma((2,)), dma((8,)),
            dma((1,)), dma((1,)), dma((2,)), dma((2, 7, 2)),
        ],
        compiler_params=pltpu.CompilerParams(
            collective_id=0, has_side_effects=True, vmem_limit_bytes=60 * 1024 * 1024
        ),
    )(
        receiver_spectra,
        reference_spectra,
        receiver_counts.reshape(1, NI),
        reference_counts.reshape(1, NJ),
        column_station.reshape(1, NJ),
        lag_window,
        observed,
        m,
        mt,
    )


def solution(mesh):
    return jax.shard_map(
        shards,
        mesh=mesh,
        in_specs=(
            P("rcv", "ref"), P("rcv", "ref"), P("rcv"), P("ref"), P("ref"),
            P(None, "rcv", "ref"), P("rcv", "ref", None),
        ),
        out_specs=(P("rcv", "ref"), P("rcv", "ref")),
        check_vma=False,
    )
```

```python
import math

import jax
import jax.numpy as jnp
import numpy as np
from jax import lax
from jax.experimental import pallas as pl
from jax.experimental.pallas import tpu as pltpu
from jax.sharding import PartitionSpec as P

L = 512
S = 16
F = 256
NP = 8
NZ = 8
NI = 8
NJ = 256
NG = 4
MESH = pl.DeviceIdType.MESH
BF = jnp.bfloat16
F32 = jnp.float32

env_floor = 0.05
misfit_scale = 0.03125


def lag_table():
    freq_ids = np.arange(F, dtype=np.int64)[:, None]
    lag_ids = np.arange(L, dtype=np.int64)[None, :] - L // 2
    angle = ((freq_ids * lag_ids) % L).astype(np.float64) * (2.0 * math.pi / L)
    cosine = np.cos(angle) / math.sqrt(F)
    sine = np.sin(angle) / math.sqrt(F)
    real_rows = np.concatenate([cosine, sine], axis=1)
    imag_rows = np.concatenate([-sine, cosine], axis=1)
    stacked = np.stack([real_rows, imag_rows], axis=1).reshape(2 * F, 2 * L)
    return stacked.astype(np.float32)


def kernel(
    u_hbm, v_hbm, rc_hbm, fc_hbm, cs_hbm, win_hbm, obs_hbm, m_hbm, mt_hbm,
    rg_out, wg_out,
    u_ref, v_ref, rc_ref, fc_ref, cs_ref, win_ref,
    um, us, ur, uq, vr, vq, ucr, ucq, bw, scr, scq, bt, bb, ninv, first, last,
    obs, m_ref, mt_ref, mq_ref, mr_ref, obst, xsr, xrr, xsq, xrq, gs, zs, zr,
    w, tbuf, rgp, rgr,
    in_sem, u_send, u_recv, ur_send, ur_recv, uq_send, uq_recv,
    vx_send, vx_recv, vy_send, vy_recv, vr_send, vr_recv, vq_send, vq_recv,
    xr_send, xr_recv, xq_send, xq_recv, z_send, z_recv,
    g_send, g_recv, t_send, t_recv,
):
    r = lax.axis_index("rcv")
    q = lax.axis_index("ref")
    p = r // NZ
    z = r % NZ
    x = p // 4
    y = p % 4
    right = p * NZ + (z + 1) % NZ
    left = p * NZ + (z + NZ - 1) % NZ
    partner = ((p + 4) % NP) * NZ + z

    def signal(rr, qq):
        pl.semaphore_signal(barrier, inc=1, device_id=(rr, qq), device_id_type=MESH)

    def remote(src, dst, send, recv, rr, qq):
        return pltpu.make_async_remote_copy(
            src_ref=src, dst_ref=dst, send_sem=send, recv_sem=recv,
            device_id=(rr, qq), device_id_type=MESH,
        )

    def plane(k):
        return ((p + k) % NP) * NZ + z

    def wait_bytes(ref, sem):
        pltpu.make_async_copy(ref, ref, sem).wait()

    small = ((u_hbm, u_ref), (v_hbm, v_ref), (rc_hbm, rc_ref), (fc_hbm, fc_ref), (cs_hbm, cs_ref), (win_hbm, win_ref))
    firsts = [pltpu.make_async_copy(src, dst, in_sem.at[3 + n]) for n, (src, dst) in enumerate(small)]
    for load in firsts:
        load.start()

    barrier = pltpu.get_barrier_semaphore()
    for k in range(NP):
        for dq in range(4):
            if k or dq:
                signal(plane(k), (q + dq) % 4)
    for k in (1, 2, 6, 7):
        signal(p * NZ + (z + k) % NZ, q)

    loads = [pltpu.make_async_copy(obs_hbm.at[i], obs.at[i], in_sem.at[0]) for i in range(NI)]
    loads.append(pltpu.make_async_copy(mt_hbm, mt_ref, in_sem.at[1]))
    loads.append(pltpu.make_async_copy(m_hbm, m_ref, in_sem.at[2]))
    for load in loads:
        load.start()

    for load in firsts:
        load.wait()

    eye = lax.broadcasted_iota(jnp.int32, (NI, NI), 0) == lax.broadcasted_iota(jnp.int32, (NI, NI), 1)
    rcounts = jnp.sum(jnp.where(eye, rc_ref[...].astype(F32), 0.0), axis=1, keepdims=True)
    pc = fc_ref[...].astype(F32)
    row_mask = (lax.broadcasted_iota(jnp.int32, (128, NJ), 0) % S).astype(F32) < pc
    mine = jnp.where(row_mask, v_ref[...].astype(F32), 0.0).astype(BF)
    vq[z, y] = mine[:, 0:128]
    vr[z, x] = mine[:, 128:256]
    seg_lane = (lax.broadcasted_iota(jnp.int32, (NI, 1024), 1) % S).astype(F32)
    keep = seg_lane < rcounts
    for half in range(2):
        part = u_ref[:, half * 1024 : (half + 1) * 1024].astype(F32)
        um[half, :, 0:1024] = jnp.where(keep, part, 0.0).astype(BF)
        um[half, :, 1024:1152] = jnp.broadcast_to(rcounts, (NI, 128)).astype(BF)

    pl.semaphore_wait(barrier, 4 * NP - 1 + 4)

    def give(own, src, dst, send, recv, rr, qq):
        @pl.when(jnp.logical_not(own))
        def _():
            remote(src, dst, send, recv, rr, qq).start()

        @pl.when(own)
        def _():
            pltpu.make_async_copy(src, dst, recv).start()

    def pass_on(buf, send, recv, zz, sub, to):
        remote(buf.at[zz, sub], buf.at[zz, sub], send.at[0], recv.at[zz, sub], to, q).start()

    def pass_r(zz, sub, to):
        pass_on(vr, vr_send, vr_recv, zz, sub, to)

    def pass_q(zz, sub, to):
        pass_on(vq, vq_send, vq_recv, zz, sub, to)

    remote(vr.at[z, x], vr.at[z, x], vx_send.at[0], vx_recv.at[0], partner, q).start()
    for k in range(1, 4):
        remote(
            vq.at[z, y], vq.at[z, y], vy_send.at[0], vy_recv.at[y], (x * 4 + (y + k) % 4) * NZ + z, q
        ).start()
    pass_r(z, x, right)
    pass_r(z, x, left)
    pass_q(z, y, right)
    pass_q(z, y, left)
    for half in range(2):
        for qq in range(4):
            yd = 2 * (q % 2) + half
            own = jnp.logical_and(yd == y, qq == q)
            give(
                own, um.at[half], ur.at[(y - yd + 4) % 4, q // 2], ur_send.at[0], ur_recv.at[0],
                (x * 4 + yd) * NZ + z, qq,
            )
    for qq in range(4):
        xd = q // 2
        own = jnp.logical_and(xd == x, qq == q)
        give(
            own, um, uq.at[2 * ((x - xd + 2) % 2) + q % 2], uq_send.at[0], uq_recv.at[0],
            (xd * 4 + y) * NZ + z, qq,
        )
    order = cs_ref[...] - q * NJ
    stations = lax.broadcasted_iota(jnp.int32, (NJ, NJ), 0)
    onehot = jnp.where(stations == order, 1.0, 0.0).astype(BF)
    nt = (((1,), (1,)), ((), ()))
    begin = lax.dot_general(win_ref[0].astype(F32).astype(BF), onehot, nt, preferred_element_type=F32)
    span = lax.dot_general(win_ref[1].astype(F32).astype(BF), onehot, nt, preferred_element_type=F32)
    inv = 1.0 / jnp.minimum(rcounts, pc)
    for h in range(2):
        for i in range(NI):
            u, lanes, side = 4 * h + i // 2, pl.ds((i % 2) * 128, 128), slice(h * 128, (h + 1) * 128)
            first[u : u + 1, lanes] = begin[i : i + 1, side]
            last[u : u + 1, lanes] = begin[i : i + 1, side] + span[i : i + 1, side]
            ninv[u : u + 1, lanes] = inv[i : i + 1, side]
    def turn(ii, c):
        for par in range(2):
            seen = jnp.dot(onehot, obs[2 * ii + par], preferred_element_type=F32)
            seen = jnp.transpose(seen, (1, 0)).astype(BF)
            for h in range(2):
                obst[4 * h + ii, :, par * 128 : (par + 1) * 128] = seen[:, h * 128 : (h + 1) * 128]
        return c

    wait_bytes(obs, in_sem.at[0])
    lax.fori_loop(0, 2, turn, 0)

    wait_bytes(vr.at[z, 1 - x], vx_recv.at[0])
    pass_r(z, 1 - x, right)
    pass_r(z, 1 - x, left)
    for k in (1, 3, 2):
        yy = (y + k) % 4
        wait_bytes(vq.at[z, yy], vy_recv.at[yy])
        pass_q(z, yy, right)
        pass_q(z, yy, left)
    for half in range(2):
        for qq in range(4):
            pp = 2 * q + half
            rr = pp * NZ + z
            own = jnp.logical_and(rr == r, qq == q)
            slot = (p - pp + NP) % NP
            give(own, um.at[half], us.at[slot], u_send.at[0], u_recv.at[0], rr, qq)

    def back(s):
        return (z + NZ - s) % NZ

    def ahead(s):
        return (z + s) % NZ

    def step(s, buf, recv, pass_to, sub, up):
        if s <= up:
            wait_bytes(buf.at[back(s), sub], recv.at[back(s), sub])
            if s < up:
                pass_to(back(s), sub, right)
        if s <= 7 - up:
            wait_bytes(buf.at[ahead(s), sub], recv.at[ahead(s), sub])
            if s < 7 - up:
                pass_to(ahead(s), sub, left)

    def step_r(s):
        for k in range(2):
            step(s, vr, vr_recv, pass_r, (x + k) % 2, 4 - k)

    def step_q(s):
        for k in (0, 1, 3, 2):
            step(s, vq, vq_recv, pass_q, (y + k) % 4, 4 if k < 2 else 3)

    row16 = lax.broadcasted_iota(jnp.int32, (16, 256), 0)
    lane256 = lax.broadcasted_iota(jnp.int32, (16, 256), 1)
    diag = (lane256 // 32) == (row16 // 2)
    mask0 = jnp.logical_and(diag, row16 % 2 == 0)
    mask1 = jnp.logical_and(diag, row16 % 2 == 1)

    def turned(uf):
        part = (lax.broadcasted_iota(jnp.int32, (NI, 1024), 1) // S) % 2
        return jnp.where(part == 0, pltpu.roll(uf, 1024 - S, 1), -pltpu.roll(uf, S, 1))

    def blocks(a, b, out):
        for i in range(NI):
            out(i, jnp.where(mask0, a[i : i + 1], jnp.where(mask1, b[i : i + 1], 0.0)).astype(BF))

    def ready_r(yk, c):
        for xx in range(2):
            uf = ur[yk, xx, :, 0:1024].astype(F32)
            ut = turned(uf)
            for zz in range(NZ):
                ucr[zz, yk, 0, :, xx * 128 : (xx + 1) * 128] = uf[:, zz * 128 : (zz + 1) * 128]
                ucr[zz, yk, 1, :, xx * 128 : (xx + 1) * 128] = ut[:, zz * 128 : (zz + 1) * 128]
        inverse = 1.0 / jnp.minimum(ur[yk, 0, :, 1024:1025].astype(F32), pc[:, 128:256])
        for i in range(NI):
            scr[yk, i] = jnp.broadcast_to(inverse[i : i + 1], (16, 128))
        return c

    def ready_q(xk, c):
        for b in range(2):
            for half in range(2):
                uf = uq[2 * xk + b, half, :, 0:1024].astype(F32)
                ut = turned(uf)
                for zz in range(NZ):
                    ucq[zz, xk, b, 0, :, half * 128 : (half + 1) * 128] = uf[:, zz * 128 : (zz + 1) * 128]
                    ucq[zz, xk, b, 1, :, half * 128 : (half + 1) * 128] = ut[:, zz * 128 : (zz + 1) * 128]
        inverse = 1.0 / jnp.minimum(uq[2 * xk, 0, :, 1024:1025].astype(F32), pc[:, 0:128])
        for i in range(NI):
            scq[xk, i] = jnp.broadcast_to(inverse[i : i + 1], (16, 128))
        return c

    def cross_r(zz):
        for yk in range(4):
            def put(i, blk):
                bw[yk, i] = blk

            blocks(ucr[zz, yk, 0], ucr[zz, yk, 1], put)
        v = jnp.dot(bw[...].reshape(512, 256), vr[zz].reshape(256, 128), preferred_element_type=F32)
        v = (v * scr[...].reshape(512, 128)).astype(BF)
        for yk in range(4):
            for i in range(NI):
                rows = v[(yk * NI + i) * 16 : (yk * NI + i + 1) * 16]
                lanes = slice((i % 2) * 128, (i % 2 + 1) * 128)
                if yk:
                    xsr[zz, yk, i // 2, :, lanes] = rows
                else:
                    xrr[i // 2, y, zz, :, lanes] = rows
        for yk in range(1, 4):
            remote(
                xsr.at[zz, yk], xrr.at[:, y, zz], xr_send.at[0], xr_recv.at[0],
                (x * 4 + (y + yk) % 4) * NZ + z, q,
            ).start()

    def cross_q(zz):
        for b in range(2):
            for xk in range(2):
                def put(i, blk):
                    bw[2 * b + xk, i] = blk

                blocks(ucq[zz, xk, b, 0], ucq[zz, xk, b, 1], put)
        for b in range(2):
            v = jnp.dot(
                bw[2 * b : 2 * b + 2].reshape(256, 256), vq[zz, 2 * b : 2 * b + 2].reshape(256, 128),
                preferred_element_type=F32,
            )
            v = (v * scq[...].reshape(256, 128)).astype(BF)
            for xk in range(2):
                for i in range(NI):
                    rows = v[(xk * NI + i) * 16 : (xk * NI + i + 1) * 16]
                    lanes = slice((i % 2) * 128, (i % 2 + 1) * 128)
                    if xk:
                        xsq[zz, i // 2, b, :, lanes] = rows
                    else:
                        xrq[i // 2, x, zz, b, :, lanes] = rows
        remote(xsq.at[zz], xrq.at[:, x, zz], xq_send.at[0], xq_recv.at[0], partner, q).start()

    def crossings(cross, start, end):
        def one(j, c):
            cross((z + NZ + ((j + 1) // 2) * (2 * (j % 2) - 1)) % NZ)
            return c

        lax.fori_loop(start, end, one, 0)

    lax.fori_loop(2, 4, turn, 0)
    step_r(1)
    wait_bytes(ur, ur_recv.at[0])
    lax.fori_loop(0, 4, ready_r, 0)
    crossings(cross_r, 0, 3)
    step_r(2)
    crossings(cross_r, 3, 5)
    step_q(1)
    wait_bytes(uq, uq_recv.at[0])
    lax.fori_loop(0, 2, ready_q, 0)
    crossings(cross_q, 0, 3)
    step_r(3)
    crossings(cross_r, 5, 7)
    step_q(2)
    crossings(cross_q, 3, 5)

    here = lax.broadcasted_iota(jnp.int32, (2 * F, 2 * F), 0)
    n = lax.broadcasted_iota(jnp.int32, (2 * F, 2 * F), 1)
    from_r = n % 8 + 8 * ((n // 16) % 8) + 64 * (n // 128) + 256 * ((n // 8) % 2)
    from_q = n % 8 + 8 * ((n // 32) % 8) + 64 * ((n // 8) % 4) + 256 * (n // 256)

    def reorder(source, out):
        pick = jnp.where(here == source, 1.0, 0.0).astype(BF)
        for b in range(4):
            rows = slice(b * 256, (b + 1) * 256)
            out[rows, :] = jnp.dot(mt_ref[rows, :], pick, preferred_element_type=F32).astype(BF)

    for load in loads[NI:]:
        load.wait()
    reorder(from_r, mr_ref)
    step_r(4)
    crossings(cross_r, 7, 8)
    step_q(3)
    crossings(cross_q, 5, 7)
    reorder(from_q, mq_ref)
    step_q(4)
    crossings(cross_q, 7, 8)

    TB = 128
    def pairs(u, got, table):
        lo = first[pl.ds(u, 1), :]
        hi = last[pl.ds(u, 1), :]
        for b in range(L // TB):
            cor = jnp.dot(table[b * TB : (b + 1) * TB, :], got, preferred_element_type=F32)
            hil = jnp.dot(table[L + b * TB : L + (b + 1) * TB, :], got, preferred_element_type=F32)
            rs = lax.rsqrt(cor * cor + hil * hil + env_floor)
            lag = (lax.broadcasted_iota(jnp.int32, (TB, NJ), 0) + b * TB).astype(F32)
            inside = jnp.logical_and(lag >= lo, lag < hi)
            seen = obst[u, b * TB : (b + 1) * TB, :].astype(F32)
            wt = jnp.where(inside, (1.0 - seen * rs) * misfit_scale, 0.0)
            gs[b * TB : (b + 1) * TB, :] = (wt * cor).astype(BF)
            gs[L + b * TB : L + (b + 1) * TB, :] = (wt * hil).astype(BF)
        scale = ninv[pl.ds(u, 1), :]
        for b in range(4):
            back = jnp.dot(m_ref[b * 128 : (b + 1) * 128, :], gs[...], preferred_element_type=F32)
            zs[u, 2 * b : 2 * b + 2] = (back * scale).astype(BF).reshape(2, NG, 16, NJ)
        for k in range(1, NP):
            remote(
                zs.at[u, (p + k) % NP], zr.at[:, u, NP - k], z_send.at[u // 4], z_recv.at[u], plane(k), q
            ).start()
        zr[:, u, 0] = zs[u, p]

    def pairs_r(ii, c):
        pairs(4 + ii, xrr[ii].reshape(2 * F, NJ), mr_ref)
        return c

    def pairs_q(ii, c):
        pairs(ii, xrq[ii].reshape(2 * F, NJ), mq_ref)
        return c

    wait_bytes(xsr.at[:, 1:4], xr_recv.at[0])
    lax.fori_loop(0, 4, pairs_r, 0)
    wait_bytes(xsq, xq_recv.at[0])
    lax.fori_loop(0, 4, pairs_q, 0)

    def operand(k, c):
        uf = us[k, :, 0:1024].astype(F32)
        ut = turned(uf)
        for g in range(NG):
            def put(i, blk):
                bt[g, i // 2, i % 2, pl.ds(k * 16, 16), :] = blk

            blocks(uf[:, g * 256 : (g + 1) * 256], ut[:, g * 256 : (g + 1) * 256], put)
        return c

    wait_bytes(us, u_recv.at[0])
    lax.fori_loop(0, NP, operand, 0)

    def flip(g, c):
        for ii in range(4):
            for par in range(2):
                bb[g, par, :, ii * 128 : (ii + 1) * 128] = jnp.transpose(
                    bt[g, ii, par].astype(F32), (1, 0)
                ).astype(BF)
        return c

    lax.fori_loop(0, NG, flip, 0)

    def arrived(u):
        wait_bytes(zs.at[u, 1:NP], z_recv.at[u])

    def sums(h, start, end):
        size = (end - start) * 128
        for g in range(NG):
            part = None
            for par in range(2):
                got = zr[g, 4 * h + start : 4 * h + end, :, :, par * 128 : (par + 1) * 128].reshape(size, 128)
                one = jnp.dot(bb[g, par, :, start * 128 : end * 128], got, preferred_element_type=F32)
                part = one if part is None else part + one
            part = part.reshape(2, 128, 128)
            if start:
                part = part + w[h, 2 * g : 2 * g + 2]
            w[h, 2 * g : 2 * g + 2] = part

    def toward(n, src, h, part, to):
        rows = slice(part * 64, (part + 1) * 64)
        remote(
            src.at[rows], tbuf.at[h, n, rows], t_send.at[h], t_recv.at[h, n, part],
            p * NZ + (z + NZ + to) % NZ, q,
        ).start()

    def landed(n, h, part):
        wait_bytes(tbuf.at[h, n, part * 64 : (part + 1) * 64], t_recv.at[h, n, part])

    def tree_start(h):
        for part in range(2):
            for n, m, to in ((0, 4, 2), (2, 5, -1), (1, 3, 1)):
                toward(n, w.at[h, (z + m) % NZ], h, part, to)
        for part in range(2):
            for n, m, to in ((3, 1, 1), (4, 7, -1)):
                toward(n, w.at[h, (z + m) % NZ], h, part, to)

    def tree_middle(h):
        for part in range(2):
            rows = slice(part * 64, (part + 1) * 64)
            landed(2, h, part)
            tbuf[h, 2, rows] = tbuf[h, 2, rows] + w[h, (z + 6) % NZ, rows]
            toward(6, tbuf.at[h, 2], h, part, -2)
            landed(1, h, part)
            landed(0, h, part)
            tbuf[h, 0, rows] = tbuf[h, 0, rows] + (tbuf[h, 1, rows] + w[h, (z + 2) % NZ, rows])
            toward(5, tbuf.at[h, 0], h, part, 2)

    def tree_end(h):
        for n in (3, 4, 6, 5):
            for part in range(2):
                landed(n, h, part)
        done = (w[h, z] + tbuf[h, 3]) + (tbuf[h, 4] + tbuf[h, 6]) + tbuf[h, 5]
        cols = slice(h * 128, (h + 1) * 128)
        wg_out[:, cols] = jnp.where(row_mask[:, cols], done, 0.0)

    lane8 = (lax.broadcasted_iota(jnp.int32, (NP, 256), 1) // S) % 2

    def receivers(ii):
        for g in range(NG):
            for par in range(2):
                t = None
                for h in range(2):
                    got = zr[g, 4 * h + ii, :, :, par * 128 : (par + 1) * 128].reshape(128, 128)
                    held = vr[2 * g : 2 * g + 2, x] if h else vq[2 * g : 2 * g + 2, y]
                    block = held.reshape(256, 128)
                    part = lax.dot_general(got, block, nt, preferred_element_type=F32)
                    t = part if t is None else t + part
                t = t.reshape(NP, 16, 256)
                a0 = jnp.sum(jnp.where(mask0[None], t, 0.0), axis=1)
                a1 = jnp.sum(jnp.where(mask1[None], t, 0.0), axis=1)
                rg = a0 + jnp.where(lane8 == 0, -pltpu.roll(a1, 256 - S, 1), pltpu.roll(a1, S, 1))
                i = 2 * ii + par
                for k in range(NP):
                    rgp[k, i : i + 1, g * 256 : (g + 1) * 256] = rg[k : k + 1]

    for u in range(4, 8):
        arrived(u)
    sums(1, 0, 4)
    tree_start(1)
    arrived(0)
    receivers(0)
    tree_middle(1)
    arrived(1)
    receivers(1)
    arrived(2)
    receivers(2)
    sums(0, 0, 3)
    arrived(3)
    sums(0, 3, 4)
    tree_start(0)
    receivers(3)
    for k in range(NP):
        own = jnp.logical_and(k == 0, p // 2 == q)

        @pl.when(jnp.logical_not(own))
        def _():
            remote(rgp.at[k], rgr.at[q, p % 2], g_send.at[0], g_recv.at[0], plane(k), p // 2).start()

        @pl.when(own)
        def _():
            pltpu.make_async_copy(rgp.at[k], rgr.at[q, p % 2], g_recv.at[0]).start()

    tree_end(1)
    tree_middle(0)
    wait_bytes(rgr, g_recv.at[0])
    for half in range(2):
        total = (rgr[0, half] + rgr[1, half]) + (rgr[2, half] + rgr[3, half])
        rg_out[:, half * 1024 : (half + 1) * 1024] = jnp.where(keep, total, 0.0)
    tree_end(0)

    def sent(own, every, others, sem):
        @pl.when(jnp.logical_not(own))
        def _():
            wait_bytes(every, sem)

        @pl.when(own)
        def _():
            wait_bytes(others, sem)

    home = q == p // 2
    sent(home, us, us.at[1:NP], u_send.at[0])
    sent(q % 2 == y // 2, us, us.at[1:NP], ur_send.at[0])
    sent(q // 2 == x, uq, uq.at[1:4], uq_send.at[0])
    sent(home, rgp, rgp.at[1:NP], g_send.at[0])
    wait_bytes(vr.at[z, x], vx_send.at[0])
    wait_bytes(vq.at[z, 1:4], vy_send.at[0])
    wait_bytes(vr.at[1:NZ], vr_send.at[0])
    wait_bytes(vq.at[1:NZ], vq_send.at[0])
    wait_bytes(xsr.at[:, 1:4], xr_send.at[0])
    wait_bytes(xsq, xq_send.at[0])
    for h in range(2):
        wait_bytes(zs.at[4 * h : 4 * h + 4, 1:NP], z_send.at[h])
    for h in range(2):
        wait_bytes(tbuf.at[h], t_send.at[h])


def shards(receiver_spectra, reference_spectra, receiver_counts, reference_counts, column_station, lag_window, observed):
    table = lag_table()
    m = jnp.asarray(table, dtype=BF)
    mt = jnp.asarray(np.ascontiguousarray(table.T), dtype=BF)
    vmem = pl.BlockSpec(memory_space=pltpu.VMEM)
    hbm = pl.BlockSpec(memory_space=pl.ANY)
    dma = pltpu.SemaphoreType.DMA
    return pl.pallas_call(
        kernel,
        out_shape=(
            pltpu.VMEM((NI, 2048), F32),
            pltpu.VMEM((128, NJ), F32),
        ),
        in_specs=[hbm] * 9,
        out_specs=(pl.BlockSpec(memory_space=pltpu.MemorySpace.VMEM), pl.BlockSpec(memory_space=pltpu.MemorySpace.VMEM)),
        scratch_shapes=[
            pltpu.VMEM((NI, 2048), BF),
            pltpu.VMEM((128, NJ), BF),
            pltpu.VMEM((1, NI), jnp.int32),
            pltpu.VMEM((1, NJ), jnp.int32),
            pltpu.VMEM((1, NJ), jnp.int32),
            pltpu.VMEM((2, NI, NJ), jnp.int32),
            pltpu.VMEM((2, NI, 1152), BF),
            pltpu.VMEM((NP, NI, 1152), BF),
            pltpu.VMEM((4, 2, NI, 1152), BF),
            pltpu.VMEM((4, 2, NI, 1152), BF),
            pltpu.VMEM((NZ, 2, 128, 128), BF),
            pltpu.VMEM((NZ, 4, 128, 128), BF),
            pltpu.VMEM((NZ, 4, 2, NI, 256), F32),
            pltpu.VMEM((NZ, 2, 2, 2, NI, 256), F32),
            pltpu.VMEM((4, NI, 16, 256), BF),
            pltpu.VMEM((4, NI, 16, 128), F32),
            pltpu.VMEM((2, NI, 16, 128), F32),
            pltpu.VMEM((NG, 4, 2, 128, 256), BF),
            pltpu.VMEM((NG, 2, 256, 512), BF),
            pltpu.VMEM((8, NJ), F32),
            pltpu.VMEM((8, NJ), F32),
            pltpu.VMEM((8, NJ), F32),
            pltpu.VMEM((NI, NJ, L), BF),
            pltpu.VMEM((2 * F, 2 * L), BF),
            pltpu.VMEM((2 * L, 2 * F), BF),
            pltpu.VMEM((2 * L, 2 * F), BF),
            pltpu.VMEM((2 * L, 2 * F), BF),
            pltpu.VMEM((8, L, NJ), BF),
            pltpu.VMEM((NZ, 4, 4, 16, NJ), BF),
            pltpu.VMEM((4, 4, NZ, 16, NJ), BF),
            pltpu.VMEM((NZ, 4, 2, 16, NJ), BF),
            pltpu.VMEM((4, 2, NZ, 2, 16, NJ), BF),
            pltpu.VMEM((2 * L, NJ), BF),
            pltpu.VMEM((8, NP, NG, 16, NJ), BF),
            pltpu.VMEM((NG, 8, NP, 16, NJ), BF),
            pltpu.VMEM((2, NZ, 128, 128), F32),
            pltpu.VMEM((2, 7, 128, 128), F32),
            pltpu.VMEM((NP, NI, 1024), F32),
            pltpu.VMEM((4, 2, NI, 1024), F32),
            dma((9,)), dma((1,)), dma((1,)), dma((1,)), dma((1,)), dma((1,)), dma((1,)),
            dma((1,)), dma((1,)), dma((1,)), dma((4,)), dma((1,)), dma((NZ, 2)), dma((1,)), dma((NZ, 4)),
            dma((1,)), dma((1,)), dma((1,)), dma((1,)), dma((2,)), dma((8,)),
            dma((1,)), dma((1,)), dma((2,)), dma((2, 7, 2)),
        ],
        compiler_params=pltpu.CompilerParams(
            collective_id=0, has_side_effects=True, vmem_limit_bytes=60 * 1024 * 1024
        ),
    )(
        receiver_spectra,
        reference_spectra,
        receiver_counts.reshape(1, NI),
        reference_counts.reshape(1, NJ),
        column_station.reshape(1, NJ),
        lag_window,
        observed,
        m,
        mt,
    )


def solution(mesh):
    return jax.shard_map(
        shards,
        mesh=mesh,
        in_specs=(
            P("rcv", "ref"), P("rcv", "ref"), P("rcv"), P("ref"), P("ref"),
            P(None, "rcv", "ref"), P("rcv", "ref", None),
        ),
        out_specs=(P("rcv", "ref"), P("rcv", "ref")),
        check_vma=False,
    )
```

```python
import math

import jax
import jax.numpy as jnp
import numpy as np
from jax import lax
from jax.experimental import pallas as pl
from jax.experimental.pallas import tpu as pltpu
from jax.sharding import PartitionSpec as P

L = 512
S = 16
F = 256
NP = 8
NZ = 8
NI = 8
NJ = 256
NG = 4
MESH = pl.DeviceIdType.MESH
BF = jnp.bfloat16
F32 = jnp.float32

env_floor = 0.05
misfit_scale = 0.03125


def lag_table():
    freq_ids = np.arange(F, dtype=np.int64)[:, None]
    lag_ids = np.arange(L, dtype=np.int64)[None, :] - L // 2
    angle = ((freq_ids * lag_ids) % L).astype(np.float64) * (2.0 * math.pi / L)
    cosine = np.cos(angle) / math.sqrt(F)
    sine = np.sin(angle) / math.sqrt(F)
    real_rows = np.concatenate([cosine, sine], axis=1)
    imag_rows = np.concatenate([-sine, cosine], axis=1)
    stacked = np.stack([real_rows, imag_rows], axis=1).reshape(2 * F, 2 * L)
    return stacked.astype(np.float32)


def kernel(
    u_hbm, v_hbm, rc_hbm, fc_hbm, cs_hbm, win_hbm, obs_hbm, m_hbm, mt_hbm,
    rg_out, wg_out,
    u_ref, v_ref, rc_ref, fc_ref, cs_ref, win_ref,
    um, us, ur, uq, vr, vq, ucr, ucq, bw, scr, scq, bt, bb, ninv, first, last,
    obs, m_ref, mt_ref, mq_ref, mr_ref, obst, xsr, xrr, xsq, xrq, gs, zs, zr,
    w, tbuf, rgp, rgr,
    in_sem, u_send, u_recv, ur_send, ur_recv, uq_send, uq_recv,
    vx_send, vx_recv, vy_send, vy_recv, vr_send, vr_recv, vq_send, vq_recv,
    xr_send, xr_recv, xq_send, xq_recv, z_send, z_recv,
    g_send, g_recv, t_send, t_recv,
):
    r = lax.axis_index("rcv")
    q = lax.axis_index("ref")
    p = r // NZ
    z = r % NZ
    x = p // 4
    y = p % 4
    right = p * NZ + (z + 1) % NZ
    left = p * NZ + (z + NZ - 1) % NZ
    partner = ((p + 4) % NP) * NZ + z

    def signal(rr, qq):
        pl.semaphore_signal(barrier, inc=1, device_id=(rr, qq), device_id_type=MESH)

    def remote(src, dst, send, recv, rr, qq):
        return pltpu.make_async_remote_copy(
            src_ref=src, dst_ref=dst, send_sem=send, recv_sem=recv,
            device_id=(rr, qq), device_id_type=MESH,
        )

    def plane(k):
        return ((p + k) % NP) * NZ + z

    def wait_bytes(ref, sem):
        pltpu.make_async_copy(ref, ref, sem).wait()

    small = ((u_hbm, u_ref), (v_hbm, v_ref), (rc_hbm, rc_ref), (fc_hbm, fc_ref), (cs_hbm, cs_ref), (win_hbm, win_ref))
    firsts = [pltpu.make_async_copy(src, dst, in_sem.at[3 + n]) for n, (src, dst) in enumerate(small)]
    for load in firsts:
        load.start()

    barrier = pltpu.get_barrier_semaphore()
    for k in range(NP):
        for dq in range(4):
            if k or dq:
                signal(plane(k), (q + dq) % 4)
    for k in (1, 2, 6, 7):
        signal(p * NZ + (z + k) % NZ, q)

    loads = [pltpu.make_async_copy(obs_hbm.at[i], obs.at[i], in_sem.at[0]) for i in range(NI)]
    loads.append(pltpu.make_async_copy(mt_hbm, mt_ref, in_sem.at[1]))
    loads.append(pltpu.make_async_copy(m_hbm, m_ref, in_sem.at[2]))
    for load in loads:
        load.start()

    for load in firsts:
        load.wait()

    eye = lax.broadcasted_iota(jnp.int32, (NI, NI), 0) == lax.broadcasted_iota(jnp.int32, (NI, NI), 1)
    rcounts = jnp.sum(jnp.where(eye, rc_ref[...].astype(F32), 0.0), axis=1, keepdims=True)
    pc = fc_ref[...].astype(F32)
    row_mask = (lax.broadcasted_iota(jnp.int32, (128, NJ), 0) % S).astype(F32) < pc
    mine = jnp.where(row_mask, v_ref[...].astype(F32), 0.0).astype(BF)
    vq[z, y] = mine[:, 0:128]
    vr[z, x] = mine[:, 128:256]
    seg_lane = (lax.broadcasted_iota(jnp.int32, (NI, 1024), 1) % S).astype(F32)
    keep = seg_lane < rcounts
    for half in range(2):
        part = u_ref[:, half * 1024 : (half + 1) * 1024].astype(F32)
        um[half, :, 0:1024] = jnp.where(keep, part, 0.0).astype(BF)
        um[half, :, 1024:1152] = jnp.broadcast_to(rcounts, (NI, 128)).astype(BF)

    pl.semaphore_wait(barrier, 4 * NP - 1 + 4)

    def give(own, src, dst, send, recv, rr, qq):
        @pl.when(jnp.logical_not(own))
        def _():
            remote(src, dst, send, recv, rr, qq).start()

        @pl.when(own)
        def _():
            pltpu.make_async_copy(src, dst, recv).start()

    def pass_on(buf, send, recv, zz, sub, to):
        remote(buf.at[zz, sub], buf.at[zz, sub], send.at[0], recv.at[zz, sub], to, q).start()

    def pass_r(zz, sub, to):
        pass_on(vr, vr_send, vr_recv, zz, sub, to)

    def pass_q(zz, sub, to):
        pass_on(vq, vq_send, vq_recv, zz, sub, to)

    remote(vr.at[z, x], vr.at[z, x], vx_send.at[0], vx_recv.at[0], partner, q).start()
    for k in range(1, 4):
        remote(
            vq.at[z, y], vq.at[z, y], vy_send.at[0], vy_recv.at[y], (x * 4 + (y + k) % 4) * NZ + z, q
        ).start()
    pass_r(z, x, right)
    pass_r(z, x, left)
    pass_q(z, y, right)
    pass_q(z, y, left)
    for half in range(2):
        for qq in range(4):
            yd = 2 * (q % 2) + half
            own = jnp.logical_and(yd == y, qq == q)
            give(
                own, um.at[half], ur.at[(y - yd + 4) % 4, q // 2], ur_send.at[0], ur_recv.at[0],
                (x * 4 + yd) * NZ + z, qq,
            )
    for qq in range(4):
        xd = q // 2
        own = jnp.logical_and(xd == x, qq == q)
        give(
            own, um, uq.at[2 * ((x - xd + 2) % 2) + q % 2], uq_send.at[0], uq_recv.at[0],
            (xd * 4 + y) * NZ + z, qq,
        )
    order = cs_ref[...] - q * NJ
    stations = lax.broadcasted_iota(jnp.int32, (NJ, NJ), 0)
    onehot = jnp.where(stations == order, 1.0, 0.0).astype(BF)
    nt = (((1,), (1,)), ((), ()))
    begin = lax.dot_general(win_ref[0].astype(F32).astype(BF), onehot, nt, preferred_element_type=F32)
    span = lax.dot_general(win_ref[1].astype(F32).astype(BF), onehot, nt, preferred_element_type=F32)
    inv = 1.0 / jnp.minimum(rcounts, pc)
    for h in range(2):
        for i in range(NI):
            u, lanes, side = 4 * h + i // 2, pl.ds((i % 2) * 128, 128), slice(h * 128, (h + 1) * 128)
            first[u : u + 1, lanes] = begin[i : i + 1, side]
            last[u : u + 1, lanes] = begin[i : i + 1, side] + span[i : i + 1, side]
            ninv[u : u + 1, lanes] = inv[i : i + 1, side]
    def turn(ii, c):
        for par in range(2):
            seen = jnp.dot(onehot, obs[2 * ii + par], preferred_element_type=F32)
            seen = jnp.transpose(seen, (1, 0)).astype(BF)
            for h in range(2):
                obst[4 * h + ii, :, par * 128 : (par + 1) * 128] = seen[:, h * 128 : (h + 1) * 128]
        return c

    wait_bytes(obs, in_sem.at[0])
    lax.fori_loop(0, 2, turn, 0)

    wait_bytes(vr.at[z, 1 - x], vx_recv.at[0])
    pass_r(z, 1 - x, right)
    pass_r(z, 1 - x, left)
    for k in (1, 3, 2):
        yy = (y + k) % 4
        wait_bytes(vq.at[z, yy], vy_recv.at[yy])
        pass_q(z, yy, right)
        pass_q(z, yy, left)
    def back(s):
        return (z + NZ - s) % NZ

    def ahead(s):
        return (z + s) % NZ

    def step(s, buf, recv, pass_to, sub, up):
        if s <= up:
            wait_bytes(buf.at[back(s), sub], recv.at[back(s), sub])
            if s < up:
                pass_to(back(s), sub, right)
        if s <= 7 - up:
            wait_bytes(buf.at[ahead(s), sub], recv.at[ahead(s), sub])
            if s < 7 - up:
                pass_to(ahead(s), sub, left)

    def step_r(s):
        for k in range(2):
            step(s, vr, vr_recv, pass_r, (x + k) % 2, 4 - k)

    def step_q(s):
        for k in (0, 1, 3, 2):
            step(s, vq, vq_recv, pass_q, (y + k) % 4, 4 if k < 2 else 3)

    row16 = lax.broadcasted_iota(jnp.int32, (16, 256), 0)
    lane256 = lax.broadcasted_iota(jnp.int32, (16, 256), 1)
    diag = (lane256 // 32) == (row16 // 2)
    mask0 = jnp.logical_and(diag, row16 % 2 == 0)
    mask1 = jnp.logical_and(diag, row16 % 2 == 1)

    def turned(uf):
        part = (lax.broadcasted_iota(jnp.int32, (NI, 1024), 1) // S) % 2
        return jnp.where(part == 0, pltpu.roll(uf, 1024 - S, 1), -pltpu.roll(uf, S, 1))

    def blocks(a, b, out):
        for i in range(NI):
            out(i, jnp.where(mask0, a[i : i + 1], jnp.where(mask1, b[i : i + 1], 0.0)).astype(BF))

    def ready_r(yk, c):
        for xx in range(2):
            uf = ur[yk, xx, :, 0:1024].astype(F32)
            ut = turned(uf)
            for zz in range(NZ):
                ucr[zz, yk, 0, :, xx * 128 : (xx + 1) * 128] = uf[:, zz * 128 : (zz + 1) * 128]
                ucr[zz, yk, 1, :, xx * 128 : (xx + 1) * 128] = ut[:, zz * 128 : (zz + 1) * 128]
        inverse = 1.0 / jnp.minimum(ur[yk, 0, :, 1024:1025].astype(F32), pc[:, 128:256])
        for i in range(NI):
            scr[yk, i] = jnp.broadcast_to(inverse[i : i + 1], (16, 128))
        return c

    def ready_q(xk, c):
        for b in range(2):
            for half in range(2):
                uf = uq[2 * xk + b, half, :, 0:1024].astype(F32)
                ut = turned(uf)
                for zz in range(NZ):
                    ucq[zz, xk, b, 0, :, half * 128 : (half + 1) * 128] = uf[:, zz * 128 : (zz + 1) * 128]
                    ucq[zz, xk, b, 1, :, half * 128 : (half + 1) * 128] = ut[:, zz * 128 : (zz + 1) * 128]
        inverse = 1.0 / jnp.minimum(uq[2 * xk, 0, :, 1024:1025].astype(F32), pc[:, 0:128])
        for i in range(NI):
            scq[xk, i] = jnp.broadcast_to(inverse[i : i + 1], (16, 128))
        return c

    def cross_r(zz):
        for yk in range(4):
            def put(i, blk):
                bw[yk, i] = blk

            blocks(ucr[zz, yk, 0], ucr[zz, yk, 1], put)
        v = jnp.dot(bw[...].reshape(512, 256), vr[zz].reshape(256, 128), preferred_element_type=F32)
        v = (v * scr[...].reshape(512, 128)).astype(BF)
        for yk in range(4):
            for i in range(NI):
                rows = v[(yk * NI + i) * 16 : (yk * NI + i + 1) * 16]
                lanes = slice((i % 2) * 128, (i % 2 + 1) * 128)
                if yk:
                    xsr[zz, yk, i // 2, :, lanes] = rows
                else:
                    xrr[i // 2, y, zz, :, lanes] = rows
        for yk in range(1, 4):
            remote(
                xsr.at[zz, yk], xrr.at[:, y, zz], xr_send.at[0], xr_recv.at[0],
                (x * 4 + (y + yk) % 4) * NZ + z, q,
            ).start()

    def cross_q(zz):
        for b in range(2):
            for xk in range(2):
                def put(i, blk):
                    bw[2 * b + xk, i] = blk

                blocks(ucq[zz, xk, b, 0], ucq[zz, xk, b, 1], put)
        for b in range(2):
            v = jnp.dot(
                bw[2 * b : 2 * b + 2].reshape(256, 256), vq[zz, 2 * b : 2 * b + 2].reshape(256, 128),
                preferred_element_type=F32,
            )
            v = (v * scq[...].reshape(256, 128)).astype(BF)
            for xk in range(2):
                for i in range(NI):
                    rows = v[(xk * NI + i) * 16 : (xk * NI + i + 1) * 16]
                    lanes = slice((i % 2) * 128, (i % 2 + 1) * 128)
                    if xk:
                        xsq[zz, i // 2, b, :, lanes] = rows
                    else:
                        xrq[i // 2, x, zz, b, :, lanes] = rows
        remote(xsq.at[zz], xrq.at[:, x, zz], xq_send.at[0], xq_recv.at[0], partner, q).start()

    def crossings(cross, start, end):
        def one(j, c):
            cross((z + NZ + ((j + 1) // 2) * (2 * (j % 2) - 1)) % NZ)
            return c

        lax.fori_loop(start, end, one, 0)

    lax.fori_loop(2, 4, turn, 0)
    step_r(1)
    wait_bytes(ur, ur_recv.at[0])
    lax.fori_loop(0, 4, ready_r, 0)
    crossings(cross_r, 0, 3)
    step_r(2)
    crossings(cross_r, 3, 5)
    step_q(1)
    wait_bytes(uq, uq_recv.at[0])
    lax.fori_loop(0, 2, ready_q, 0)
    crossings(cross_q, 0, 3)
    for half in range(2):
        for qq in range(4):
            pp = 2 * q + half
            rr = pp * NZ + z
            own = jnp.logical_and(rr == r, qq == q)
            slot = (p - pp + NP) % NP
            give(own, um.at[half], us.at[slot], u_send.at[0], u_recv.at[0], rr, qq)
    step_r(3)
    crossings(cross_r, 5, 7)
    step_q(2)
    crossings(cross_q, 3, 5)

    here = lax.broadcasted_iota(jnp.int32, (2 * F, 2 * F), 0)
    n = lax.broadcasted_iota(jnp.int32, (2 * F, 2 * F), 1)
    from_r = n % 8 + 8 * ((n // 16) % 8) + 64 * (n // 128) + 256 * ((n // 8) % 2)
    from_q = n % 8 + 8 * ((n // 32) % 8) + 64 * ((n // 8) % 4) + 256 * (n // 256)

    def reorder(source, out):
        pick = jnp.where(here == source, 1.0, 0.0).astype(BF)
        for b in range(4):
            rows = slice(b * 256, (b + 1) * 256)
            out[rows, :] = jnp.dot(mt_ref[rows, :], pick, preferred_element_type=F32).astype(BF)

    for load in loads[NI:]:
        load.wait()
    reorder(from_r, mr_ref)
    step_r(4)
    crossings(cross_r, 7, 8)
    step_q(3)
    crossings(cross_q, 5, 7)
    reorder(from_q, mq_ref)
    step_q(4)
    crossings(cross_q, 7, 8)

    TB = 128
    def pairs(u, got, table):
        lo = first[pl.ds(u, 1), :]
        hi = last[pl.ds(u, 1), :]
        for b in range(L // TB):
            cor = jnp.dot(table[b * TB : (b + 1) * TB, :], got, preferred_element_type=F32)
            hil = jnp.dot(table[L + b * TB : L + (b + 1) * TB, :], got, preferred_element_type=F32)
            rs = lax.rsqrt(cor * cor + hil * hil + env_floor)
            lag = (lax.broadcasted_iota(jnp.int32, (TB, NJ), 0) + b * TB).astype(F32)
            inside = jnp.logical_and(lag >= lo, lag < hi)
            seen = obst[u, b * TB : (b + 1) * TB, :].astype(F32)
            wt = jnp.where(inside, (1.0 - seen * rs) * misfit_scale, 0.0)
            gs[b * TB : (b + 1) * TB, :] = (wt * cor).astype(BF)
            gs[L + b * TB : L + (b + 1) * TB, :] = (wt * hil).astype(BF)
        scale = ninv[pl.ds(u, 1), :]
        for b in range(4):
            back = jnp.dot(m_ref[b * 128 : (b + 1) * 128, :], gs[...], preferred_element_type=F32)
            zs[u, 2 * b : 2 * b + 2] = (back * scale).astype(BF).reshape(2, NG, 16, NJ)
        for k in range(1, NP):
            remote(
                zs.at[u, (p + k) % NP], zr.at[:, u, NP - k], z_send.at[u // 4], z_recv.at[u], plane(k), q
            ).start()
        zr[:, u, 0] = zs[u, p]

    def pairs_r(ii, c):
        pairs(4 + ii, xrr[ii].reshape(2 * F, NJ), mr_ref)
        return c

    def pairs_q(ii, c):
        pairs(ii, xrq[ii].reshape(2 * F, NJ), mq_ref)
        return c

    wait_bytes(xsr.at[:, 1:4], xr_recv.at[0])
    lax.fori_loop(0, 4, pairs_r, 0)
    wait_bytes(xsq, xq_recv.at[0])
    lax.fori_loop(0, 4, pairs_q, 0)

    def operand(k, c):
        uf = us[k, :, 0:1024].astype(F32)
        ut = turned(uf)
        for g in range(NG):
            def put(i, blk):
                bt[g, i // 2, i % 2, pl.ds(k * 16, 16), :] = blk

            blocks(uf[:, g * 256 : (g + 1) * 256], ut[:, g * 256 : (g + 1) * 256], put)
        return c

    wait_bytes(us, u_recv.at[0])
    lax.fori_loop(0, NP, operand, 0)

    def flip(g, c):
        for ii in range(4):
            for par in range(2):
                bb[g, par, :, ii * 128 : (ii + 1) * 128] = jnp.transpose(
                    bt[g, ii, par].astype(F32), (1, 0)
                ).astype(BF)
        return c

    lax.fori_loop(0, NG, flip, 0)

    def arrived(u):
        wait_bytes(zs.at[u, 1:NP], z_recv.at[u])

    def sums(h, start, end):
        size = (end - start) * 128
        for g in range(NG):
            part = None
            for par in range(2):
                got = zr[g, 4 * h + start : 4 * h + end, :, :, par * 128 : (par + 1) * 128].reshape(size, 128)
                one = jnp.dot(bb[g, par, :, start * 128 : end * 128], got, preferred_element_type=F32)
                part = one if part is None else part + one
            part = part.reshape(2, 128, 128)
            if start:
                part = part + w[h, 2 * g : 2 * g + 2]
            w[h, 2 * g : 2 * g + 2] = part

    def toward(n, src, h, part, to):
        rows = slice(part * 64, (part + 1) * 64)
        remote(
            src.at[rows], tbuf.at[h, n, rows], t_send.at[h], t_recv.at[h, n, part],
            p * NZ + (z + NZ + to) % NZ, q,
        ).start()

    def landed(n, h, part):
        wait_bytes(tbuf.at[h, n, part * 64 : (part + 1) * 64], t_recv.at[h, n, part])

    def tree_start(h):
        for part in range(2):
            for n, m, to in ((0, 4, 2), (2, 5, -1), (1, 3, 1)):
                toward(n, w.at[h, (z + m) % NZ], h, part, to)
        for part in range(2):
            for n, m, to in ((3, 1, 1), (4, 7, -1)):
                toward(n, w.at[h, (z + m) % NZ], h, part, to)

    def tree_middle(h):
        for part in range(2):
            rows = slice(part * 64, (part + 1) * 64)
            landed(2, h, part)
            tbuf[h, 2, rows] = tbuf[h, 2, rows] + w[h, (z + 6) % NZ, rows]
            toward(6, tbuf.at[h, 2], h, part, -2)
            landed(1, h, part)
            landed(0, h, part)
            tbuf[h, 0, rows] = tbuf[h, 0, rows] + (tbuf[h, 1, rows] + w[h, (z + 2) % NZ, rows])
            toward(5, tbuf.at[h, 0], h, part, 2)

    def tree_end(h):
        for n in (3, 4, 6, 5):
            for part in range(2):
                landed(n, h, part)
        done = (w[h, z] + tbuf[h, 3]) + (tbuf[h, 4] + tbuf[h, 6]) + tbuf[h, 5]
        cols = slice(h * 128, (h + 1) * 128)
        wg_out[:, cols] = jnp.where(row_mask[:, cols], done, 0.0)

    lane8 = (lax.broadcasted_iota(jnp.int32, (NP, 256), 1) // S) % 2

    def receivers(ii):
        for g in range(NG):
            for par in range(2):
                t = None
                for h in range(2):
                    got = zr[g, 4 * h + ii, :, :, par * 128 : (par + 1) * 128].reshape(128, 128)
                    held = vr[2 * g : 2 * g + 2, x] if h else vq[2 * g : 2 * g + 2, y]
                    block = held.reshape(256, 128)
                    part = lax.dot_general(got, block, nt, preferred_element_type=F32)
                    t = part if t is None else t + part
                t = t.reshape(NP, 16, 256)
                a0 = jnp.sum(jnp.where(mask0[None], t, 0.0), axis=1)
                a1 = jnp.sum(jnp.where(mask1[None], t, 0.0), axis=1)
                rg = a0 + jnp.where(lane8 == 0, -pltpu.roll(a1, 256 - S, 1), pltpu.roll(a1, S, 1))
                i = 2 * ii + par
                for k in range(NP):
                    rgp[k, i : i + 1, g * 256 : (g + 1) * 256] = rg[k : k + 1]

    for u in range(4, 8):
        arrived(u)
    sums(1, 0, 4)
    tree_start(1)
    arrived(0)
    receivers(0)
    tree_middle(1)
    arrived(1)
    receivers(1)
    arrived(2)
    receivers(2)
    sums(0, 0, 3)
    arrived(3)
    sums(0, 3, 4)
    tree_start(0)
    receivers(3)
    for k in range(NP):
        own = jnp.logical_and(k == 0, p // 2 == q)

        @pl.when(jnp.logical_not(own))
        def _():
            remote(rgp.at[k], rgr.at[q, p % 2], g_send.at[0], g_recv.at[0], plane(k), p // 2).start()

        @pl.when(own)
        def _():
            pltpu.make_async_copy(rgp.at[k], rgr.at[q, p % 2], g_recv.at[0]).start()

    tree_end(1)
    tree_middle(0)
    wait_bytes(rgr, g_recv.at[0])
    for half in range(2):
        total = (rgr[0, half] + rgr[1, half]) + (rgr[2, half] + rgr[3, half])
        rg_out[:, half * 1024 : (half + 1) * 1024] = jnp.where(keep, total, 0.0)
    tree_end(0)

    def sent(own, every, others, sem):
        @pl.when(jnp.logical_not(own))
        def _():
            wait_bytes(every, sem)

        @pl.when(own)
        def _():
            wait_bytes(others, sem)

    home = q == p // 2
    sent(home, us, us.at[1:NP], u_send.at[0])
    sent(q % 2 == y // 2, us, us.at[1:NP], ur_send.at[0])
    sent(q // 2 == x, uq, uq.at[1:4], uq_send.at[0])
    sent(home, rgp, rgp.at[1:NP], g_send.at[0])
    wait_bytes(vr.at[z, x], vx_send.at[0])
    wait_bytes(vq.at[z, 1:4], vy_send.at[0])
    wait_bytes(vr.at[1:NZ], vr_send.at[0])
    wait_bytes(vq.at[1:NZ], vq_send.at[0])
    wait_bytes(xsr.at[:, 1:4], xr_send.at[0])
    wait_bytes(xsq, xq_send.at[0])
    for h in range(2):
        wait_bytes(zs.at[4 * h : 4 * h + 4, 1:NP], z_send.at[h])
    for h in range(2):
        wait_bytes(tbuf.at[h], t_send.at[h])


def shards(receiver_spectra, reference_spectra, receiver_counts, reference_counts, column_station, lag_window, observed):
    table = lag_table()
    m = jnp.asarray(table, dtype=BF)
    mt = jnp.asarray(np.ascontiguousarray(table.T), dtype=BF)
    vmem = pl.BlockSpec(memory_space=pltpu.VMEM)
    hbm = pl.BlockSpec(memory_space=pl.ANY)
    dma = pltpu.SemaphoreType.DMA
    return pl.pallas_call(
        kernel,
        out_shape=(
            pltpu.VMEM((NI, 2048), F32),
            pltpu.VMEM((128, NJ), F32),
        ),
        in_specs=[hbm] * 9,
        out_specs=(pl.BlockSpec(memory_space=pltpu.MemorySpace.VMEM), pl.BlockSpec(memory_space=pltpu.MemorySpace.VMEM)),
        scratch_shapes=[
            pltpu.VMEM((NI, 2048), BF),
            pltpu.VMEM((128, NJ), BF),
            pltpu.VMEM((1, NI), jnp.int32),
            pltpu.VMEM((1, NJ), jnp.int32),
            pltpu.VMEM((1, NJ), jnp.int32),
            pltpu.VMEM((2, NI, NJ), jnp.int32),
            pltpu.VMEM((2, NI, 1152), BF),
            pltpu.VMEM((NP, NI, 1152), BF),
            pltpu.VMEM((4, 2, NI, 1152), BF),
            pltpu.VMEM((4, 2, NI, 1152), BF),
            pltpu.VMEM((NZ, 2, 128, 128), BF),
            pltpu.VMEM((NZ, 4, 128, 128), BF),
            pltpu.VMEM((NZ, 4, 2, NI, 256), F32),
            pltpu.VMEM((NZ, 2, 2, 2, NI, 256), F32),
            pltpu.VMEM((4, NI, 16, 256), BF),
            pltpu.VMEM((4, NI, 16, 128), F32),
            pltpu.VMEM((2, NI, 16, 128), F32),
            pltpu.VMEM((NG, 4, 2, 128, 256), BF),
            pltpu.VMEM((NG, 2, 256, 512), BF),
            pltpu.VMEM((8, NJ), F32),
            pltpu.VMEM((8, NJ), F32),
            pltpu.VMEM((8, NJ), F32),
            pltpu.VMEM((NI, NJ, L), BF),
            pltpu.VMEM((2 * F, 2 * L), BF),
            pltpu.VMEM((2 * L, 2 * F), BF),
            pltpu.VMEM((2 * L, 2 * F), BF),
            pltpu.VMEM((2 * L, 2 * F), BF),
            pltpu.VMEM((8, L, NJ), BF),
            pltpu.VMEM((NZ, 4, 4, 16, NJ), BF),
            pltpu.VMEM((4, 4, NZ, 16, NJ), BF),
            pltpu.VMEM((NZ, 4, 2, 16, NJ), BF),
            pltpu.VMEM((4, 2, NZ, 2, 16, NJ), BF),
            pltpu.VMEM((2 * L, NJ), BF),
            pltpu.VMEM((8, NP, NG, 16, NJ), BF),
            pltpu.VMEM((NG, 8, NP, 16, NJ), BF),
            pltpu.VMEM((2, NZ, 128, 128), F32),
            pltpu.VMEM((2, 7, 128, 128), F32),
            pltpu.VMEM((NP, NI, 1024), F32),
            pltpu.VMEM((4, 2, NI, 1024), F32),
            dma((9,)), dma((1,)), dma((1,)), dma((1,)), dma((1,)), dma((1,)), dma((1,)),
            dma((1,)), dma((1,)), dma((1,)), dma((4,)), dma((1,)), dma((NZ, 2)), dma((1,)), dma((NZ, 4)),
            dma((1,)), dma((1,)), dma((1,)), dma((1,)), dma((2,)), dma((8,)),
            dma((1,)), dma((1,)), dma((2,)), dma((2, 7, 2)),
        ],
        compiler_params=pltpu.CompilerParams(
            collective_id=0, has_side_effects=True, vmem_limit_bytes=60 * 1024 * 1024
        ),
    )(
        receiver_spectra,
        reference_spectra,
        receiver_counts.reshape(1, NI),
        reference_counts.reshape(1, NJ),
        column_station.reshape(1, NJ),
        lag_window,
        observed,
        m,
        mt,
    )


def solution(mesh):
    return jax.shard_map(
        shards,
        mesh=mesh,
        in_specs=(
            P("rcv", "ref"), P("rcv", "ref"), P("rcv"), P("ref"), P("ref"),
            P(None, "rcv", "ref"), P("rcv", "ref", None),
        ),
        out_specs=(P("rcv", "ref"), P("rcv", "ref")),
        check_vma=False,
    )
```
